256 devices in a mesh: section: 4 (over y), row: 4 (over x), col: 16 (over z, core).
Axes of the slice: x: 4, y: 4, z: 8, core: 2. Of those that a mesh axis runs over, the one named last changes fastest.
Arguments:
- hidden: bfloat16 [4, 256, 2, 3072], P(None, ('row', 'col')), may hold values from -6 to 6
- patch_counts: int32 [2, 4], replicated, may hold values from 128 to 256, as said below
- timestep: int32 [1], replicated, may hold values from 0 to 999
- time_table: float32 [1000, 512], replicated, may hold values from -6 to 6
- ada_weight: bfloat16 [4, 512, 18432], P('section', None, ('row', 'col')), may hold values from -0.25 to 0.25
- qkv_weight: bfloat16 [4, 3072, 9216], P('section', None, 'col'), may hold values from -0.109375 to 0.109375
- out_weight: bfloat16 [4, 3072, 3072], P('section', 'col'), may hold values from -0.109375 to 0.109375
- qk_gain: float32 [4, 2, 64], P('section'), may hold values from 1 to 3
- stale_kv: bfloat16 [4, 1024, 2, 48, 128], P('section', None, None, 'col'), may hold values from -8 to 8
- stale_inputs: bfloat16 [4, 64, 2, 3072], P('section', ('row', 'col')), may hold values from -6 to 6
- recompute_slots: int32 [2, 64], replicated, may hold values from 0 to 1023, as said below
Outputs:
- layer_outputs: bfloat16 [4, 4, 256, 2, 3072], P('section', None, ('row', 'col'))
The draws below stay inside these ranges and needn't reach their ends.
Inputs may be any that keep to these rules, and one draw needn't show every extreme that they name: `patch_counts`: in every request one patch holds exactly 256 live tokens and another exactly 128. `recompute_slots`: the slots of one request are distinct.
All inputs are finite; a program needn't handle non-finite values.
Results may differ from the reference program's by a relative error of at most 0.035.
Values may be sent and summed in bfloat16 or wider, within the bound.
No kernel may reach another device: no remote copies, remote signals or barrier semaphores. Data moves between devices by JAX's collectives and lax.ppermute only.
A program may use at most 64 MiB of HBM per device.

```python
import math
import jax
import jax.numpy as jnp
from jax import lax

HEADS = 48
HD = 64
D = 3072
TEMB = 512
TXT = 226
STEPS = 1000
GH = 30
GW = 45
REQS = 2
PATCHES = 4
PLEN = 256
LEN = 1024
HPC = 3
REC = 64
N_SECTION = 4
N_COL = 16


def draw_patch_counts(key, part):
    counts = jax.random.randint(key, (REQS, PATCHES), PLEN // 2, PLEN + 1)
    full_patch = jax.random.randint(jax.random.fold_in(key, 7), (REQS,), 0, PATCHES)
    short_patch = (full_patch + 1) % PATCHES
    patch_ids = jnp.arange(PATCHES)[None, :]
    counts = jnp.where(patch_ids == full_patch[:, None], PLEN, counts)
    counts = jnp.where(patch_ids == short_patch[:, None], PLEN // 2, counts)
    return counts.astype(jnp.int32)


def draw_recompute_slots(key, part):
    keys_all = jax.random.split(key, REQS)

    def pick_slots(one_key):
        return jax.random.permutation(one_key, LEN)[:REC].astype(jnp.int32)
    return jax.vmap(pick_slots)(keys_all)


def block_scale(stream_key, extent, shards, least, top_value):
    def one(position, parts):
        draws = jax.random.uniform(jax.random.fold_in(jax.random.fold_in(stream_key, 6), position), (parts,), jnp.float32, least / len(shards), top_value / len(shards))
        return jnp.repeat(jnp.exp(draws), extent[position] // parts).reshape((-1,) + (1,) * (len(extent) - position - 1))

    level = one(*shards[0])
    for cut in shards[1:]:
        level = level * one(*cut)
    return level


def bell_draw(stream_key, shape, deviation, reach, shards=(), held_as=jnp.bfloat16):
    values = jax.random.normal(stream_key, shape, jnp.float32) * deviation
    if len(shards) > 0:
        values = block_scale(stream_key, shape, shards, -0.22, 0.18) * values
    return jnp.clip(values, min=-reach, max=reach).astype(held_as)


def setup_inputs(seed: int = 0) -> dict:
    key_list = jax.random.split(jax.random.key(seed), 12)
    hidden = bell_draw(key_list[0], (PATCHES, PLEN, REQS, D), 1.0, 6.0, ((1, 64),))
    patch_counts = draw_patch_counts(jax.random.fold_in(key_list[11], 71), 0)
    timestep = jax.random.randint(key_list[2], (1,), 0, STEPS).astype(jnp.int32)
    time_table = bell_draw(key_list[3], (STEPS, TEMB), 1.0, 6.0, (), jnp.float32)
    ada_weight = bell_draw(key_list[4], (N_SECTION, TEMB, 6 * D), TEMB ** -0.5, 0.25, ((0, 4), (2, 64)))
    qkv_weight = bell_draw(key_list[5], (N_SECTION, D, 3 * D), D ** -0.5, 0.109375, ((0, 4), (2, 16)))
    out_weight = bell_draw(key_list[6], (N_SECTION, D, D), D ** -0.5, 0.109375, ((0, 4), (1, 16)))
    qk_gain = jnp.clip(jnp.exp(math.log(3.0) - 1.0986123 * jax.random.uniform(key_list[7], (N_SECTION, 2, HD), jnp.float32) ** block_scale(key_list[7], (N_SECTION, 2, HD), ((0, 4),), -0.2, 0.2)), 1.0, 3.0)
    stale_kv = bell_draw(key_list[8], (N_SECTION, LEN, REQS, HEADS, 2 * HD), 1.5, 8.0, ((0, 4), (3, 16)))
    stale_inputs = bell_draw(key_list[9], (N_SECTION, REC, REQS, D), 1.0, 6.0, ((0, 4), (1, 64)))
    recompute_slots = draw_recompute_slots(jax.random.fold_in(key_list[11], 71), 0)
    return {"hidden": hidden, "patch_counts": patch_counts, "timestep": timestep, "time_table": time_table, "ada_weight": ada_weight, "qkv_weight": qkv_weight, "out_weight": out_weight, "qk_gain": qk_gain, "stale_kv": stale_kv, "stale_inputs": stale_inputs, "recompute_slots": recompute_slots}


def layer_norm(values, epsilon):
    centered = values - lax.optimization_barrier(jnp.mean(values, axis=-1, keepdims=True))
    return centered * lax.rsqrt(lax.optimization_barrier(jnp.mean(centered * centered, axis=-1, keepdims=True)) + epsilon)

def rotary_tables(positions):
    video_index = jnp.maximum(positions - TXT, 0)
    is_video = positions >= TXT
    frame_index = video_index // (GH * GW)
    height_index = video_index // GW % GH
    width_index = video_index % GW
    phase_parts = []
    for coordinate, part_size in ((frame_index, HD // 4), (height_index, HD * 3 // 8), (width_index, HD * 3 // 8)):
        frequency = 1.0 / 10000.0 ** (jnp.arange(0, part_size, 2).astype(jnp.float32) / part_size)
        phase_part = coordinate.astype(jnp.float32)[..., None] * frequency
        phase_parts.append(jnp.repeat(phase_part, 2, axis=-1))
    phase_all = jnp.concatenate(phase_parts, axis=-1)
    cosine = jnp.where(is_video[..., None], jnp.cos(phase_all), 1.0)
    sine_table = jnp.where(is_video[..., None], jnp.sin(phase_all), 0.0)
    return (cosine, sine_table)

def rotate_pairs(values, cosine, sine_table):
    paired = values.reshape(values.shape[:-1] + (values.shape[-1] // 2, 2))
    turned = jnp.stack([-paired[..., 1], paired[..., 0]], axis=-1).reshape(values.shape)
    return values * cosine + turned * sine_table

def heads_from(mixed_rows, positions, gain_pair, with_queries):
    cosine, sine_table = rotary_tables(positions)
    cosine = cosine[..., None, :]
    sine_table = sine_table[..., None, :]
    keys_new = rotate_pairs(layer_norm(mixed_rows[..., 1, :], 1e-06) * gain_pair[1], cosine, sine_table).astype(jnp.bfloat16)
    values_new = mixed_rows[..., 2, :].astype(jnp.bfloat16)
    key_value = jnp.concatenate([keys_new, values_new], axis=-1)
    if with_queries:
        queries = rotate_pairs(layer_norm(mixed_rows[..., 0, :], 1e-06) * gain_pair[0], cosine, sine_table).astype(jnp.bfloat16)
        return (queries, key_value)
    return key_value

def modulate(row_values, positions, modulation):
    is_text = (positions < TXT)[..., None]
    shifts = jnp.where(is_text, modulation[3], modulation[0])
    scales = jnp.where(is_text, modulation[4], modulation[1])
    normed = layer_norm(row_values.astype(jnp.float32), 1e-05)
    return (normed * (1.0 + scales) + shifts).astype(jnp.bfloat16)

def reference(hidden, patch_counts, timestep, time_table, ada_weight, qkv_weight, out_weight, qk_gain, stale_kv, stale_inputs, recompute_slots):
    starts = jnp.cumsum(patch_counts, axis=1) - patch_counts
    slot_index = jnp.arange(LEN, dtype=jnp.int32)
    slot_patch = slot_index // PLEN
    slot_offset = slot_index % PLEN
    positions = starts[:, slot_patch] + slot_offset[None, :]
    live_mask = slot_offset[None, :] < patch_counts[:, slot_patch]
    slot_positions = positions.T
    embedding = jax.nn.silu(time_table[timestep[0]]).astype(jnp.bfloat16)
    scale_factor = HD ** (-0.5)
    current = hidden
    results = []
    for layer_index in range(N_SECTION):
        modulation = jnp.dot(embedding, ada_weight[layer_index], preferred_element_type=jnp.float32).reshape(6, D)
        slot_rows = current.reshape(LEN, REQS, D)
        normed = modulate(slot_rows, slot_positions, modulation)
        mixed_rows = jnp.dot(normed.reshape(LEN * REQS, D), qkv_weight[layer_index], preferred_element_type=jnp.float32)
        queries, fresh_pairs = heads_from(mixed_rows.reshape(LEN, REQS, HEADS, 3, HD), slot_positions, qk_gain[layer_index], True)
        rec_positions = jnp.take_along_axis(positions, recompute_slots, axis=1).T
        rec_normed = modulate(stale_inputs[layer_index], rec_positions, modulation)
        rec_mixed = jnp.dot(rec_normed.reshape(REC * REQS, D), qkv_weight[layer_index], preferred_element_type=jnp.float32)
        rec_pairs = heads_from(rec_mixed.reshape(REC, REQS, HEADS, 3, HD), rec_positions, qk_gain[layer_index], False)
        base_cache = stale_kv[layer_index]
        for request in range(REQS):
            base_cache = base_cache.at[recompute_slots[request], request].set(rec_pairs[:, request])
        patch_outputs = []
        for patch_index in range(PATCHES):
            use_fresh = (slot_patch <= patch_index)[:, None, None, None]
            cache_table = jnp.where(use_fresh, fresh_pairs, base_cache)
            patch_queries = queries[patch_index * PLEN:(patch_index + 1) * PLEN]
            scores = jnp.einsum('qrhd,krhd->rhqk', patch_queries.astype(jnp.float32), cache_table[..., :HD].astype(jnp.float32)) * scale_factor
            weights = jnp.where(live_mask[:, None, None, :], jnp.exp(scores), 0.0)
            totals = lax.optimization_barrier(jnp.sum(weights, axis=-1))
            rounded = lax.optimization_barrier(weights.astype(jnp.bfloat16)).astype(jnp.float32)
            attended = jnp.einsum('rhqk,krhd->qrhd', rounded, cache_table[..., HD:].astype(jnp.float32))
            attended = (attended / jnp.transpose(totals, (2, 0, 1))[..., None]).astype(jnp.bfloat16)
            grouped = lax.optimization_barrier(attended).reshape(PLEN * REQS, N_COL, HPC * HD).astype(jnp.float32)
            weight_groups = out_weight[layer_index].reshape(N_COL, HPC * HD, D).astype(jnp.float32)
            partials = jnp.einsum('ngc,gcd->gnd', grouped, weight_groups)
            partials = lax.optimization_barrier(partials.astype(jnp.bfloat16)).astype(jnp.float32)
            projected = lax.optimization_barrier(jnp.sum(partials, axis=0)).reshape(PLEN, REQS, D)
            patch_positions = slot_positions[patch_index * PLEN:(patch_index + 1) * PLEN]
            is_text = (patch_positions < TXT)[..., None]
            gate_rows = jnp.where(is_text, modulation[5], modulation[2])
            old_rows = current[patch_index].astype(jnp.float32)
            patch_outputs.append((old_rows + gate_rows * projected).astype(jnp.bfloat16))
        current = jnp.stack(patch_outputs, axis=0)
        results.append(current)
    return jnp.stack(results, axis=0)
```

```python
import jax
import jax.numpy as jnp
import numpy as np
from jax import lax
from jax.experimental import pallas as pl
from jax.experimental.pallas import tpu as pltpu
from jax.sharding import Mesh
from jax.sharding import PartitionSpec as P

HD = 64
D = 3072
TXT = 226
GH = 30
GW = 45
PLEN = 256
GROUP = 128
REC_GROUP = 32
BF = jnp.bfloat16
F32 = jnp.float32
COL = ("z", "core")
ROW = ("req", "half")
ROW_AXES = ("req", "half", "z", "core")


def call(kernel, out_shape, n_smem, n_vmem, name, scratch=()):
    return pl.pallas_call(
        kernel,
        out_shape=out_shape,
        in_specs=[pl.BlockSpec(memory_space=pltpu.SMEM)] * n_smem
        + [pl.BlockSpec(memory_space=pltpu.VMEM)] * n_vmem,
        scratch_shapes=list(scratch),
        compiler_params=pltpu.CompilerParams(vmem_limit_bytes=48 * 1024 * 1024),
        name=name,
    )


def iota(shape, dim):
    return lax.broadcasted_iota(jnp.int32, shape, dim)


def shape_of(shape, dtype):
    return jax.ShapeDtypeStruct(shape, dtype)


def frequencies():
    parts = []
    for size in (HD // 4, HD * 3 // 8, HD * 3 // 8):
        rate = 1.0 / np.float32(10000.0) ** (
            np.arange(0, size, 2).astype(np.float32) / np.float32(size)
        )
        parts.append(np.repeat(rate.astype(np.float32), 2))
    rate = np.concatenate(parts)
    return np.concatenate([rate, rate])[None, :].astype(np.float32)


def offset_in_patch(index, half):
    return (2 * ((index >> 2) & 1) + half) * 64 + 4 * (index >> 3) + (index & 3)


def prepare_kernel(scalars, row_ref, ada_ref, rate_ref, rec_ref, mod_out, cos_out, sin_out, text_out):
    half = scalars[0]
    time_row = row_ref[pl.ds(scalars[5], 1), :]
    embedding = (time_row / (1.0 + jnp.exp(-time_row))).astype(BF)
    embedding = jnp.broadcast_to(embedding, (8, embedding.shape[1]))
    part = jnp.dot(embedding, ada_ref[...], preferred_element_type=F32)[0:1]
    high = part.astype(BF)
    mod_out[0:1, :] = high
    mod_out[1:2, :] = (part - high.astype(F32)).astype(BF)

    rate = rate_ref[...]

    def tables(position, rows, at):
        text = position < TXT
        index = jnp.maximum(position - TXT, 0).astype(F32)
        frame = jnp.floor((index + 0.5) * (1.0 / (GH * GW)))
        line = jnp.floor((index + 0.5) * (1.0 / GW))
        width = index - line * GW
        height = line - jnp.floor((line + 0.5) * (1.0 / GH)) * GH
        lane = iota((rows, 128), 1) & (HD - 1)
        coordinate = jnp.where(lane < HD // 4, frame, jnp.where(lane < HD // 4 + HD * 3 // 8, height, width))
        phase = coordinate * rate
        cos_out[at : at + rows, :] = jnp.where(text, 1.0, jnp.cos(phase))
        sin_out[at : at + rows, :] = jnp.where(text, 0.0, jnp.sin(phase))
        text_out[at : at + rows, :] = jnp.where(text, 1.0, 0.0)

    for patch in range(4):
        offset = offset_in_patch(iota((GROUP, 128), 0), half)
        tables(offset + scalars[1 + patch], GROUP, patch * GROUP)
    slot = rec_ref[...]
    start = jnp.where(
        slot < PLEN,
        scalars[1],
        jnp.where(slot < 2 * PLEN, scalars[2], jnp.where(slot < 3 * PLEN, scalars[3], scalars[4])),
    )
    tables(start + (slot & (PLEN - 1)), REC_GROUP, 4 * GROUP)


def qkv_body(patch, blocks, w_ref, mod_ref, gain_ref, cos_ref, sin_ref, text_ref, q_out, kv_out, norm_ref):
    chunks = D // 128
    for x_ref, at, table_at in blocks:
        rows = x_ref.shape[0]
        text = text_ref[pl.ds(table_at, rows), :] > 0.5
        total = jnp.zeros((rows, 128), F32)
        for k in range(chunks):
            total = total + x_ref[:, 128 * k : 128 * k + 128].astype(F32)
        mean = jnp.sum(total, axis=1, keepdims=True) * (1.0 / D)
        total = jnp.zeros((rows, 128), F32)
        for k in range(chunks):
            centered = x_ref[:, 128 * k : 128 * k + 128].astype(F32) - mean
            total = total + centered * centered
        factor = lax.rsqrt(jnp.sum(total, axis=1, keepdims=True) * (1.0 / D) + 1e-5)
        for k in range(chunks):
            lanes = slice(128 * k, 128 * k + 128)
            shift = jnp.where(text, mod_ref[3:4, lanes], mod_ref[0:1, lanes])
            scale = jnp.where(text, mod_ref[4:5, lanes], mod_ref[1:2, lanes])
            centered = x_ref[:, lanes].astype(F32) - mean
            norm_ref[at : at + rows, lanes] = (centered * factor * (1.0 + scale) + shift).astype(BF)
    rows = norm_ref.shape[0]
    mixed = jnp.dot(norm_ref[...], w_ref[...], preferred_element_type=F32)
    lane = iota((128, 128), 1)
    block = jnp.where((iota((128, 128), 0) >> 6) == (lane >> 6), 1.0 / HD, 0.0).astype(BF)

    def group_mean(values):
        high = values.astype(BF)
        low = (values - high.astype(F32)).astype(BF)
        return jnp.dot(high, block, preferred_element_type=F32) + jnp.dot(
            low, block, preferred_element_type=F32
        )

    low_half = iota((rows, 128), 1) < HD
    even = (iota((rows, 128), 1) & 1) == 0
    cosine = jnp.concatenate([cos_ref[pl.ds(at, x.shape[0]), :] for x, _, at in blocks], axis=0)
    sine = jnp.concatenate([sin_ref[pl.ds(at, x.shape[0]), :] for x, _, at in blocks], axis=0)
    gain_q = gain_ref[0:1, :]
    gain_k = gain_ref[1:2, :]
    gains = (
        jnp.where(low_half, gain_q, gain_k),
        jnp.broadcast_to(gain_q, (rows, 128)),
        jnp.broadcast_to(gain_k, (rows, 128)),
        jnp.where(low_half, gain_q, gain_k),
    )
    plain, turned = [], []
    for k in range(4):
        values = mixed[:, 128 * k : 128 * k + 128]
        plain.append(values)
        centered = values - group_mean(values)
        scaled = centered * lax.rsqrt(group_mean(centered * centered) + 1e-6) * gains[k]
        partner = jnp.where(even, -pltpu.roll(scaled, 127, 1), pltpu.roll(scaled, 1, 1))
        turned.append(scaled * cosine + partner * sine)
    last = jnp.concatenate([mixed[:, 512:576], jnp.zeros((rows, 64), F32)], axis=1)
    kv_out[:, 0:128] = pltpu.roll(jnp.where(low_half, plain[1], turned[0]), 64, 1).astype(BF)
    kv_out[:, 128:256] = jnp.where(low_half, turned[2], plain[2]).astype(BF)
    kv_out[:, 256:384] = pltpu.roll(jnp.where(low_half, last, turned[3]), 64, 1).astype(BF)
    zero = jnp.zeros((GROUP, 128), F32)
    low = low_half[:GROUP]
    q_out[:, 0:128] = (jnp.where(low, turned[0][:GROUP], zero) * 0.125).astype(BF)
    q_out[:, 128:256] = (jnp.where(low, pltpu.roll(turned[1][:GROUP], 64, 1), zero) * 0.125).astype(BF)
    q_out[:, 256:384] = (jnp.where(low, turned[3][:GROUP], zero) * 0.125).astype(BF)


def qkv_first_kernel(x_ref, rec_ref, w_ref, mod_ref, gain_ref, cos_ref, sin_ref, text_ref, q_out, kv_out, norm_ref):
    blocks = ((x_ref, 0, 0), (rec_ref, GROUP, 4 * GROUP))
    qkv_body(0, blocks, w_ref, mod_ref, gain_ref, cos_ref, sin_ref, text_ref, q_out, kv_out, norm_ref)


def qkv_kernel(scalars, x_ref, w_ref, mod_ref, gain_ref, cos_ref, sin_ref, text_ref, q_out, kv_out, norm_ref):
    at = pl.multiple_of(scalars[0] * GROUP, GROUP)
    blocks = ((x_ref, 0, at),)
    qkv_body(0, blocks, w_ref, mod_ref, gain_ref, cos_ref, sin_ref, text_ref, q_out, kv_out, norm_ref)


def attend(scalars, q_ref, cache_ref, keep_out, send_out):
    patch, half, core = scalars[0], scalars[1], scalars[2]
    key = iota((8, 1024), 1)
    key_patch = key >> 8
    within = key & (PLEN - 1)
    fresh_offset = (2 * ((within >> 2) & 1) + (within >> 7)) * 64 + 4 * ((within >> 3) & 15) + (within & 3)
    offset = jnp.where(key_patch <= patch, fresh_offset, within)
    count = jnp.where(
        key_patch == 0,
        scalars[3],
        jnp.where(key_patch == 1, scalars[4], jnp.where(key_patch == 2, scalars[5], scalars[6])),
    )
    live = (offset < count)[0:1]
    outs = []
    for head in range(3):
        lanes = slice(128 * head, 128 * head + 128)
        table = cache_ref[:, lanes]
        scores = lax.dot_general(
            q_ref[:, lanes], table, (((1,), (1,)), ((), ())), preferred_element_type=F32
        )
        weights = jnp.where(live, jnp.exp(scores), 0.0)
        total = jnp.sum(weights, axis=1, keepdims=True)
        mixed = jnp.dot(weights.astype(BF), table, preferred_element_type=F32)
        outs.append(mixed / total)
    low = iota((GROUP, 128), 1) < HD
    first = jnp.where(low, pltpu.roll(outs[0], 64, 1), outs[1]).astype(BF)
    second = jnp.where(low, pltpu.roll(outs[2], 64, 1), 0.0).astype(BF)
    for z in range(8):
        to = slice(8 * z, 8 * z + 8)
        even, odd = slice(16 * z, 16 * z + 8), slice(16 * z + 8, 16 * z + 16)
        for value, lanes in ((first, slice(0, 128)), (second, slice(128, 256))):
            keep_out[to, lanes] = jnp.where(core == 0, value[even], value[odd])
            send_out[to, lanes] = jnp.where(core == 0, value[odd], value[even])


def store_fresh(scalars, own_ref, other_ref, cache_out):
    patch, half = scalars[0], scalars[1]
    own_at = pl.multiple_of(patch * PLEN + half * GROUP, GROUP)
    other_at = pl.multiple_of(patch * PLEN + (1 - half) * GROUP, GROUP)
    cache_out[pl.ds(own_at, GROUP), :] = own_ref[0:GROUP, :]
    cache_out[pl.ds(other_at, GROUP), :] = other_ref[0:GROUP, :]


def attend_first_kernel(scalars, q_ref, own_ref, other_ref, base_ref, target_ref, keep_out, send_out, cache_out, rec_ref):
    rec_ref[0:REC_GROUP, :] = own_ref[GROUP : GROUP + REC_GROUP, :]
    rec_ref[REC_GROUP : 2 * REC_GROUP, :] = other_ref[GROUP : GROUP + REC_GROUP, :]
    rec_ref[2 * REC_GROUP :, :] = jnp.zeros((128 - 2 * REC_GROUP, 384), BF)
    match = iota((1024, 128), 0) == target_ref[0:1, :]
    chosen = jnp.where(match, 1.0, 0.0)
    hit = jnp.sum(chosen, axis=1, keepdims=True) > 0.5
    placed = jnp.dot(chosen.astype(BF), rec_ref[...], preferred_element_type=F32)
    cache_out[...] = jnp.where(hit, placed, base_ref[...].astype(F32)).astype(BF)
    store_fresh(scalars, own_ref, other_ref, cache_out)
    attend(scalars, q_ref, cache_out, keep_out, send_out)


def attend_kernel(scalars, q_ref, own_ref, other_ref, cache_ref, keep_out, send_out, cache_out):
    cache_out[...] = cache_ref[...]
    store_fresh(scalars, own_ref, other_ref, cache_out)
    attend(scalars, q_ref, cache_out, keep_out, send_out)


def project_kernel(keep_ref, got_ref, own_ref, other_ref, out_ref):
    out = jnp.dot(keep_ref[...], own_ref[...], preferred_element_type=F32)
    out = out + jnp.dot(got_ref[...], other_ref[...], preferred_element_type=F32)
    out_ref[...] = out.astype(BF)


def residual_kernel(scalars, parts_ref, x_ref, mod_ref, out_ref):
    row = iota((8, 128), 0)
    offset = (2 * (row >> 2) + scalars[1]) * 64 + 4 * scalars[2] + (row & 3)
    text = (offset + scalars[0]) < TXT
    for k in range(D // 128):
        lanes = slice(128 * k, 128 * k + 128)
        total = parts_ref[0, :, lanes].astype(F32)
        for source in range(1, 8):
            total = total + parts_ref[source, :, lanes].astype(F32)
        gate = jnp.where(text, mod_ref[5:6, lanes], mod_ref[2:3, lanes])
        out_ref[:, lanes] = (x_ref[:, lanes].astype(F32) + gate * total).astype(BF)


def time_block(timestep, time_table):
    return lax.dynamic_slice(time_table, ((timestep[0] // 8) * 8, 0), (8, time_table.shape[1]))


def swapped(value, axis):
    return lax.ppermute(value, axis, [(0, 1), (1, 0)])


def local(
    hidden,
    patch_counts,
    timestep,
    time_table,
    ada_weight,
    qkv_weight,
    out_weight,
    qk_gain,
    stale_kv,
    stale_inputs,
    recompute_slots,
):
    section = lax.axis_index("section")
    req = lax.axis_index("req")
    half = lax.axis_index("half")
    core = lax.axis_index("core")
    col = lax.axis_index("z") * 2 + core
    first_req = req == 0
    sections = lax.axis_size("section")
    patches = hidden.shape[0]

    def of_request(value, axis):
        both = [lax.index_in_dim(value, r, axis, keepdims=False) for r in range(2)]
        return jnp.where(first_req, both[0], both[1]), jnp.where(first_req, both[1], both[0])

    hidden_own, hidden_other = of_request(hidden.reshape(patches * 4, 2, D), 1)
    rec_own, rec_other = of_request(stale_inputs.reshape(1, 2, D), 1)
    got = swapped(jnp.concatenate([hidden_other, rec_other], axis=0), "req")
    hidden_got = got[: patches * 4].reshape(patches, 4, D)
    hidden_own = hidden_own.reshape(patches, 4, D)
    rec_got = got[patches * 4 :]
    tokens = jnp.where(
        first_req,
        jnp.concatenate([hidden_own, hidden_got], axis=1),
        jnp.concatenate([hidden_got, hidden_own], axis=1),
    )
    rec_tokens = jnp.where(
        first_req,
        jnp.concatenate([rec_own, rec_got], axis=0),
        jnp.concatenate([rec_got, rec_own], axis=0),
    )

    counts, _ = of_request(patch_counts, 0)
    starts = jnp.stack([jnp.int32(0), counts[0], counts[0] + counts[1], counts[0] + counts[1] + counts[2]])
    slots, _ = of_request(recompute_slots, 0)
    slots = slots.reshape(2, 2, 16)
    target_own = jnp.where(half == 0, slots[:, 0], slots[:, 1]).T.reshape(REC_GROUP)
    target_other = jnp.where(half == 0, slots[:, 1], slots[:, 0]).T.reshape(REC_GROUP)
    targets = jnp.concatenate([target_own, target_other, jnp.full((64,), -1, jnp.int32)])
    targets = jnp.broadcast_to(targets[None, :], (8, 128))

    scalars = jnp.concatenate([half[None], starts, timestep % 8]).astype(jnp.int32)
    mod_part, cosine, sine, text = call(
        prepare_kernel,
        (
            shape_of((2, 288), BF),
            shape_of((4 * GROUP + REC_GROUP, 128), F32),
            shape_of((4 * GROUP + REC_GROUP, 128), F32),
            shape_of((4 * GROUP + REC_GROUP, 128), F32),
        ),
        1,
        4,
        "prepare",
    )(
        scalars,
        time_block(timestep, time_table),
        ada_weight[0],
        jnp.asarray(frequencies()),
        jnp.broadcast_to(target_own[:, None], (REC_GROUP, 128)),
    )

    payload = jnp.concatenate(
        [
            tokens[0],
            rec_tokens.reshape(8, 768),
            jnp.pad(mod_part.reshape(8, 72), ((0, 0), (0, 56))),
        ],
        axis=1,
    )
    gathered = lax.all_gather(payload, COL, axis=0, tiled=True)
    rec_rows = gathered[:, D : D + 768].reshape(REC_GROUP, D)
    pieces = gathered[:, D + 768 : D + 840].reshape(16, 2, 288).astype(F32)
    modulation = lax.all_gather(pieces[:, 0] + pieces[:, 1], ROW, axis=0, tiled=False).reshape(6, D)

    weights_qkv = qkv_weight[0]
    out_own = jnp.pad(out_weight[0], ((0, 64), (0, 0)))
    out_other = swapped(out_own, "core")
    gains = jnp.concatenate([qk_gain[0], qk_gain[0]], axis=1)
    base, _ = of_request(stale_kv[0], 1)
    cache = base.reshape(1024, 384)

    def qkv_shapes(rows):
        return (shape_of((GROUP, 384), BF), shape_of((rows, 384), BF))

    def attend_shapes():
        return (shape_of((64, 256), BF), shape_of((64, 256), BF), shape_of((1024, 384), BF))

    leavings = []
    current = tokens[0]
    for turn in range(patches + sections - 1):
        patch = jnp.clip(turn - section, 0, patches - 1)
        attend_scalars = jnp.concatenate([jnp.stack([patch, half, core]), counts]).astype(jnp.int32)
        if turn == 0:
            rows = GROUP + REC_GROUP
            queries, fresh = call(
                qkv_first_kernel, qkv_shapes(rows), 0, 8, "qkv_first", [pltpu.VMEM((rows, D), BF)]
            )(gathered[:, :D], rec_rows, weights_qkv, modulation, gains, cosine, sine, text)
        else:
            group = lax.all_gather(current, COL, axis=0, tiled=True)
            queries, fresh = call(
                qkv_kernel, qkv_shapes(GROUP), 1, 7, "qkv", [pltpu.VMEM((GROUP, D), BF)]
            )(patch[None].astype(jnp.int32), group, weights_qkv, modulation, gains, cosine, sine, text)
        fresh_other = swapped(fresh, "half")
        if turn == 0:
            keep, send, cache = call(
                attend_first_kernel, attend_shapes(), 1, 5, "attend_first", [pltpu.VMEM((128, 384), BF)]
            )(attend_scalars, queries, fresh, fresh_other, cache, targets)
        else:
            keep, send, cache = call(attend_kernel, attend_shapes(), 1, 4, "attend")(
                attend_scalars, queries, fresh, fresh_other, cache
            )
        projected = call(project_kernel, shape_of((64, D), BF), 0, 4, "project")(
            keep, swapped(send, "core"), out_own, out_other
        )
        parts = lax.all_to_all(projected.reshape(8, 8, D), "z", 0, 0)
        start = lax.dynamic_index_in_dim(starts, patch, 0, keepdims=False)
        leaving = call(residual_kernel, shape_of((8, D), BF), 1, 3, "residual")(
            jnp.stack([start, half, col]).astype(jnp.int32), parts, current, modulation
        )
        leavings.append(leaving)
        if turn + 1 < patches + sections - 1:
            incoming = lax.ppermute(leaving, "section", [(i, i + 1) for i in range(sections - 1)])
            entering = tokens[min(turn + 1, patches - 1)]
            current = jnp.where(section == 0, entering, incoming)

    stacked = lax.dynamic_slice_in_dim(jnp.stack(leavings), section, patches, 0)
    stacked = stacked.reshape(patches, 2, 4, D)
    mine, theirs = of_request(stacked, 1)
    returned = swapped(theirs, "req")
    out = jnp.where(first_req, jnp.stack([mine, returned], 2), jnp.stack([returned, mine], 2))
    return out[None]


def solution(mesh):
    sizes = tuple(mesh.devices.shape)
    fine = Mesh(
        mesh.devices.reshape(sizes[0], 2, sizes[1] // 2, sizes[2] // 2, 2),
        ("section", "req", "half", "z", "core"),
    )
    return jax.shard_map(
        local,
        mesh=fine,
        in_specs=(
            P(None, ROW_AXES, None, None),
            P(),
            P(),
            P(),
            P("section", None, ROW_AXES),
            P("section", None, COL),
            P("section", COL, None),
            P("section", None, None),
            P("section", None, None, COL, None),
            P("section", ROW_AXES, None, None),
            P(),
        ),
        out_specs=P("section", None, ROW_AXES, None, None),
        check_vma=False,
    )
```

```python
import jax
import jax.numpy as jnp
import numpy as np
from jax import lax
from jax.experimental import pallas as pl
from jax.experimental.pallas import tpu as pltpu
from jax.sharding import Mesh
from jax.sharding import PartitionSpec as P

HD = 64
D = 3072
TXT = 226
GH = 30
GW = 45
PLEN = 256
GROUP = 128
REC_GROUP = 32
BF = jnp.bfloat16
F32 = jnp.float32
COL = ("z", "core")
ROW = ("req", "half")
ROW_AXES = ("req", "half", "z", "core")


SMEM = pl.BlockSpec(memory_space=pltpu.SMEM)
VMEM = pl.BlockSpec(memory_space=pltpu.VMEM)
HBM = pl.BlockSpec(memory_space=pltpu.HBM)


def call(kernel, out_shape, in_specs, name, out_specs=None, scratch=(), aliases=None):
    if out_specs is None:
        out_specs = jax.tree.map(lambda _: VMEM, out_shape)
    return pl.pallas_call(
        kernel,
        out_shape=out_shape,
        in_specs=in_specs,
        out_specs=out_specs,
        scratch_shapes=list(scratch),
        input_output_aliases=aliases or {},
        compiler_params=pltpu.CompilerParams(vmem_limit_bytes=24 * 1024 * 1024),
        name=name,
    )


def iota(shape, dim):
    return lax.broadcasted_iota(jnp.int32, shape, dim)


def shape_of(shape, dtype):
    return jax.ShapeDtypeStruct(shape, dtype)


def frequencies():
    parts = []
    for size in (HD // 4, HD * 3 // 8, HD * 3 // 8):
        rate = 1.0 / np.float32(10000.0) ** (
            np.arange(0, size, 2).astype(np.float32) / np.float32(size)
        )
        parts.append(np.repeat(rate.astype(np.float32), 2))
    rate = np.concatenate(parts)
    return np.concatenate([rate, rate])[None, :].astype(np.float32)


def offset_in_patch(index, half):
    return (2 * ((index >> 2) & 1) + half) * 64 + 4 * (index >> 3) + (index & 3)


def prepare_kernel(scalars, row_ref, ada_ref, rate_ref, rec_ref, mod_out, cos_out, sin_out, text_out):
    half = scalars[0]
    time_row = row_ref[pl.ds(scalars[5], 1), :]
    embedding = (time_row / (1.0 + jnp.exp(-time_row))).astype(BF)
    embedding = jnp.broadcast_to(embedding, (8, embedding.shape[1]))
    part = lax.dot_general(
        embedding, ada_ref[...], (((1,), (1,)), ((), ())), preferred_element_type=F32
    )[0:1]
    high = part.astype(BF)
    mod_out[0:1, :] = high
    mod_out[1:2, :] = (part - high.astype(F32)).astype(BF)

    rate = rate_ref[...]

    def tables(position, rows, at):
        text = position < TXT
        index = jnp.maximum(position - TXT, 0).astype(F32)
        frame = jnp.floor((index + 0.5) * (1.0 / (GH * GW)))
        line = jnp.floor((index + 0.5) * (1.0 / GW))
        width = index - line * GW
        height = line - jnp.floor((line + 0.5) * (1.0 / GH)) * GH
        lane = iota((rows, 128), 1) & (HD - 1)
        coordinate = jnp.where(lane < HD // 4, frame, jnp.where(lane < HD // 4 + HD * 3 // 8, height, width))
        phase = coordinate * rate
        cos_out[at : at + rows, :] = jnp.where(text, 1.0, jnp.cos(phase))
        sin_out[at : at + rows, :] = jnp.where(text, 0.0, jnp.sin(phase))
        text_out[at : at + rows, :] = jnp.where(text, 1.0, 0.0)

    for patch in range(4):
        offset = offset_in_patch(iota((GROUP, 128), 0), half)
        tables(offset + scalars[1 + patch], GROUP, patch * GROUP)
    slot = rec_ref[...]
    start = jnp.where(
        slot < PLEN,
        scalars[1],
        jnp.where(slot < 2 * PLEN, scalars[2], jnp.where(slot < 3 * PLEN, scalars[3], scalars[4])),
    )
    tables(start + (slot & (PLEN - 1)), REC_GROUP, 4 * GROUP)


def qkv_body(blocks, w_ref, mod_ref, gain_ref, cos_ref, sin_ref, text_ref, q_out, kv_out, norm_ref, w_vmem, w_sems):
    chunks = D // 128
    pieces = w_sems.shape[0]
    width = D // pieces

    def fetch(k):
        lanes = pl.ds(k * width, width)
        return pltpu.make_async_copy(w_ref.at[:, lanes], w_vmem.at[:, lanes], w_sems.at[k])

    for k in range(pieces):
        fetch(k).start()
    for x_ref, at, table_at in blocks:
        rows = x_ref.shape[0]
        text = text_ref[pl.ds(table_at, rows), :] > 0.5

        def add(k, total):
            return total + x_ref[:, pl.ds(pl.multiple_of(k * 128, 128), 128)].astype(F32)

        total = lax.fori_loop(0, chunks, add, jnp.zeros((rows, 128), F32), unroll=2)
        mean = jnp.sum(total, axis=1, keepdims=True) * (1.0 / D)

        def add_square(k, total):
            centered = x_ref[:, pl.ds(pl.multiple_of(k * 128, 128), 128)].astype(F32) - mean
            return total + centered * centered

        total = lax.fori_loop(0, chunks, add_square, jnp.zeros((rows, 128), F32), unroll=2)
        factor = lax.rsqrt(jnp.sum(total, axis=1, keepdims=True) * (1.0 / D) + 1e-5)

        def write(k, carry):
            lanes = pl.ds(pl.multiple_of(k * 128, 128), 128)
            shift = jnp.where(text, mod_ref[3:4, lanes], mod_ref[0:1, lanes])
            scale = jnp.where(text, mod_ref[4:5, lanes], mod_ref[1:2, lanes])
            centered = x_ref[:, lanes].astype(F32) - mean
            norm_ref[at : at + rows, lanes] = (centered * factor * (1.0 + scale) + shift).astype(BF)
            return carry

        lax.fori_loop(0, chunks, write, 0, unroll=2)
    rows = norm_ref.shape[0]
    mixed = jnp.zeros((rows, 576), F32)
    for k in range(pieces):
        fetch(k).wait()
        lanes = slice(k * width, (k + 1) * width)
        mixed = mixed + lax.dot_general(
            norm_ref[:, lanes], w_vmem[:, lanes], (((1,), (1,)), ((), ())), preferred_element_type=F32
        )
    lane = iota((128, 128), 1)
    block = jnp.where((iota((128, 128), 0) >> 6) == (lane >> 6), 1.0 / HD, 0.0).astype(BF)

    def group_mean(values):
        high = values.astype(BF)
        low = (values - high.astype(F32)).astype(BF)
        return jnp.dot(high, block, preferred_element_type=F32) + jnp.dot(
            low, block, preferred_element_type=F32
        )

    low_half = iota((rows, 128), 1) < HD
    even = (iota((rows, 128), 1) & 1) == 0
    cosine = jnp.concatenate([cos_ref[pl.ds(at, x.shape[0]), :] for x, _, at in blocks], axis=0)
    sine = jnp.concatenate([sin_ref[pl.ds(at, x.shape[0]), :] for x, _, at in blocks], axis=0)
    gain_q = gain_ref[0:1, :]
    gain_k = gain_ref[1:2, :]
    gains = (
        jnp.where(low_half, gain_q, gain_k),
        jnp.broadcast_to(gain_q, (rows, 128)),
        jnp.broadcast_to(gain_k, (rows, 128)),
        jnp.where(low_half, gain_q, gain_k),
    )
    plain, turned = [], []
    for k in range(4):
        values = mixed[:, 128 * k : 128 * k + 128]
        plain.append(values)
        centered = values - group_mean(values)
        scaled = centered * lax.rsqrt(group_mean(centered * centered) + 1e-6) * gains[k]
        partner = jnp.where(even, -pltpu.roll(scaled, 127, 1), pltpu.roll(scaled, 1, 1))
        turned.append(scaled * cosine + partner * sine)
    last = jnp.concatenate([mixed[:, 512:576], jnp.zeros((rows, 64), F32)], axis=1)
    kv_out[:, 0:128] = pltpu.roll(jnp.where(low_half, plain[1], turned[0]), 64, 1).astype(BF)
    kv_out[:, 128:256] = jnp.where(low_half, turned[2], plain[2]).astype(BF)
    kv_out[:, 256:384] = pltpu.roll(jnp.where(low_half, last, turned[3]), 64, 1).astype(BF)
    zero = jnp.zeros((GROUP, 128), F32)
    low = low_half[:GROUP]
    q_out[:, 0:128] = (jnp.where(low, turned[0][:GROUP], zero) * 0.125).astype(BF)
    q_out[:, 128:256] = (jnp.where(low, pltpu.roll(turned[1][:GROUP], 64, 1), zero) * 0.125).astype(BF)
    q_out[:, 256:384] = (jnp.where(low, turned[3][:GROUP], zero) * 0.125).astype(BF)


def qkv_first_kernel(x_ref, rec_ref, mod_ref, gain_ref, cos_ref, sin_ref, text_ref, w_ref, q_out, kv_out, norm_ref, w_vmem, w_sems):
    blocks = ((x_ref, 0, 0), (rec_ref, GROUP, 4 * GROUP))
    qkv_body(blocks, w_ref, mod_ref, gain_ref, cos_ref, sin_ref, text_ref, q_out, kv_out, norm_ref, w_vmem, w_sems)


def qkv_kernel(
    turn_ref, table, x_ref, mod_ref, gain_ref, cos_ref, sin_ref, text_ref, w_ref, cache_ref,
    q_out, kv_out, stage_out, norm_ref, w_vmem, w_sems, sem,
):
    stage = pltpu.make_async_copy(cache_ref, stage_out, sem)
    stage.start()
    at = pl.multiple_of(table[turn_ref[0], 0] * GROUP, GROUP)
    blocks = ((x_ref, 0, at),)
    qkv_body(blocks, w_ref, mod_ref, gain_ref, cos_ref, sin_ref, text_ref, q_out, kv_out, norm_ref, w_vmem, w_sems)
    stage.wait()


def attend(table, turn, q_ref, cache_ref, keep_out, send_out):
    patch, half, core = table[turn, 0], table[turn, 1], table[turn, 2]
    key = iota((8, 1024), 1)
    key_patch = key >> 8
    within = key & (PLEN - 1)
    fresh_offset = (2 * ((within >> 2) & 1) + (within >> 7)) * 64 + 4 * ((within >> 3) & 15) + (within & 3)
    offset = jnp.where(key_patch <= patch, fresh_offset, within)
    count = jnp.where(
        key_patch == 0,
        table[turn, 4],
        jnp.where(key_patch == 1, table[turn, 5], jnp.where(key_patch == 2, table[turn, 6], table[turn, 7])),
    )
    live = (offset < count)[0:1]
    outs = []
    for head in range(3):
        lanes = slice(128 * head, 128 * head + 128)
        keys_values = cache_ref[:, lanes]
        scores = lax.dot_general(
            q_ref[:, lanes], keys_values, (((1,), (1,)), ((), ())), preferred_element_type=F32
        )
        weights = jnp.where(live, jnp.exp(scores), 0.0)
        total = jnp.sum(weights, axis=1, keepdims=True)
        mixed = jnp.dot(weights.astype(BF), keys_values, preferred_element_type=F32)
        outs.append(mixed / total)
    low = iota((GROUP, 128), 1) < HD
    first = jnp.where(low, pltpu.roll(outs[0], 64, 1), outs[1]).astype(BF)
    second = jnp.where(low, pltpu.roll(outs[2], 64, 1), 0.0).astype(BF)
    for z in range(8):
        to = slice(8 * z, 8 * z + 8)
        even, odd = slice(16 * z, 16 * z + 8), slice(16 * z + 8, 16 * z + 16)
        for value, lanes in ((first, slice(0, 128)), (second, slice(128, 256))):
            keep_out[to, lanes] = jnp.where(core == 0, value[even], value[odd])
            send_out[to, lanes] = jnp.where(core == 0, value[odd], value[even])


def fresh_rows(table, turn):
    patch, half = table[turn, 0], table[turn, 1]
    own_at = pl.multiple_of(patch * PLEN + half * GROUP, GROUP)
    other_at = pl.multiple_of(patch * PLEN + (1 - half) * GROUP, GROUP)
    return pl.ds(own_at, GROUP), pl.ds(other_at, GROUP)


def weight_copies(own_hbm, other_hbm, weights_out, sems):
    return (
        pltpu.make_async_copy(own_hbm, weights_out.at[0], sems.at[0]),
        pltpu.make_async_copy(other_hbm, weights_out.at[1], sems.at[1]),
    )


def attend_first_kernel(
    table, q_ref, own_ref, other_ref, base_ref, target_ref, own_hbm, other_hbm,
    keep_out, send_out, weights_out, cache_out, rec_ref, cache_ref, sems,
):
    weights = weight_copies(own_hbm, other_hbm, weights_out, sems)
    for copy in weights:
        copy.start()
    rec_ref[0:REC_GROUP, :] = own_ref[GROUP : GROUP + REC_GROUP, :]
    rec_ref[REC_GROUP : 2 * REC_GROUP, :] = other_ref[GROUP : GROUP + REC_GROUP, :]
    rec_ref[2 * REC_GROUP :, :] = jnp.zeros((128 - 2 * REC_GROUP, 384), BF)
    match = iota((1024, 128), 0) == target_ref[0:1, :]
    chosen = jnp.where(match, 1.0, 0.0)
    hit = jnp.sum(chosen, axis=1, keepdims=True) > 0.5
    placed = jnp.dot(chosen.astype(BF), rec_ref[...], preferred_element_type=F32)
    for head in range(3):
        lanes = slice(128 * head, 128 * head + 128)
        cache_ref[:, lanes] = jnp.where(hit, placed[:, lanes], base_ref[head].astype(F32)).astype(BF)
    own_rows, other_rows = fresh_rows(table, 0)
    cache_ref[own_rows, :] = own_ref[0:GROUP, :]
    cache_ref[other_rows, :] = other_ref[0:GROUP, :]
    keep_cache = pltpu.make_async_copy(cache_ref, cache_out, sems.at[2])
    keep_cache.start()
    attend(table, 0, q_ref, cache_ref, keep_out, send_out)
    for copy in weights:
        copy.wait()
    keep_cache.wait()


def attend_kernel(
    turn_ref, table, q_ref, own_ref, other_ref, stage_ref, own_hbm, other_hbm, cache_hbm,
    keep_out, send_out, weights_out, cache_out, cache_ref, sems,
):
    del cache_hbm
    turn = turn_ref[0]
    weights = weight_copies(own_hbm, other_hbm, weights_out, sems)
    for copy in weights:
        copy.start()
    own_rows, other_rows = fresh_rows(table, turn)
    keep_own = pltpu.make_async_copy(own_ref, cache_out.at[own_rows, :], sems.at[2])
    keep_other = pltpu.make_async_copy(other_ref, cache_out.at[other_rows, :], sems.at[3])
    keep_own.start()
    keep_other.start()
    cache_ref[...] = stage_ref[...]
    cache_ref[own_rows, :] = own_ref[...]
    cache_ref[other_rows, :] = other_ref[...]
    attend(table, turn, q_ref, cache_ref, keep_out, send_out)
    for copy in weights:
        copy.wait()
    keep_own.wait()
    keep_other.wait()


def project_kernel(keep_ref, got_ref, weights_ref, out_ref):
    out = jnp.dot(keep_ref[:, 0:192], weights_ref[0], preferred_element_type=F32)
    out = out + jnp.dot(got_ref[:, 0:192], weights_ref[1], preferred_element_type=F32)
    out_ref[...] = out.astype(BF)


def residual_kernel(turn_ref, table, parts_ref, x_ref, mod_ref, tokens_hbm, out_ref, ring_ref, enter_ref, sem):
    turn = turn_ref[0]
    entering = jnp.minimum(turn + 1, tokens_hbm.shape[0] - 1)
    enter = pltpu.make_async_copy(tokens_hbm.at[entering], enter_ref, sem)
    enter.start()
    half, col, patch = table[turn, 1], table[turn, 3], table[turn, 0]
    start = jnp.where(
        patch == 0,
        table[turn, 8],
        jnp.where(patch == 1, table[turn, 9], jnp.where(patch == 2, table[turn, 10], table[turn, 11])),
    )
    row = iota((8, 128), 0)
    offset = (2 * (row >> 2) + half) * 64 + 4 * col + (row & 3)
    text = (offset + start) < TXT
    for k in range(D // 128):
        lanes = slice(128 * k, 128 * k + 128)
        total = parts_ref[0, :, lanes].astype(F32)
        for source in range(1, 8):
            total = total + parts_ref[source, :, lanes].astype(F32)
        gate = jnp.where(text, mod_ref[5:6, lanes], mod_ref[2:3, lanes])
        out_ref[:, lanes] = (x_ref[:, lanes].astype(F32) + gate * total).astype(BF)
    enter.wait()
    ring_ref[...] = jnp.where(table[turn, 12] == 1, enter_ref[...], out_ref[...])


def time_block(timestep, time_table):
    return lax.dynamic_slice(time_table, ((timestep[0] // 8) * 8, 0), (8, time_table.shape[1]))


def swapped(value, axis):
    return lax.ppermute(value, axis, [(0, 1), (1, 0)])


def local(
    hidden,
    patch_counts,
    timestep,
    time_table,
    ada_weight,
    qkv_weight,
    out_weight,
    qk_gain,
    stale_kv,
    stale_inputs,
    recompute_slots,
):
    section = lax.axis_index("section")
    req = lax.axis_index("req")
    half = lax.axis_index("half")
    core = lax.axis_index("core")
    col = lax.axis_index("z") * 2 + core
    first_req = req == 0
    sections = lax.axis_size("section")
    patches = hidden.shape[0]

    def of_request(value, axis):
        both = [lax.index_in_dim(value, r, axis, keepdims=False) for r in range(2)]
        return jnp.where(first_req, both[0], both[1]), jnp.where(first_req, both[1], both[0])

    def by_request(value, got):
        own = [lax.index_in_dim(value, r, 2, keepdims=False) for r in range(2)]
        far = [lax.index_in_dim(got, r, 2, keepdims=False) for r in range(2)]
        return jnp.where(
            first_req, jnp.concatenate([own[0], far[0]], axis=1), jnp.concatenate([far[1], own[1]], axis=1)
        )

    tokens = by_request(hidden, swapped(hidden, "req"))
    rec_tokens = by_request(stale_inputs, swapped(stale_inputs, "req"))[0]

    counts, _ = of_request(patch_counts, 0)
    starts = jnp.stack([jnp.int32(0), counts[0], counts[0] + counts[1], counts[0] + counts[1] + counts[2]])
    slots, _ = of_request(recompute_slots, 0)
    slots = slots.reshape(2, 2, 16)
    target_own = jnp.where(half == 0, slots[:, 0], slots[:, 1]).T.reshape(REC_GROUP)
    target_other = jnp.where(half == 0, slots[:, 1], slots[:, 0]).T.reshape(REC_GROUP)
    targets = jnp.concatenate([target_own, target_other, jnp.full((64,), -1, jnp.int32)])
    targets = jnp.broadcast_to(targets[None, :], (8, 128))

    turns = patches + sections - 1
    patch_of = jnp.clip(jnp.arange(turns, dtype=jnp.int32) - section, 0, patches - 1)
    fixed = jnp.concatenate(
        [jnp.stack([half, core, col]), counts, starts, (section == sections - 1)[None]]
    ).astype(jnp.int32)
    table = jnp.concatenate([patch_of[:, None], jnp.broadcast_to(fixed[None, :], (turns, 12))], axis=1)

    scalars = jnp.concatenate([half[None], starts, timestep % 8]).astype(jnp.int32)
    table_rows = shape_of((4 * GROUP + REC_GROUP, 128), F32)
    mod_part, cosine, sine, text = call(
        prepare_kernel,
        (shape_of((2, 288), BF), table_rows, table_rows, table_rows),
        [SMEM, VMEM, VMEM, VMEM, VMEM],
        "prepare",
    )(
        scalars,
        time_block(timestep, time_table),
        ada_weight[0].T,
        jnp.asarray(frequencies()),
        jnp.broadcast_to(target_own[:, None], (REC_GROUP, 128)),
    )

    payload = jnp.concatenate(
        [
            tokens[0],
            rec_tokens.reshape(8, 768),
            jnp.pad(mod_part.reshape(8, 72), ((0, 0), (0, 56))),
        ],
        axis=1,
    )
    gathered = lax.all_gather(payload, COL, axis=0, tiled=True)
    rec_rows = gathered[:, D : D + 768].reshape(REC_GROUP, D)
    pieces = gathered[:, D + 768 : D + 840].reshape(16, 2, 288).astype(F32)
    summed = pieces[:, 0] + pieces[:, 1]
    rows = lax.axis_size(ROW)
    modulation = lax.all_to_all(jnp.broadcast_to(summed[None], (rows, 16, 288)), ROW, 0, 0).reshape(6, D)

    weights_qkv = qkv_weight[0].T
    out_own = out_weight[0]
    out_other = swapped(out_own, "core")
    gains = jnp.concatenate([qk_gain[0], qk_gain[0]], axis=1)
    stale = jnp.transpose(stale_kv[0], (2, 0, 1, 3))
    base = jnp.stack([jnp.where(first_req, stale[h, :, 0], stale[h, :, 1]) for h in range(3)])

    def qkv_shapes(rows):
        return (shape_of((GROUP, 384), BF), shape_of((rows, 384), BF))

    def qkv_scratch(rows):
        return [pltpu.VMEM((rows, D), BF), pltpu.VMEM((576, D), BF), pltpu.SemaphoreType.DMA((4,))]

    half_rows = shape_of((64, 256), BF)
    attend_shapes = (half_rows, half_rows, shape_of((2, 192, D), BF), shape_of((1024, 384), BF))
    attend_specs = (VMEM, VMEM, VMEM, HBM)

    def finish(turn, current, queries_keep, weights_out):
        keep, send = queries_keep
        projected = call(project_kernel, shape_of((64, D), BF), [VMEM] * 3, "project")(
            keep, swapped(send, "core"), weights_out
        )
        parts = lax.all_to_all(projected.reshape(8, 8, D), "z", 0, 0)
        return call(
            residual_kernel,
            (shape_of((8, D), BF), shape_of((8, D), BF)),
            [SMEM, SMEM, VMEM, VMEM, VMEM, HBM],
            "residual",
            scratch=[pltpu.VMEM((8, D), BF), pltpu.SemaphoreType.DMA],
        )(turn, table, parts, current, modulation, tokens)

    def onward(ring):
        return lax.ppermute(ring, "section", [(i, (i + 1) % sections) for i in range(sections)])

    queries, fresh = call(
        qkv_first_kernel,
        qkv_shapes(GROUP + REC_GROUP),
        [VMEM] * 7 + [HBM],
        "qkv_first",
        scratch=qkv_scratch(GROUP + REC_GROUP),
    )(gathered[:, :D], rec_rows, modulation, gains, cosine, sine, text, weights_qkv)
    keep, send, weights_out, cache = call(
        attend_first_kernel,
        attend_shapes,
        [SMEM] + [VMEM] * 5 + [HBM] * 2,
        "attend_first",
        out_specs=attend_specs,
        scratch=[pltpu.VMEM((128, 384), BF), pltpu.VMEM((1024, 384), BF), pltpu.SemaphoreType.DMA((3,))],
    )(table, queries, fresh, swapped(fresh, "half"), base, targets, out_own, out_other)
    leaving, ring = finish(jnp.zeros((1,), jnp.int32), tokens[0], (keep, send), weights_out)
    stacked = jnp.zeros((turns, 8, D), BF).at[0].set(leaving)

    def one_turn(turn, current, cache, stacked):
        turn = turn.reshape(1)
        group = lax.all_gather(current, COL, axis=0, tiled=True)
        queries, fresh, stage = call(
            qkv_kernel,
            qkv_shapes(GROUP) + (shape_of((1024, 384), BF),),
            [SMEM] * 2 + [VMEM] * 6 + [HBM] * 2,
            "qkv",
            scratch=qkv_scratch(GROUP) + [pltpu.SemaphoreType.DMA],
        )(turn, table, group, modulation, gains, cosine, sine, text, weights_qkv, cache)
        keep, send, weights_out, cache = call(
            attend_kernel,
            attend_shapes,
            [SMEM] * 2 + [VMEM] * 4 + [HBM] * 3,
            "attend",
            out_specs=attend_specs,
            scratch=[pltpu.VMEM((1024, 384), BF), pltpu.SemaphoreType.DMA((4,))],
            aliases={8: 3},
        )(turn, table, queries, fresh, swapped(fresh, "half"), stage, out_own, out_other, cache)
        leaving, ring = finish(turn, current, (keep, send), weights_out)
        return ring, cache, lax.dynamic_update_slice(stacked, leaving[None], (turn[0], 0, 0))

    def body(turn, state):
        ring, cache, stacked = one_turn(turn, *state)
        return onward(ring), cache, stacked

    current, cache, stacked = lax.fori_loop(1, turns - 1, body, (onward(ring), cache, stacked))
    _, _, stacked = one_turn(jnp.int32(turns - 1), current, cache, stacked)
    stacked = lax.dynamic_slice_in_dim(stacked, section, patches, 0)
    stacked = stacked.reshape(patches, 2, 4, D)
    mine, theirs = of_request(stacked, 1)
    returned = swapped(theirs, "req")
    out = jnp.where(first_req, jnp.stack([mine, returned], 2), jnp.stack([returned, mine], 2))
    return out[None]


def solution(mesh):
    sizes = tuple(mesh.devices.shape)
    fine = Mesh(
        mesh.devices.reshape(sizes[0], 2, sizes[1] // 2, sizes[2] // 2, 2),
        ("section", "req", "half", "z", "core"),
    )
    return jax.shard_map(
        local,
        mesh=fine,
        in_specs=(
            P(None, ROW_AXES, None, None),
            P(),
            P(),
            P(),
            P("section", None, ROW_AXES),
            P("section", None, COL),
            P("section", COL, None),
            P("section", None, None),
            P("section", None, None, COL, None),
            P("section", ROW_AXES, None, None),
            P(),
        ),
        out_specs=P("section", None, ROW_AXES, None, None),
        check_vma=False,
    )
```

```python
import jax
import jax.numpy as jnp
import numpy as np
from jax import lax
from jax.experimental import pallas as pl
from jax.experimental.pallas import tpu as pltpu
from jax.sharding import Mesh
from jax.sharding import PartitionSpec as P

HD = 64
D = 3072
TXT = 226
GH = 30
GW = 45
PLEN = 256
GROUP = 128
REC_GROUP = 32
BF = jnp.bfloat16
F32 = jnp.float32
COL = ("z", "core")
ROW = ("req", "half")
ROW_AXES = ("req", "half", "z", "core")


SMEM = pl.BlockSpec(memory_space=pltpu.SMEM)
VMEM = pl.BlockSpec(memory_space=pltpu.VMEM)
HBM = pl.BlockSpec(memory_space=pltpu.HBM)


def call(kernel, out_shape, in_specs, name, out_specs=None, scratch=(), aliases=None):
    if out_specs is None:
        out_specs = jax.tree.map(lambda _: VMEM, out_shape)
    return pl.pallas_call(
        kernel,
        out_shape=out_shape,
        in_specs=in_specs,
        out_specs=out_specs,
        scratch_shapes=list(scratch),
        input_output_aliases=aliases or {},
        compiler_params=pltpu.CompilerParams(vmem_limit_bytes=24 * 1024 * 1024),
        name=name,
    )


def iota(shape, dim):
    return lax.broadcasted_iota(jnp.int32, shape, dim)


def shape_of(shape, dtype):
    return jax.ShapeDtypeStruct(shape, dtype)


def frequencies():
    parts = []
    for size in (HD // 4, HD * 3 // 8, HD * 3 // 8):
        rate = 1.0 / np.float32(10000.0) ** (
            np.arange(0, size, 2).astype(np.float32) / np.float32(size)
        )
        parts.append(np.repeat(rate.astype(np.float32), 2))
    rate = np.concatenate(parts)
    return np.concatenate([rate, rate])[None, :].astype(np.float32)


def offset_in_patch(index, half):
    return (2 * ((index >> 2) & 1) + half) * 64 + 4 * (index >> 3) + (index & 3)


def prepare_kernel(scalars, row_ref, ada_ref, rate_ref, rec_ref, mod_out, cos_out, sin_out, text_out):
    half = scalars[0]
    time_row = row_ref[pl.ds(scalars[5], 1), :]
    embedding = (time_row / (1.0 + jnp.exp(-time_row))).astype(BF)
    embedding = jnp.broadcast_to(embedding, (8, embedding.shape[1]))
    part = lax.dot_general(
        embedding, ada_ref[...], (((1,), (1,)), ((), ())), preferred_element_type=F32
    )[0:1]
    high = part.astype(BF)
    mod_out[0:1, :] = high
    mod_out[1:2, :] = (part - high.astype(F32)).astype(BF)

    rate = rate_ref[...]

    def tables(position, rows, at):
        text = position < TXT
        index = jnp.maximum(position - TXT, 0).astype(F32)
        frame = jnp.floor((index + 0.5) * (1.0 / (GH * GW)))
        line = jnp.floor((index + 0.5) * (1.0 / GW))
        width = index - line * GW
        height = line - jnp.floor((line + 0.5) * (1.0 / GH)) * GH
        lane = iota((rows, 128), 1) & (HD - 1)
        coordinate = jnp.where(lane < HD // 4, frame, jnp.where(lane < HD // 4 + HD * 3 // 8, height, width))
        phase = coordinate * rate
        cos_out[at : at + rows, :] = jnp.where(text, 1.0, jnp.cos(phase))
        sin_out[at : at + rows, :] = jnp.where(text, 0.0, jnp.sin(phase))
        text_out[at : at + rows, :] = jnp.where(text, 1.0, 0.0)

    tables(offset_in_patch(iota((GROUP, 128), 0), half) + scalars[6], GROUP, 0)
    slot = rec_ref[...]
    start = jnp.where(
        slot < PLEN,
        scalars[1],
        jnp.where(slot < 2 * PLEN, scalars[2], jnp.where(slot < 3 * PLEN, scalars[3], scalars[4])),
    )
    tables(start + (slot & (PLEN - 1)), REC_GROUP, GROUP)


def normalize(x_ref, mod_ref, layer, text_ref, norm_ref):
    chunks = D // 128
    rows = x_ref.shape[0]
    text = text_ref[...] > 0.5

    def over_chunks(step, start):
        return lax.fori_loop(0, chunks, lambda k, carry: step(pl.ds(pl.multiple_of(k * 128, 128), 128), carry), start, unroll=6)

    def add(lanes, total):
        return total + x_ref[:, lanes].astype(F32)

    mean = jnp.sum(over_chunks(add, jnp.zeros((rows, 128), F32)), axis=1, keepdims=True) * (1.0 / D)

    def add_square(lanes, total):
        centered = x_ref[:, lanes].astype(F32) - mean
        return total + centered * centered

    total = jnp.sum(over_chunks(add_square, jnp.zeros((rows, 128), F32)), axis=1, keepdims=True)
    factor = lax.rsqrt(total * (1.0 / D) + 1e-5)

    def write(lanes, carry):
        shift = jnp.where(text, mod_ref[layer, 3:4, lanes], mod_ref[layer, 0:1, lanes])
        scale = jnp.where(text, mod_ref[layer, 4:5, lanes], mod_ref[layer, 1:2, lanes])
        centered = x_ref[:, lanes].astype(F32) - mean
        norm_ref[:, lanes] = (centered * factor * (1.0 + scale) + shift).astype(BF)
        return carry

    over_chunks(write, 0)


def heads_from(mixed, gain_ref, cos_ref, sin_ref, q_out, kv_out):
    rows = mixed.shape[0]
    lane = iota((128, 128), 1)
    block = jnp.where((iota((128, 128), 0) >> 6) == (lane >> 6), 1.0 / HD, 0.0).astype(BF)

    def group_mean(values):
        high = values.astype(BF)
        low = (values - high.astype(F32)).astype(BF)
        return jnp.dot(high, block, preferred_element_type=F32) + jnp.dot(
            low, block, preferred_element_type=F32
        )

    low_half = iota((rows, 128), 1) < HD
    even = (iota((rows, 128), 1) & 1) == 0
    cosine, sine = cos_ref[...], sin_ref[...]
    gain_q = gain_ref[0:1, :]
    gain_k = gain_ref[1:2, :]
    gains = (
        jnp.where(low_half, gain_q, gain_k),
        jnp.broadcast_to(gain_q, (rows, 128)),
        jnp.broadcast_to(gain_k, (rows, 128)),
        jnp.where(low_half, gain_q, gain_k),
    )
    plain, turned = [], []
    for k in range(4):
        values = mixed[:, 128 * k : 128 * k + 128]
        plain.append(values)
        centered = values - group_mean(values)
        scaled = centered * lax.rsqrt(group_mean(centered * centered) + 1e-6) * gains[k]
        partner = jnp.where(even, -pltpu.roll(scaled, 127, 1), pltpu.roll(scaled, 1, 1))
        turned.append(scaled * cosine + partner * sine)
    last = jnp.concatenate([mixed[:, 512:576], jnp.zeros((rows, 64), F32)], axis=1)
    keys_values = (
        pltpu.roll(jnp.where(low_half, plain[1], turned[0]), 64, 1).astype(BF),
        jnp.where(low_half, turned[2], plain[2]).astype(BF),
        pltpu.roll(jnp.where(low_half, last, turned[3]), 64, 1).astype(BF),
    )
    for copy in range(kv_out.shape[0]):
        for head in range(3):
            kv_out[copy, :, 128 * head : 128 * head + 128] = keys_values[head]
    if q_out is None:
        return
    zero = jnp.zeros((rows, 128), F32)
    q_out[:, 0:128] = (jnp.where(low_half, turned[0], zero) * 0.125).astype(BF)
    q_out[:, 128:256] = (jnp.where(low_half, pltpu.roll(turned[1], 64, 1), zero) * 0.125).astype(BF)
    q_out[:, 256:384] = (jnp.where(low_half, turned[3], zero) * 0.125).astype(BF)


def times_weights(norm, weights):
    return lax.dot_general(norm, weights, (((1,), (1,)), ((), ())), preferred_element_type=F32)


def rec_kernel(scalars, x_ref, mod_ref, gain_ref, cos_ref, sin_ref, text_ref, w_ref, kv_out, norm_ref, w_vmem, sem):
    fetch = pltpu.make_async_copy(w_ref, w_vmem, sem)
    fetch.start()
    normalize(x_ref, mod_ref, scalars[7], text_ref, norm_ref)
    fetch.wait()
    heads_from(times_weights(norm_ref[...], w_vmem[...]), gain_ref, cos_ref, sin_ref, None, kv_out)


def qkv_kernel_of(layer):
    def qkv_kernel(x_ref, mod_ref, gain_ref, cos_ref, sin_ref, text_ref, packed_ref, q_out, kv_out, weights_out, norm_ref, w_vmem, sems):
        def fetch(k):
            to = w_vmem.at[pl.ds(288 * (k % 2), 288), pl.ds(384 * (k // 2), 384)]
            return pltpu.make_async_copy(packed_ref.at[k, pl.ds(0, 288), :], to, sems.at[k])

        def pass_on(k):
            to = weights_out.at[pl.ds(96 * (k % 2), 96), pl.ds(384 * (k // 2), 384)]
            return pltpu.make_async_copy(packed_ref.at[k, pl.ds(288, 96), :], to, sems.at[16 + k])

        for k in range(16):
            fetch(k).start()
        for k in range(16):
            pass_on(k).start()
        normalize(x_ref, mod_ref, layer, text_ref, norm_ref)
        mixed = jnp.zeros((GROUP, 576), F32)
        for piece in range(4):
            for k in range(4 * piece, 4 * piece + 4):
                fetch(k).wait()
            lanes = slice(768 * piece, 768 * piece + 768)
            mixed = mixed + times_weights(norm_ref[:, lanes], w_vmem[:, lanes])
        heads_from(mixed, gain_ref, cos_ref, sin_ref, q_out, kv_out)
        for k in range(16):
            pass_on(k).wait()

    return qkv_kernel


def pack_kernel(scalars, w_ref, out_ref, base_ref, packed, sems):
    row = scalars[8]
    copies = []
    for k in range(4):
        lanes = pl.ds(pl.multiple_of(row * 768 + 384 * (k // 2), 128), 384)
        copies += [
            (w_ref.at[pl.ds(288 * (k % 2), 288), lanes], packed.at[k, pl.ds(0, 288), :]),
            (out_ref.at[pl.ds(96 * (k % 2), 96), lanes], packed.at[k, pl.ds(288, 96), :]),
            (base_ref.at[k], packed.at[k, pl.ds(384, 128), :]),
        ]
    copies = [pltpu.make_async_copy(a, b, sems.at[n]) for n, (a, b) in enumerate(copies)]
    for copy in copies:
        copy.start()
    for copy in copies:
        copy.wait()


def attend(scalars, q_ref, cache_ref, keep_out, send_out):
    patch, core = scalars[7], scalars[9]
    key = iota((8, 1024), 1)
    key_patch = key >> 8
    within = key & (PLEN - 1)
    fresh_offset = (2 * ((within >> 2) & 1) + (within >> 7)) * 64 + 4 * ((within >> 3) & 15) + (within & 3)
    offset = jnp.where(key_patch <= patch, fresh_offset, within)
    count = jnp.where(
        key_patch == 0,
        scalars[11],
        jnp.where(key_patch == 1, scalars[12], jnp.where(key_patch == 2, scalars[13], scalars[14])),
    )
    live = (offset < count)[0:1]
    outs = []
    for head in range(3):
        lanes = slice(128 * head, 128 * head + 128)
        keys_values = cache_ref[:, lanes]
        scores = lax.dot_general(
            q_ref[:, lanes], keys_values, (((1,), (1,)), ((), ())), preferred_element_type=F32
        )
        weights = jnp.where(live, jnp.exp(scores), 0.0)
        total = jnp.sum(weights, axis=1, keepdims=True)
        mixed = jnp.dot(weights.astype(BF), keys_values, preferred_element_type=F32)
        outs.append(mixed / total)
    low = iota((GROUP, 128), 1) < HD
    first = jnp.where(low, pltpu.roll(outs[0], 64, 1), outs[1]).astype(BF)
    second = jnp.where(low, pltpu.roll(outs[2], 64, 1), 0.0).astype(BF)
    for z in range(8):
        to = slice(8 * z, 8 * z + 8)
        even, odd = slice(16 * z, 16 * z + 8), slice(16 * z + 8, 16 * z + 16)
        for value, lanes in ((first, slice(0, 128)), (second, slice(128, 256))):
            keep_out[to, lanes] = jnp.where(core == 0, value[even], value[odd])
            send_out[to, lanes] = jnp.where(core == 0, value[odd], value[even])


def attend_kernel_of(layer):
    def attend_kernel(
        scalars, q_ref, fresh_ref, rec_ref, target_ref, packed_ref, own_hbm, other_hbm,
        keep_out, send_out, weights_out, base_ref, cache_ref, rec_vmem, sems,
    ):
        section, req = scalars[7], scalars[15]
        rec_copies = [
            pltpu.make_async_copy(
                rec_ref.at[2 * layer + h], rec_vmem.at[pl.ds(REC_GROUP * h, REC_GROUP), :], sems.at[18 + h]
            )
            for h in range(2)
        ]
        for copy in rec_copies:
            copy.start()
        from_base = []
        for k in range(16):
            rows = pl.ds(pl.multiple_of(384 + 64 * req, 64), 64)
            from_base.append(
                pltpu.make_async_copy(packed_ref.at[k, rows, :], base_ref.at[pl.ds(64 * k, 64), :], sems.at[k])
            )
        weights = [
            pltpu.make_async_copy(own_hbm, weights_out.at[0], sems.at[16]),
            pltpu.make_async_copy(other_hbm, weights_out.at[1], sems.at[17]),
        ]
        for copy in from_base + weights:
            copy.start()
        rec_vmem[64:, :] = jnp.zeros((64, 384), BF)
        match = iota((1024, 128), 0) == target_ref[0:1, :]
        chosen = jnp.where(match, 1.0, 0.0)
        hit = jnp.sum(chosen, axis=1, keepdims=True) > 0.5
        for copy in rec_copies:
            copy.wait()
        placed = jnp.dot(chosen.astype(BF), rec_vmem[...], preferred_element_type=F32)
        for copy in from_base:
            copy.wait()
        for patch in range(4):
            rows = slice(PLEN * patch, PLEN * patch + PLEN)

            @pl.when(patch <= section)
            def _(patch=patch, rows=rows):
                cache_ref[rows, :] = jnp.concatenate([fresh_ref[2 * patch], fresh_ref[2 * patch + 1]], axis=0)

            @pl.when(patch > section)
            def _(rows=rows):
                cache_ref[rows, :] = jnp.where(hit[rows], placed[rows], base_ref[rows, :].astype(F32)).astype(BF)

        attend(scalars, q_ref, cache_ref, keep_out, send_out)
        for copy in weights:
            copy.wait()

    return attend_kernel


def project_kernel(keep_ref, got_ref, weights_ref, out_ref):
    out = jnp.dot(keep_ref[:, 0:192], weights_ref[0], preferred_element_type=F32)
    out = out + jnp.dot(got_ref[:, 0:192], weights_ref[1], preferred_element_type=F32)
    out_ref[...] = out.astype(BF)


def residual_kernel_of(layer):
    def residual_kernel(scalars, parts_ref, x_ref, mod_ref, out_ref):
        row = iota((8, 128), 0)
        offset = (2 * (row >> 2) + scalars[0]) * 64 + 4 * scalars[10] + (row & 3)
        text = (offset + scalars[6]) < TXT
        for k in range(D // 128):
            lanes = slice(128 * k, 128 * k + 128)
            total = parts_ref[0, :, lanes].astype(F32)
            for source in range(1, 8):
                total = total + parts_ref[source, :, lanes].astype(F32)
            gate = jnp.where(text, mod_ref[layer, 5:6, lanes], mod_ref[layer, 2:3, lanes])
            out_ref[:, lanes] = (x_ref[:, lanes].astype(F32) + gate * total).astype(BF)

    return residual_kernel


def time_block(timestep, time_table):
    return lax.dynamic_slice(time_table, ((timestep[0] // 8) * 8, 0), (8, time_table.shape[1]))


def swapped(value, axis):
    return lax.ppermute(value, axis, [(0, 1), (1, 0)])


def local(
    hidden,
    patch_counts,
    timestep,
    time_table,
    ada_weight,
    qkv_weight,
    out_weight,
    qk_gain,
    stale_kv,
    stale_inputs,
    recompute_slots,
):
    section = lax.axis_index("section")
    req = lax.axis_index("req")
    half = lax.axis_index("half")
    core = lax.axis_index("core")
    col = lax.axis_index("z") * 2 + core
    first_req = req == 0
    sections = lax.axis_size("section")
    patches = hidden.shape[0]

    def of_request(value, axis):
        both = [lax.index_in_dim(value, r, axis, keepdims=False) for r in range(2)]
        return jnp.where(first_req, both[0], both[1]), jnp.where(first_req, both[1], both[0])

    def by_request(value, got):
        own = [lax.index_in_dim(value, r, 1, keepdims=False) for r in range(2)]
        far = [lax.index_in_dim(got, r, 1, keepdims=False) for r in range(2)]
        return jnp.where(
            first_req, jnp.concatenate([own[0], far[0]], axis=0), jnp.concatenate([far[1], own[1]], axis=0)
        )

    patch_rows = lax.dynamic_index_in_dim(hidden, section, 0, keepdims=False)
    tokens = by_request(patch_rows, swapped(patch_rows, "req"))
    rec_tokens = by_request(stale_inputs[0], swapped(stale_inputs[0], "req"))

    counts, _ = of_request(patch_counts, 0)
    starts = jnp.stack([jnp.int32(0), counts[0], counts[0] + counts[1], counts[0] + counts[1] + counts[2]])
    slots, _ = of_request(recompute_slots, 0)
    slots = slots.reshape(2, 2, 16)
    by_half = [slots[:, h].T.reshape(REC_GROUP) for h in range(2)]
    target_own = jnp.where(half == 0, by_half[0], by_half[1])
    targets = jnp.concatenate(by_half + [jnp.full((64,), -1, jnp.int32)])
    targets = jnp.broadcast_to(targets[None, :], (8, 128))

    own_start = lax.dynamic_index_in_dim(starts, section, 0, keepdims=True)
    row_index = req * 2 + half
    scalars = jnp.concatenate(
        [half[None], starts, timestep % 8, own_start, jnp.stack([section, row_index, core, col]), counts, req[None]]
    ).astype(jnp.int32)
    table_rows = shape_of((GROUP + REC_GROUP, 128), F32)
    mod_part, cosine, sine, text = call(
        prepare_kernel,
        (shape_of((2, 288), BF), table_rows, table_rows, table_rows),
        [SMEM, VMEM, VMEM, VMEM, VMEM],
        "prepare",
    )(
        scalars,
        time_block(timestep, time_table),
        ada_weight[0].T,
        jnp.asarray(frequencies()),
        jnp.broadcast_to(target_own[:, None], (REC_GROUP, 128)),
    )

    stale_rows = lax.dynamic_slice_in_dim(stale_kv[0], row_index * 256, 256, 0)
    stale_rows = jnp.transpose(stale_rows.reshape(4, 64, 2, 384), (0, 2, 1, 3)).reshape(4, 128, 384)
    weights_qkv = qkv_weight[0].T
    packed = call(
        pack_kernel,
        shape_of((4, 512, 384), BF),
        [SMEM, HBM, HBM, HBM],
        "pack",
        out_specs=HBM,
        scratch=[pltpu.SemaphoreType.DMA((12,))],
    )(scalars, weights_qkv, out_weight[0], stale_rows)
    chunks = lax.all_to_all(packed, "section", 0, 0)
    layers = [
        lax.all_gather(chunks[layer], ("req", "half", "section"), axis=0, tiled=False) for layer in range(sections)
    ]

    payload = jnp.concatenate(
        [
            tokens,
            rec_tokens.reshape(8, 768),
            jnp.pad(mod_part.reshape(8, 72), ((0, 0), (0, 56))),
        ],
        axis=1,
    )
    gathered = lax.all_gather(payload, COL, axis=0, tiled=True)
    rec_rows = gathered[:, D : D + 768].reshape(REC_GROUP, D)
    pieces = gathered[:, D + 768 : D + 840].reshape(16, 2, 288).astype(F32)
    summed = pieces[:, 0] + pieces[:, 1]
    gain_row = jnp.pad(qk_gain[0].reshape(1, 128), ((0, 0), (0, 160)))
    rows = lax.all_gather(jnp.concatenate([summed, gain_row], axis=0), ("section",) + ROW, axis=0, tiled=False)
    modulation = rows[:, :16].reshape(sections, 6, D)
    all_gains = rows.reshape(sections, 4, 17, 288)[:, 0, 16, :128].reshape(sections, 2, HD)
    all_gains = jnp.concatenate([all_gains, all_gains], axis=2)
    own_gains = jnp.concatenate([qk_gain[0], qk_gain[0]], axis=1)

    peers = ("section", "half")
    copies = lax.axis_size(peers)

    rec_fresh = call(
        rec_kernel,
        shape_of((copies, REC_GROUP, 384), BF),
        [SMEM] + [VMEM] * 6 + [HBM],
        "rec",
        scratch=[pltpu.VMEM((REC_GROUP, D), BF), pltpu.VMEM((576, D), BF), pltpu.SemaphoreType.DMA],
    )(scalars, rec_rows, modulation, own_gains, cosine[GROUP:], sine[GROUP:], text[GROUP:], weights_qkv)
    rec_all = lax.all_to_all(rec_fresh, peers, 0, 0)
    cosine, sine, text = cosine[:GROUP], sine[:GROUP], text[:GROUP]

    half_rows = shape_of((64, 256), BF)
    group, rec_all = lax.optimization_barrier((gathered[:, :D], rec_all))
    current, outs = tokens, []
    for layer in range(sections):
        packed = pltpu.with_memory_space_constraint(layers[layer], pltpu.HBM)
        if layer > 0:
            group = lax.all_gather(current, COL, axis=0, tiled=True)
        queries, fresh, out_own = call(
            qkv_kernel_of(layer),
            (shape_of((GROUP, 384), BF), shape_of((copies, GROUP, 384), BF), shape_of((192, D), BF)),
            [VMEM] * 6 + [HBM],
            "qkv",
            out_specs=(VMEM, VMEM, HBM),
            scratch=[pltpu.VMEM((GROUP, D), BF), pltpu.VMEM((576, D), BF), pltpu.SemaphoreType.DMA((32,))],
        )(group, modulation, all_gains[layer], cosine, sine, text, packed)
        out_other = swapped(out_own, "core")
        fresh = lax.all_to_all(fresh, peers, 0, 0)
        keep, send, weights_out = call(
            attend_kernel_of(layer),
            (half_rows, half_rows, shape_of((2, 192, D), BF)),
            [SMEM] + [VMEM] * 2 + [HBM, VMEM, HBM, HBM, HBM],
            "attend",
            scratch=[
                pltpu.VMEM((1024, 384), BF),
                pltpu.VMEM((1024, 384), BF),
                pltpu.VMEM((128, 384), BF),
                pltpu.SemaphoreType.DMA((20,)),
            ],
        )(scalars, queries, fresh, rec_all, targets, packed, out_own, out_other)
        projected = call(project_kernel, shape_of((64, D), BF), [VMEM] * 3, "project")(
            keep, swapped(send, "core"), weights_out
        )
        parts = lax.all_to_all(projected.reshape(8, 8, D), "z", 0, 0)
        current = call(residual_kernel_of(layer), shape_of((8, D), BF), [SMEM, VMEM, VMEM, VMEM], "residual")(
            scalars, parts, current, modulation
        )
        outs.append(current)

    leaving = jnp.stack(outs).reshape(sections * 2, 4, D)
    out = lax.all_to_all(leaving, ("section", "req"), 0, 0).reshape(patches, 2, 4, D)
    return jnp.transpose(out, (0, 2, 1, 3))[None]


def solution(mesh):
    sizes = tuple(mesh.devices.shape)
    fine = Mesh(
        mesh.devices.reshape(sizes[0], 2, sizes[1] // 2, sizes[2] // 2, 2),
        ("section", "req", "half", "z", "core"),
    )
    return jax.shard_map(
        local,
        mesh=fine,
        in_specs=(
            P(None, ROW_AXES, None, None),
            P(),
            P(),
            P(),
            P("section", None, ROW_AXES),
            P("section", None, COL),
            P("section", COL, None),
            P("section", None, None),
            P("section", None, None, COL, None),
            P("section", ROW_AXES, None, None),
            P(),
        ),
        out_specs=P("section", None, ROW_AXES, None, None),
        check_vma=False,
    )
```

```python
import jax
import jax.numpy as jnp
import numpy as np
from jax import lax
from jax.experimental import pallas as pl
from jax.experimental.pallas import tpu as pltpu
from jax.sharding import Mesh
from jax.sharding import PartitionSpec as P

HD = 64
D = 3072
TXT = 226
GH = 30
GW = 45
PLEN = 256
GROUP = 128
REC_GROUP = 32
STALE = 384
BF = jnp.bfloat16
F32 = jnp.float32
COL = ("z", "core")
ROW = ("req", "half")
ROW_AXES = ("req", "half", "z", "core")


SMEM = pl.BlockSpec(memory_space=pltpu.SMEM)
VMEM = pl.BlockSpec(memory_space=pltpu.VMEM)
HBM = pl.BlockSpec(memory_space=pltpu.HBM)


def call(kernel, out_shape, in_specs, name, out_specs=None, scratch=(), aliases=None):
    if out_specs is None:
        out_specs = jax.tree.map(lambda _: VMEM, out_shape)
    return pl.pallas_call(
        kernel,
        out_shape=out_shape,
        in_specs=in_specs,
        out_specs=out_specs,
        scratch_shapes=list(scratch),
        input_output_aliases=aliases or {},
        compiler_params=pltpu.CompilerParams(vmem_limit_bytes=24 * 1024 * 1024),
        name=name,
    )


def iota(shape, dim):
    return lax.broadcasted_iota(jnp.int32, shape, dim)


def shape_of(shape, dtype):
    return jax.ShapeDtypeStruct(shape, dtype)


def frequencies():
    parts = []
    for size in (HD // 4, HD * 3 // 8, HD * 3 // 8):
        rate = 1.0 / np.float32(10000.0) ** (
            np.arange(0, size, 2).astype(np.float32) / np.float32(size)
        )
        parts.append(np.repeat(rate.astype(np.float32), 2))
    rate = np.concatenate(parts)
    return np.concatenate([rate, rate])[None, :].astype(np.float32)


def offset_in_patch(index, half):
    return (2 * ((index >> 2) & 1) + half) * 64 + 4 * (index >> 3) + (index & 3)


def prepare_kernel(scalars, row_ref, ada_ref, rate_ref, rec_ref, mod_out, cos_out, sin_out, text_out):
    half = scalars[0]
    time_row = row_ref[pl.ds(scalars[5], 1), :]
    embedding = (time_row / (1.0 + jnp.exp(-time_row))).astype(BF)
    embedding = jnp.broadcast_to(embedding, (8, embedding.shape[1]))
    part = lax.dot_general(
        embedding, ada_ref[...], (((1,), (1,)), ((), ())), preferred_element_type=F32
    )[0:1]
    high = part.astype(BF)
    mod_out[0:1, :] = high
    mod_out[1:2, :] = (part - high.astype(F32)).astype(BF)

    rate = rate_ref[...]

    def tables(position, rows, at):
        text = position < TXT
        index = jnp.maximum(position - TXT, 0).astype(F32)
        frame = jnp.floor((index + 0.5) * (1.0 / (GH * GW)))
        line = jnp.floor((index + 0.5) * (1.0 / GW))
        width = index - line * GW
        height = line - jnp.floor((line + 0.5) * (1.0 / GH)) * GH
        lane = iota((rows, 128), 1) & (HD - 1)
        coordinate = jnp.where(lane < HD // 4, frame, jnp.where(lane < HD // 4 + HD * 3 // 8, height, width))
        phase = coordinate * rate
        cos_out[at : at + rows, :] = jnp.where(text, 1.0, jnp.cos(phase))
        sin_out[at : at + rows, :] = jnp.where(text, 0.0, jnp.sin(phase))
        text_out[at : at + rows, :] = jnp.where(text, 1.0, 0.0)

    tables(offset_in_patch(iota((GROUP, 128), 0), half) + scalars[6], GROUP, 0)
    slot = rec_ref[...]
    start = jnp.where(
        slot < PLEN,
        scalars[1],
        jnp.where(slot < 2 * PLEN, scalars[2], jnp.where(slot < 3 * PLEN, scalars[3], scalars[4])),
    )
    tables(start + (slot & (PLEN - 1)), REC_GROUP, GROUP)


def normalize(x_ref, mod_ref, layer, text_ref, norm_ref):
    chunks = D // 128
    rows = x_ref.shape[0]
    text = text_ref[...] > 0.5

    def over_chunks(step, start):
        return lax.fori_loop(0, chunks, lambda k, carry: step(pl.ds(pl.multiple_of(k * 128, 128), 128), carry), start, unroll=6)

    def add(lanes, total):
        return total + x_ref[:, lanes].astype(F32)

    mean = jnp.sum(over_chunks(add, jnp.zeros((rows, 128), F32)), axis=1, keepdims=True) * (1.0 / D)

    def add_square(lanes, total):
        centered = x_ref[:, lanes].astype(F32) - mean
        return total + centered * centered

    total = jnp.sum(over_chunks(add_square, jnp.zeros((rows, 128), F32)), axis=1, keepdims=True)
    factor = lax.rsqrt(total * (1.0 / D) + 1e-5)

    def write(lanes, carry):
        shift = jnp.where(text, mod_ref[layer, 3:4, lanes], mod_ref[layer, 0:1, lanes])
        scale = jnp.where(text, mod_ref[layer, 4:5, lanes], mod_ref[layer, 1:2, lanes])
        centered = x_ref[:, lanes].astype(F32) - mean
        norm_ref[:, lanes] = (centered * factor * (1.0 + scale) + shift).astype(BF)
        return carry

    over_chunks(write, 0)


def heads_from(mixed, gain_ref, cos_ref, sin_ref, q_out, kv_out):
    rows = mixed.shape[0]
    lane = iota((128, 128), 1)
    block = jnp.where((iota((128, 128), 0) >> 6) == (lane >> 6), 1.0 / HD, 0.0).astype(BF)

    def group_mean(values):
        high = values.astype(BF)
        low = (values - high.astype(F32)).astype(BF)
        return jnp.dot(high, block, preferred_element_type=F32) + jnp.dot(
            low, block, preferred_element_type=F32
        )

    low_half = iota((rows, 128), 1) < HD
    even = (iota((rows, 128), 1) & 1) == 0
    cosine, sine = cos_ref[...], sin_ref[...]
    gain_q = gain_ref[0:1, :]
    gain_k = gain_ref[1:2, :]
    gains = (
        jnp.where(low_half, gain_q, gain_k),
        jnp.broadcast_to(gain_q, (rows, 128)),
        jnp.broadcast_to(gain_k, (rows, 128)),
        jnp.where(low_half, gain_q, gain_k),
    )
    plain, turned = [], []
    for k in range(4):
        values = mixed[:, 128 * k : 128 * k + 128]
        plain.append(values)
        centered = values - group_mean(values)
        scaled = centered * lax.rsqrt(group_mean(centered * centered) + 1e-6) * gains[k]
        partner = jnp.where(even, -pltpu.roll(scaled, 127, 1), pltpu.roll(scaled, 1, 1))
        turned.append(scaled * cosine + partner * sine)
    last = jnp.concatenate([mixed[:, 512:576], jnp.zeros((rows, 64), F32)], axis=1)
    keys_values = (
        pltpu.roll(jnp.where(low_half, plain[1], turned[0]), 64, 1).astype(BF),
        jnp.where(low_half, turned[2], plain[2]).astype(BF),
        pltpu.roll(jnp.where(low_half, last, turned[3]), 64, 1).astype(BF),
    )
    for copy in range(kv_out.shape[0]):
        for head in range(3):
            kv_out[copy, 0:rows, 128 * head : 128 * head + 128] = keys_values[head]
    if q_out is None:
        return
    zero = jnp.zeros((rows, 128), F32)
    q_out[:, 0:128] = (jnp.where(low_half, turned[0], zero) * 0.125).astype(BF)
    q_out[:, 128:256] = (jnp.where(low_half, pltpu.roll(turned[1], 64, 1), zero) * 0.125).astype(BF)
    q_out[:, 256:384] = (jnp.where(low_half, turned[3], zero) * 0.125).astype(BF)


def times_weights(norm, weights):
    return lax.dot_general(norm, weights, (((1,), (1,)), ((), ())), preferred_element_type=F32)


def rec_kernel(scalars, x_ref, mod_ref, gain_ref, cos_ref, sin_ref, text_ref, w_ref, kv_out, norm_ref, w_vmem, sem):
    fetch = pltpu.make_async_copy(w_ref, w_vmem, sem)
    fetch.start()
    normalize(x_ref, mod_ref, scalars[7], text_ref, norm_ref)
    fetch.wait()
    heads_from(times_weights(norm_ref[...], w_vmem[...]), gain_ref, cos_ref, sin_ref, None, kv_out)


def qkv_kernel_of(layer):
    def qkv_kernel(x_ref, mod_ref, gain_ref, cos_ref, sin_ref, text_ref, rec_ref, packed_ref, q_out, kv_out, weights_out, norm_ref, w_vmem, sems):
        def fetch(k):
            to = w_vmem.at[pl.ds(288 * (k % 2), 288), pl.ds(384 * (k // 2), 384)]
            return pltpu.make_async_copy(packed_ref.at[k, pl.ds(0, 288), :], to, sems.at[k])

        def pass_on(k):
            to = weights_out.at[pl.ds(96 * (k % 2), 96), pl.ds(384 * (k // 2), 384)]
            return pltpu.make_async_copy(packed_ref.at[k, pl.ds(288, 96), :], to, sems.at[16 + k])

        for k in range(16):
            fetch(k).start()
        for k in range(16):
            pass_on(k).start()
        normalize(x_ref, mod_ref, layer, text_ref, norm_ref)
        mixed = jnp.zeros((GROUP, 576), F32)
        for piece in range(4):
            for k in range(4 * piece, 4 * piece + 4):
                fetch(k).wait()
            lanes = slice(768 * piece, 768 * piece + 768)
            mixed = mixed + times_weights(norm_ref[:, lanes], w_vmem[:, lanes])
        heads_from(mixed, gain_ref, cos_ref, sin_ref, q_out, kv_out)
        if layer == 0:
            for copy in range(kv_out.shape[0]):
                kv_out[copy, GROUP:, :] = rec_ref[0]
        for k in range(16):
            pass_on(k).wait()

    return qkv_kernel


def pack_kernel(row_ref, w_ref, out_ref, packed, sems):
    copies = []
    for k in range(4):
        lanes = pl.ds(pl.multiple_of(row_ref[0] * 768 + 384 * (k // 2), 128), 384)
        copies += [
            (w_ref.at[pl.ds(288 * (k % 2), 288), lanes], packed.at[k, pl.ds(0, 288), :]),
            (out_ref.at[pl.ds(96 * (k % 2), 96), lanes], packed.at[k, pl.ds(288, 96), :]),
        ]
    copies = [pltpu.make_async_copy(a, b, sems.at[n]) for n, (a, b) in enumerate(copies)]
    for copy in copies:
        copy.start()
    for copy in copies:
        copy.wait()


def attend(scalars, q_ref, cache_ref, keep_out, send_out):
    patch, core = scalars[7], scalars[9]
    key = iota((8, 1024), 1)
    key_patch = key >> 8
    within = key & (PLEN - 1)
    fresh_offset = (2 * ((within >> 2) & 1) + (within >> 7)) * 64 + 4 * ((within >> 3) & 15) + (within & 3)
    offset = jnp.where(key_patch <= patch, fresh_offset, within)
    count = jnp.where(
        key_patch == 0,
        scalars[11],
        jnp.where(key_patch == 1, scalars[12], jnp.where(key_patch == 2, scalars[13], scalars[14])),
    )
    live = (offset < count)[0:1]
    outs = []
    for head in range(3):
        lanes = slice(128 * head, 128 * head + 128)
        keys_values = cache_ref[:, lanes]
        scores = lax.dot_general(
            q_ref[:, lanes], keys_values, (((1,), (1,)), ((), ())), preferred_element_type=F32
        )
        weights = jnp.where(live, jnp.exp(scores), 0.0)
        total = jnp.sum(weights, axis=1, keepdims=True)
        mixed = jnp.dot(weights.astype(BF), keys_values, preferred_element_type=F32)
        outs.append(mixed / total)
    low = iota((GROUP, 128), 1) < HD
    first = jnp.where(low, pltpu.roll(outs[0], 64, 1), outs[1]).astype(BF)
    second = jnp.where(low, pltpu.roll(outs[2], 64, 1), 0.0).astype(BF)
    for z in range(8):
        to = slice(8 * z, 8 * z + 8)
        even, odd = slice(16 * z, 16 * z + 8), slice(16 * z + 8, 16 * z + 16)
        for value, lanes in ((first, slice(0, 128)), (second, slice(128, 256))):
            keep_out[to, lanes] = jnp.where(core == 0, value[even], value[odd])
            send_out[to, lanes] = jnp.where(core == 0, value[odd], value[even])


def attend_kernel_of(layer):
    def attend_kernel(
        scalars, q_ref, fresh_ref, target_ref, rec_ref, stale_ref, own_hbm, other_hbm,
        keep_out, send_out, weights_out, base_ref, cache_ref, rec_vmem, sems,
    ):
        section = scalars[7]
        rec_copies = [
            pltpu.make_async_copy(
                rec_ref.at[2 * layer + h, pl.ds(GROUP, REC_GROUP), :],
                rec_vmem.at[pl.ds(REC_GROUP * h, REC_GROUP), :],
                sems.at[4 + h],
            )
            for h in range(2)
        ]
        for copy in rec_copies:
            copy.start()
        from_base = [
            pltpu.make_async_copy(
                stale_ref.at[2 * layer + h], base_ref.at[pl.ds(PLEN + STALE * h, STALE), :], sems.at[h]
            )
            for h in range(2)
        ]
        weights = [
            pltpu.make_async_copy(own_hbm, weights_out.at[0], sems.at[2]),
            pltpu.make_async_copy(other_hbm, weights_out.at[1], sems.at[3]),
        ]
        for copy in from_base + weights:
            copy.start()
        rec_vmem[64:, :] = jnp.zeros((64, 384), BF)
        match = iota((1024, 128), 0) == target_ref[0:1, :]
        chosen = jnp.where(match, 1.0, 0.0)
        hit = jnp.sum(chosen, axis=1, keepdims=True) > 0.5
        for copy in rec_copies:
            copy.wait()
        placed = jnp.dot(chosen.astype(BF), rec_vmem[...], preferred_element_type=F32)
        for copy in from_base:
            copy.wait()
        for patch in range(4):
            rows = slice(PLEN * patch, PLEN * patch + PLEN)

            @pl.when(patch <= section)
            def _(patch=patch, rows=rows):
                cache_ref[rows, :] = jnp.concatenate(
                    [fresh_ref[2 * patch, 0:GROUP, :], fresh_ref[2 * patch + 1, 0:GROUP, :]], axis=0
                )

            if patch == 0:
                continue

            @pl.when(patch > section)
            def _(rows=rows):
                cache_ref[rows, :] = jnp.where(hit[rows], placed[rows], base_ref[rows, :].astype(F32)).astype(BF)

        attend(scalars, q_ref, cache_ref, keep_out, send_out)
        for copy in weights:
            copy.wait()

    return attend_kernel


def project_kernel(keep_ref, got_ref, weights_ref, out_ref):
    out = jnp.dot(keep_ref[:, 0:192], weights_ref[0], preferred_element_type=F32)
    out = out + jnp.dot(got_ref[:, 0:192], weights_ref[1], preferred_element_type=F32)
    out_ref[...] = out.astype(BF)


def residual_kernel_of(layer):
    def residual_kernel(scalars, parts_ref, x_ref, mod_ref, out_ref):
        row = iota((8, 128), 0)
        offset = (2 * (row >> 2) + scalars[0]) * 64 + 4 * scalars[10] + (row & 3)
        text = (offset + scalars[6]) < TXT
        for k in range(D // 128):
            lanes = slice(128 * k, 128 * k + 128)
            total = parts_ref[0, :, lanes].astype(F32)
            for source in range(1, 8):
                total = total + parts_ref[source, :, lanes].astype(F32)
            gate = jnp.where(text, mod_ref[layer, 5:6, lanes], mod_ref[layer, 2:3, lanes])
            out_ref[:, lanes] = (x_ref[:, lanes].astype(F32) + gate * total).astype(BF)

    return residual_kernel


def time_block(timestep, time_table):
    return lax.dynamic_slice(time_table, ((timestep[0] // 8) * 8, 0), (8, time_table.shape[1]))


def swapped(value, axis):
    return lax.ppermute(value, axis, [(0, 1), (1, 0)])


def local(
    hidden,
    patch_counts,
    timestep,
    time_table,
    ada_weight,
    qkv_weight,
    out_weight,
    qk_gain,
    stale_kv,
    stale_inputs,
    recompute_slots,
):
    section = lax.axis_index("section")
    req = lax.axis_index("req")
    half = lax.axis_index("half")
    core = lax.axis_index("core")
    col = lax.axis_index("z") * 2 + core
    first_req = req == 0
    sections = lax.axis_size("section")
    patches = hidden.shape[0]

    row_index = req * 2 + half
    weights_qkv = pltpu.with_memory_space_constraint(qkv_weight[0].T, pltpu.HBM)
    packed = call(
        pack_kernel,
        shape_of((4, 384, 384), BF),
        [SMEM, HBM, HBM],
        "pack",
        out_specs=HBM,
        scratch=[pltpu.SemaphoreType.DMA((8,))],
    )(
        row_index[None].astype(jnp.int32),
        weights_qkv,
        pltpu.with_memory_space_constraint(out_weight[0], pltpu.HBM),
    )
    chunks = lax.all_to_all(packed, "section", 0, 0)
    layers = [
        lax.all_gather(chunks[layer], ("req", "half", "section"), axis=0, tiled=False) for layer in range(sections)
    ]
    peers = ("section", "half")
    copies = lax.axis_size(peers)
    stale_share = lax.dynamic_slice(stale_kv, (0, PLEN + STALE * half, req, 0, 0), (1, STALE, 1, 3, 128))
    stale_share = stale_share.reshape(1, STALE, 384)
    stale_all = lax.all_to_all(jnp.broadcast_to(stale_share, (copies, STALE, 384)), peers, 0, 0)

    def of_request(value, axis):
        both = [lax.index_in_dim(value, r, axis, keepdims=False) for r in range(2)]
        return jnp.where(first_req, both[0], both[1]), jnp.where(first_req, both[1], both[0])

    def by_request(value, got):
        own = [lax.index_in_dim(value, r, 1, keepdims=False) for r in range(2)]
        far = [lax.index_in_dim(got, r, 1, keepdims=False) for r in range(2)]
        return jnp.where(
            first_req, jnp.concatenate([own[0], far[0]], axis=0), jnp.concatenate([far[1], own[1]], axis=0)
        )

    patch_rows = lax.dynamic_index_in_dim(hidden, section, 0, keepdims=False)
    tokens = by_request(patch_rows, swapped(patch_rows, "req"))
    rec_tokens = by_request(stale_inputs[0], swapped(stale_inputs[0], "req"))

    counts, _ = of_request(patch_counts, 0)
    starts = jnp.stack([jnp.int32(0), counts[0], counts[0] + counts[1], counts[0] + counts[1] + counts[2]])
    slots, _ = of_request(recompute_slots, 0)
    slots = slots.reshape(2, 2, 16)
    by_half = [slots[:, h].T.reshape(REC_GROUP) for h in range(2)]
    target_own = jnp.where(half == 0, by_half[0], by_half[1])
    targets = jnp.concatenate(by_half + [jnp.full((64,), -1, jnp.int32)])
    targets = jnp.broadcast_to(targets[None, :], (8, 128))

    own_start = lax.dynamic_index_in_dim(starts, section, 0, keepdims=True)
    scalars = jnp.concatenate(
        [half[None], starts, timestep % 8, own_start, jnp.stack([section, row_index, core, col]), counts, req[None]]
    ).astype(jnp.int32)
    table_rows = shape_of((GROUP + REC_GROUP, 128), F32)
    mod_part, cosine, sine, text = call(
        prepare_kernel,
        (shape_of((2, 288), BF), table_rows, table_rows, table_rows),
        [SMEM, VMEM, VMEM, VMEM, VMEM],
        "prepare",
    )(
        scalars,
        time_block(timestep, time_table),
        ada_weight[0].T,
        jnp.asarray(frequencies()),
        jnp.broadcast_to(target_own[:, None], (REC_GROUP, 128)),
    )

    payload = jnp.concatenate(
        [
            tokens,
            rec_tokens.reshape(8, 768),
            jnp.pad(mod_part.reshape(8, 72), ((0, 0), (0, 56))),
        ],
        axis=1,
    )
    gathered = lax.all_gather(payload, COL, axis=0, tiled=True)
    rec_rows = gathered[:, D : D + 768].reshape(REC_GROUP, D)
    pieces = gathered[:, D + 768 : D + 840].reshape(16, 2, 288).astype(F32)
    summed = pieces[:, 0] + pieces[:, 1]
    gain_row = jnp.pad(qk_gain[0].reshape(1, 128), ((0, 0), (0, 160)))
    rows = jnp.concatenate([summed, gain_row], axis=0)[None]
    everyone = ("section",) + ROW
    rows = lax.all_to_all(jnp.broadcast_to(rows, (lax.axis_size(everyone), 17, 288)), everyone, 0, 0)
    modulation = rows[:, :16].reshape(sections, 6, D)
    all_gains = rows.reshape(sections, 4, 17, 288)[:, 0, 16, :128].reshape(sections, 2, HD)
    all_gains = jnp.concatenate([all_gains, all_gains], axis=2)
    own_gains = jnp.concatenate([qk_gain[0], qk_gain[0]], axis=1)

    rec_fresh = call(
        rec_kernel,
        shape_of((1, REC_GROUP, 384), BF),
        [SMEM] + [VMEM] * 6 + [HBM],
        "rec",
        scratch=[pltpu.VMEM((REC_GROUP, D), BF), pltpu.VMEM((576, D), BF), pltpu.SemaphoreType.DMA],
    )(scalars, rec_rows, modulation, own_gains, cosine[GROUP:], sine[GROUP:], text[GROUP:], weights_qkv)
    cosine, sine, text = cosine[:GROUP], sine[:GROUP], text[:GROUP]

    half_rows = shape_of((64, 256), BF)
    current, group, outs, first_fresh = tokens, gathered[:, :D], [], None
    for layer in range(sections):
        packed = pltpu.with_memory_space_constraint(layers[layer], pltpu.HBM)
        if layer > 0:
            group = lax.all_gather(current, COL, axis=0, tiled=True)
        queries, fresh, out_own = call(
            qkv_kernel_of(layer),
            (
                shape_of((GROUP, 384), BF),
                shape_of((copies, GROUP + (REC_GROUP if layer == 0 else 0), 384), BF),
                shape_of((192, D), BF),
            ),
            [VMEM] * 7 + [HBM],
            "qkv",
            scratch=[pltpu.VMEM((GROUP, D), BF), pltpu.VMEM((576, D), BF), pltpu.SemaphoreType.DMA((32,))],
        )(group, modulation, all_gains[layer], cosine, sine, text, rec_fresh, packed)
        out_other = swapped(out_own, "core")
        fresh = lax.all_to_all(fresh, peers, 0, 0)
        first_fresh = fresh if layer == 0 else first_fresh
        keep, send, weights_out = call(
            attend_kernel_of(layer),
            (half_rows, half_rows, shape_of((2, 192, D), BF)),
            [SMEM] + [VMEM] * 3 + [HBM] * 4,
            "attend",
            scratch=[
                pltpu.VMEM((1024, 384), BF),
                pltpu.VMEM((1024, 384), BF),
                pltpu.VMEM((128, 384), BF),
                pltpu.SemaphoreType.DMA((6,)),
            ],
        )(scalars, queries, fresh, targets, first_fresh, stale_all, out_own, out_other)
        projected = call(project_kernel, shape_of((64, D), BF), [VMEM] * 3, "project")(
            keep, swapped(send, "core"), weights_out
        )
        parts = lax.all_to_all(projected.reshape(8, 8, D), "z", 0, 0)
        current = call(residual_kernel_of(layer), shape_of((8, D), BF), [SMEM, VMEM, VMEM, VMEM], "residual")(
            scalars, parts, current, modulation
        )
        outs.append(current)

    leaving = jnp.stack(outs).reshape(sections * 2, 4, D)
    out = lax.all_to_all(leaving, ("section", "req"), 0, 0).reshape(patches, 2, 4, D)
    return jnp.transpose(out, (0, 2, 1, 3))[None]


def solution(mesh):
    sizes = tuple(mesh.devices.shape)
    fine = Mesh(
        mesh.devices.reshape(sizes[0], 2, sizes[1] // 2, sizes[2] // 2, 2),
        ("section", "req", "half", "z", "core"),
    )
    return jax.shard_map(
        local,
        mesh=fine,
        in_specs=(
            P(None, ROW_AXES, None, None),
            P(),
            P(),
            P(),
            P("section", None, ROW_AXES),
            P("section", None, COL),
            P("section", COL, None),
            P("section", None, None),
            P("section", None, None, COL, None),
            P("section", ROW_AXES, None, None),
            P(),
        ),
        out_specs=P("section", None, ROW_AXES, None, None),
        check_vma=False,
    )
```

```python
import jax
import jax.numpy as jnp
import numpy as np
from jax import lax
from jax.experimental import pallas as pl
from jax.experimental.pallas import tpu as pltpu
from jax.sharding import Mesh
from jax.sharding import PartitionSpec as P

HD = 64
D = 3072
TXT = 226
GH = 30
GW = 45
PLEN = 256
GROUP = 128
REC_GROUP = 32
STALE = 384
BF = jnp.bfloat16
F32 = jnp.float32
COL = ("z", "core")
ROW = ("req", "half")
ROW_AXES = ("req", "half", "z", "core")


SMEM = pl.BlockSpec(memory_space=pltpu.SMEM)
VMEM = pl.BlockSpec(memory_space=pltpu.VMEM)
HBM = pl.BlockSpec(memory_space=pltpu.HBM)


def call(kernel, out_shape, in_specs, name, out_specs=None, scratch=(), aliases=None):
    if out_specs is None:
        out_specs = jax.tree.map(lambda _: VMEM, out_shape)
    return pl.pallas_call(
        kernel,
        out_shape=out_shape,
        in_specs=in_specs,
        out_specs=out_specs,
        scratch_shapes=list(scratch),
        input_output_aliases=aliases or {},
        compiler_params=pltpu.CompilerParams(vmem_limit_bytes=24 * 1024 * 1024),
        name=name,
    )


def iota(shape, dim):
    return lax.broadcasted_iota(jnp.int32, shape, dim)


def shape_of(shape, dtype):
    return jax.ShapeDtypeStruct(shape, dtype)


def frequencies():
    parts = []
    for size in (HD // 4, HD * 3 // 8, HD * 3 // 8):
        rate = 1.0 / np.float32(10000.0) ** (
            np.arange(0, size, 2).astype(np.float32) / np.float32(size)
        )
        parts.append(np.repeat(rate.astype(np.float32), 2))
    rate = np.concatenate(parts)
    return np.concatenate([rate, rate])[None, :].astype(np.float32)


def offset_in_patch(index, half):
    return (2 * ((index >> 2) & 1) + half) * 64 + 4 * (index >> 3) + (index & 3)


def prepare_kernel(scalars, row_ref, ada_ref, rate_ref, rec_ref, mod_out, tables_out):
    half = scalars[0]
    time_row = row_ref[pl.ds(scalars[5], 1), :]
    embedding = (time_row / (1.0 + jnp.exp(-time_row))).astype(BF)
    embedding = jnp.broadcast_to(embedding, (8, embedding.shape[1]))
    part = lax.dot_general(
        embedding, ada_ref[...], (((1,), (1,)), ((), ())), preferred_element_type=F32
    )[0:1]
    high = part.astype(BF)
    mod_out[0:1, :] = high
    mod_out[1:2, :] = (part - high.astype(F32)).astype(BF)

    rate = rate_ref[...]

    def tables(position, rows, at):
        text = position < TXT
        index = jnp.maximum(position - TXT, 0).astype(F32)
        frame = jnp.floor((index + 0.5) * (1.0 / (GH * GW)))
        line = jnp.floor((index + 0.5) * (1.0 / GW))
        width = index - line * GW
        height = line - jnp.floor((line + 0.5) * (1.0 / GH)) * GH
        lane = iota((rows, 128), 1) & (HD - 1)
        coordinate = jnp.where(lane < HD // 4, frame, jnp.where(lane < HD // 4 + HD * 3 // 8, height, width))
        phase = coordinate * rate
        tables_out[0, at : at + rows, :] = jnp.where(text, 1.0, jnp.cos(phase))
        tables_out[1, at : at + rows, :] = jnp.where(text, 0.0, jnp.sin(phase))
        tables_out[2, at : at + rows, :] = jnp.where(text, 1.0, 0.0)

    tables(offset_in_patch(iota((GROUP, 128), 0), half) + scalars[6], GROUP, 0)
    slot = rec_ref[...]
    start = jnp.where(
        slot < PLEN,
        scalars[1],
        jnp.where(slot < 2 * PLEN, scalars[2], jnp.where(slot < 3 * PLEN, scalars[3], scalars[4])),
    )
    tables(start + (slot & (PLEN - 1)), REC_GROUP, GROUP)


def normalize(x_ref, mod_ref, tables_ref, norm_ref, small):
    chunks = D // 128
    rows = x_ref.shape[0]

    def over_chunks(step, start):
        return lax.fori_loop(0, chunks, lambda k, carry: step(pl.ds(pl.multiple_of(k * 128, 128), 128), carry), start, unroll=6)

    def add(lanes, total):
        return total + x_ref[:, lanes].astype(F32)

    mean = jnp.sum(over_chunks(add, jnp.zeros((rows, 128), F32)), axis=1, keepdims=True) * (1.0 / D)

    def add_square(lanes, total):
        centered = x_ref[:, lanes].astype(F32) - mean
        return total + centered * centered

    total = jnp.sum(over_chunks(add_square, jnp.zeros((rows, 128), F32)), axis=1, keepdims=True)
    factor = lax.rsqrt(total * (1.0 / D) + 1e-5)
    for copy in small:
        copy.wait()
    text = tables_ref[2] > 0.5

    def write(lanes, carry):
        shift = jnp.where(text, mod_ref[3:4, lanes], mod_ref[0:1, lanes])
        scale = jnp.where(text, mod_ref[4:5, lanes], mod_ref[1:2, lanes])
        centered = x_ref[:, lanes].astype(F32) - mean
        norm_ref[:, lanes] = (centered * factor * (1.0 + scale) + shift).astype(BF)
        return carry

    over_chunks(write, 0)


def heads_from(mixed, gain_ref, tables_ref, q_out, kv_out):
    rows = mixed.shape[0]
    lane = iota((128, 128), 1)
    block = jnp.where((iota((128, 128), 0) >> 6) == (lane >> 6), 1.0 / HD, 0.0).astype(BF)

    def group_mean(values):
        high = values.astype(BF)
        low = (values - high.astype(F32)).astype(BF)
        return jnp.dot(high, block, preferred_element_type=F32) + jnp.dot(
            low, block, preferred_element_type=F32
        )

    low_half = iota((rows, 128), 1) < HD
    even = (iota((rows, 128), 1) & 1) == 0
    cosine, sine = tables_ref[0], tables_ref[1]
    gain = gain_ref[...]
    other_gain = pltpu.roll(jnp.broadcast_to(gain, (8, 128)), 64, 1)[0:1]
    gains = (gain, other_gain, other_gain, gain)
    plain, turned = [], []
    for k in range(4):
        values = mixed[:, 128 * k : 128 * k + 128]
        plain.append(values)
        centered = values - group_mean(values)
        scaled = centered * lax.rsqrt(group_mean(centered * centered) + 1e-6) * gains[k]
        partner = jnp.where(even, -pltpu.roll(scaled, 127, 1), pltpu.roll(scaled, 1, 1))
        turned.append(scaled * cosine + partner * sine)
    last = jnp.concatenate([mixed[:, 512:576], jnp.zeros((rows, 64), F32)], axis=1)
    keys_values = (
        pltpu.roll(jnp.where(low_half, plain[1], turned[0]), 64, 1).astype(BF),
        jnp.where(low_half, turned[2], plain[2]).astype(BF),
        pltpu.roll(jnp.where(low_half, last, turned[3]), 64, 1).astype(BF),
    )
    for copy in range(kv_out.shape[0]):
        for head in range(3):
            kv_out[copy, 0:rows, 128 * head : 128 * head + 128] = keys_values[head]
    if q_out is None:
        return
    zero = jnp.zeros((rows, 128), F32)
    q_out[:, 0:128] = (jnp.where(low_half, turned[0], zero) * 0.125).astype(BF)
    q_out[:, 128:256] = (jnp.where(low_half, pltpu.roll(turned[1], 64, 1), zero) * 0.125).astype(BF)
    q_out[:, 256:384] = (jnp.where(low_half, turned[3], zero) * 0.125).astype(BF)


def times_weights(norm, weights):
    return lax.dot_general(norm, weights, (((1,), (1,)), ((), ())), preferred_element_type=F32)


def small_copies(mod_hbm, rows_hbm, tables_hbm, layer, rows, mod_ref, gain_ref, tables_ref, sems):
    copies = [
        pltpu.make_async_copy(mod_hbm.at[layer], mod_ref, sems.at[0]),
        pltpu.make_async_copy(rows_hbm.at[4 * layer, pl.ds(16, 1), pl.ds(0, 128)], gain_ref, sems.at[1]),
        pltpu.make_async_copy(tables_hbm.at[:, rows, :], tables_ref, sems.at[2]),
    ]
    for copy in copies:
        copy.start()
    return copies


def small_scratch(rows):
    return [
        pltpu.VMEM((6, D), F32),
        pltpu.VMEM((1, 128), F32),
        pltpu.VMEM((3, rows, 128), F32),
        pltpu.SemaphoreType.DMA((3,)),
    ]


def rec_kernel(
    scalars, gathered_ref, mod_hbm, rows_hbm, tables_hbm, w_ref,
    kv_out, x_ref, norm_ref, w_vmem, sem, mod_ref, gain_ref, tables_ref, sems,
):
    fetch = pltpu.make_async_copy(w_ref, w_vmem, sem)
    fetch.start()
    rows = pl.ds(GROUP, REC_GROUP)
    small = small_copies(mod_hbm, rows_hbm, tables_hbm, scalars[7], rows, mod_ref, gain_ref, tables_ref, sems)
    share = gathered_ref[:, D : D + 768]
    for k in range(4):
        pick = iota((REC_GROUP, GROUP), 1) == 4 * iota((REC_GROUP, GROUP), 0) + k
        pick = jnp.where(pick, 1.0, 0.0).astype(BF)
        x_ref[:, 768 * k : 768 * k + 768] = jnp.dot(pick, share, preferred_element_type=F32).astype(BF)
    normalize(x_ref, mod_ref, tables_ref, norm_ref, small)
    fetch.wait()
    heads_from(times_weights(norm_ref[...], w_vmem[...]), gain_ref, tables_ref, None, kv_out)


def qkv_kernel_of(layer):
    def qkv_kernel(
        x_ref, rec_ref, mod_hbm, rows_hbm, tables_hbm, packed_ref,
        q_out, kv_out, weights_out, norm_ref, w_vmem, sems, mod_ref, gain_ref, tables_ref, small_sems,
    ):
        rows = pl.ds(0, GROUP)
        small = small_copies(mod_hbm, rows_hbm, tables_hbm, layer, rows, mod_ref, gain_ref, tables_ref, small_sems)

        def fetch(k):
            to = w_vmem.at[pl.ds(288 * (k % 2), 288), pl.ds(384 * (k // 2), 384)]
            return pltpu.make_async_copy(packed_ref.at[k, pl.ds(0, 288), :], to, sems.at[k])

        def pass_on(k):
            to = weights_out.at[pl.ds(96 * (k % 2), 96), pl.ds(384 * (k // 2), 384)]
            return pltpu.make_async_copy(packed_ref.at[k, pl.ds(288, 96), :], to, sems.at[16 + k])

        for k in range(16):
            fetch(k).start()
        for k in range(16):
            pass_on(k).start()
        normalize(x_ref, mod_ref, tables_ref, norm_ref, small)
        mixed = jnp.zeros((GROUP, 576), F32)
        for piece in range(4):
            for k in range(4 * piece, 4 * piece + 4):
                fetch(k).wait()
            lanes = slice(768 * piece, 768 * piece + 768)
            mixed = mixed + times_weights(norm_ref[:, lanes], w_vmem[:, lanes])
        heads_from(mixed, gain_ref, tables_ref, q_out, kv_out)
        if layer == 0:
            for copy in range(kv_out.shape[0]):
                kv_out[copy, GROUP:, :] = rec_ref[0]
        for k in range(16):
            pass_on(k).wait()

    return qkv_kernel


def pack_kernel(row_ref, w_ref, out_ref, packed, sems):
    copies = []
    for k in range(4):
        lanes = pl.ds(pl.multiple_of(row_ref[0] * 768 + 384 * (k // 2), 128), 384)
        copies += [
            (w_ref.at[pl.ds(288 * (k % 2), 288), lanes], packed.at[k, pl.ds(0, 288), :]),
            (out_ref.at[pl.ds(96 * (k % 2), 96), lanes], packed.at[k, pl.ds(288, 96), :]),
        ]
    copies = [pltpu.make_async_copy(a, b, sems.at[n]) for n, (a, b) in enumerate(copies)]
    for copy in copies:
        copy.start()
    for copy in copies:
        copy.wait()


def attend(scalars, q_ref, cache_ref, keep_out, send_out):
    patch, core = scalars[7], scalars[9]
    key = iota((8, 1024), 1)
    key_patch = key >> 8
    within = key & (PLEN - 1)
    fresh_offset = (2 * ((within >> 2) & 1) + (within >> 7)) * 64 + 4 * ((within >> 3) & 15) + (within & 3)
    offset = jnp.where(key_patch <= patch, fresh_offset, within)
    count = jnp.where(
        key_patch == 0,
        scalars[11],
        jnp.where(key_patch == 1, scalars[12], jnp.where(key_patch == 2, scalars[13], scalars[14])),
    )
    live = (offset < count)[0:1]
    outs = []
    for head in range(3):
        lanes = slice(128 * head, 128 * head + 128)
        keys_values = cache_ref[:, lanes]
        scores = lax.dot_general(
            q_ref[:, lanes], keys_values, (((1,), (1,)), ((), ())), preferred_element_type=F32
        )
        weights = jnp.where(live, jnp.exp(scores), 0.0)
        total = jnp.sum(weights, axis=1, keepdims=True)
        mixed = jnp.dot(weights.astype(BF), keys_values, preferred_element_type=F32)
        outs.append(mixed / total)
    low = iota((GROUP, 128), 1) < HD
    first = jnp.where(low, pltpu.roll(outs[0], 64, 1), outs[1]).astype(BF)
    second = jnp.where(low, pltpu.roll(outs[2], 64, 1), 0.0).astype(BF)
    for z in range(8):
        to = slice(8 * z, 8 * z + 8)
        even, odd = slice(16 * z, 16 * z + 8), slice(16 * z + 8, 16 * z + 16)
        for value, lanes in ((first, slice(0, 128)), (second, slice(128, 256))):
            keep_out[to, lanes] = jnp.where(core == 0, value[even], value[odd])
            send_out[to, lanes] = jnp.where(core == 0, value[odd], value[even])


def attend_kernel_of(layer):
    def attend_kernel(
        scalars, q_ref, fresh_ref, targets_hbm, rec_ref, stale_ref, own_hbm, other_hbm,
        keep_out, send_out, weights_out, base_ref, cache_ref, rec_vmem, target_ref, sems,
    ):
        section = scalars[7]
        rec_copies = [
            pltpu.make_async_copy(
                rec_ref.at[2 * layer + h, pl.ds(GROUP, REC_GROUP), :],
                rec_vmem.at[pl.ds(REC_GROUP * h, REC_GROUP), :],
                sems.at[4 + h],
            )
            for h in range(2)
        ]
        rec_copies.append(pltpu.make_async_copy(targets_hbm, target_ref, sems.at[6]))
        for copy in rec_copies:
            copy.start()
        from_base = [
            pltpu.make_async_copy(
                stale_ref.at[2 * layer + h], base_ref.at[pl.ds(PLEN + STALE * h, STALE), :], sems.at[h]
            )
            for h in range(2)
        ]
        weights = [
            pltpu.make_async_copy(own_hbm, weights_out.at[0], sems.at[2]),
            pltpu.make_async_copy(other_hbm, weights_out.at[1], sems.at[3]),
        ]
        for copy in from_base + weights:
            copy.start()
        rec_vmem[64:, :] = jnp.zeros((64, 384), BF)
        for copy in rec_copies:
            copy.wait()
        match = iota((1024, 128), 0) == target_ref[0:1, :]
        chosen = jnp.where(match, 1.0, 0.0)
        hit = jnp.sum(chosen, axis=1, keepdims=True) > 0.5
        placed = jnp.dot(chosen.astype(BF), rec_vmem[...], preferred_element_type=F32)
        for copy in from_base:
            copy.wait()
        for patch in range(4):
            rows = slice(PLEN * patch, PLEN * patch + PLEN)

            @pl.when(patch <= section)
            def _(patch=patch, rows=rows):
                cache_ref[rows, :] = jnp.concatenate(
                    [fresh_ref[2 * patch, 0:GROUP, :], fresh_ref[2 * patch + 1, 0:GROUP, :]], axis=0
                )

            if patch == 0:
                continue

            @pl.when(patch > section)
            def _(rows=rows):
                cache_ref[rows, :] = jnp.where(hit[rows], placed[rows], base_ref[rows, :].astype(F32)).astype(BF)

        attend(scalars, q_ref, cache_ref, keep_out, send_out)
        for copy in weights:
            copy.wait()

    return attend_kernel


def project_kernel(keep_ref, got_ref, weights_ref, out_ref):
    out = jnp.dot(keep_ref[:, 0:192], weights_ref[0], preferred_element_type=F32)
    out = out + jnp.dot(got_ref[:, 0:192], weights_ref[1], preferred_element_type=F32)
    out_ref[...] = out.astype(BF)


def residual_kernel_of(layer):
    def residual_kernel(scalars, parts_ref, x_ref, mod_hbm, out_ref, mod_ref, sem):
        fetch = pltpu.make_async_copy(mod_hbm.at[layer], mod_ref, sem)
        fetch.start()
        row = iota((8, 128), 0)
        offset = (2 * (row >> 2) + scalars[0]) * 64 + 4 * scalars[10] + (row & 3)
        text = (offset + scalars[6]) < TXT
        chunks = [slice(128 * k, 128 * k + 128) for k in range(D // 128)]
        totals = []
        for lanes in chunks:
            total = parts_ref[0, :, lanes].astype(F32)
            for source in range(1, 8):
                total = total + parts_ref[source, :, lanes].astype(F32)
            totals.append(total)
        fetch.wait()
        for lanes, total in zip(chunks, totals):
            gate = jnp.where(text, mod_ref[5:6, lanes], mod_ref[2:3, lanes])
            out_ref[:, lanes] = (x_ref[:, lanes].astype(F32) + gate * total).astype(BF)

    return residual_kernel


def time_block(timestep, time_table):
    return lax.dynamic_slice(time_table, ((timestep[0] // 8) * 8, 0), (8, time_table.shape[1]))


def swapped(value, axis):
    return lax.ppermute(value, axis, [(0, 1), (1, 0)])


def local(
    hidden,
    patch_counts,
    timestep,
    time_table,
    ada_weight,
    qkv_weight,
    out_weight,
    qk_gain,
    stale_kv,
    stale_inputs,
    recompute_slots,
):
    section = lax.axis_index("section")
    req = lax.axis_index("req")
    half = lax.axis_index("half")
    core = lax.axis_index("core")
    col = lax.axis_index("z") * 2 + core
    first_req = req == 0
    sections = lax.axis_size("section")
    patches = hidden.shape[0]

    row_index = req * 2 + half
    weights_qkv = pltpu.with_memory_space_constraint(qkv_weight[0].T, pltpu.HBM)
    packed = call(
        pack_kernel,
        shape_of((4, 384, 384), BF),
        [SMEM, HBM, HBM],
        "pack",
        out_specs=HBM,
        scratch=[pltpu.SemaphoreType.DMA((8,))],
    )(
        row_index[None].astype(jnp.int32),
        weights_qkv,
        pltpu.with_memory_space_constraint(out_weight[0], pltpu.HBM),
    )
    chunks = lax.all_to_all(packed, "section", 0, 0)
    layers = [
        lax.all_gather(chunks[layer], ("req", "half", "section"), axis=0, tiled=False) for layer in range(sections)
    ]
    peers = ("section", "half")
    copies = lax.axis_size(peers)
    stale_share = lax.dynamic_slice(stale_kv, (0, PLEN + STALE * half, req, 0, 0), (1, STALE, 1, 3, 128))
    stale_share = stale_share.reshape(1, STALE, 384)
    stale_all = lax.all_to_all(jnp.broadcast_to(stale_share, (copies, STALE, 384)), peers, 0, 0)

    def of_request(value, axis):
        both = [lax.index_in_dim(value, r, axis, keepdims=False) for r in range(2)]
        return jnp.where(first_req, both[0], both[1]), jnp.where(first_req, both[1], both[0])

    def by_request(value, got):
        own = [lax.index_in_dim(value, r, 1, keepdims=False) for r in range(2)]
        far = [lax.index_in_dim(got, r, 1, keepdims=False) for r in range(2)]
        return jnp.where(
            first_req, jnp.concatenate([own[0], far[0]], axis=0), jnp.concatenate([far[1], own[1]], axis=0)
        )

    patch_rows = lax.dynamic_index_in_dim(hidden, section, 0, keepdims=False)
    tokens = by_request(patch_rows, swapped(patch_rows, "req"))
    rec_tokens = by_request(stale_inputs[0], swapped(stale_inputs[0], "req"))

    counts, _ = of_request(patch_counts, 0)
    starts = jnp.stack([jnp.int32(0), counts[0], counts[0] + counts[1], counts[0] + counts[1] + counts[2]])
    slots, _ = of_request(recompute_slots, 0)
    slots = slots.reshape(2, 2, 16)
    by_half = [slots[:, h].T.reshape(REC_GROUP) for h in range(2)]
    target_own = jnp.where(half == 0, by_half[0], by_half[1])
    targets = jnp.concatenate(by_half + [jnp.full((64,), -1, jnp.int32)])
    targets = jnp.broadcast_to(targets[None, :], (8, 128))

    own_start = lax.dynamic_index_in_dim(starts, section, 0, keepdims=True)
    scalars = jnp.concatenate(
        [half[None], starts, timestep % 8, own_start, jnp.stack([section, row_index, core, col]), counts, req[None]]
    ).astype(jnp.int32)
    mod_part, tables = call(
        prepare_kernel,
        (shape_of((2, 288), BF), shape_of((3, GROUP + REC_GROUP, 128), F32)),
        [SMEM, VMEM, VMEM, VMEM, VMEM],
        "prepare",
    )(
        scalars,
        time_block(timestep, time_table),
        ada_weight[0].T,
        jnp.asarray(frequencies()),
        jnp.broadcast_to(target_own[:, None], (REC_GROUP, 128)),
    )

    payload = jnp.concatenate(
        [
            tokens,
            rec_tokens.reshape(8, 768),
            jnp.pad(mod_part.reshape(8, 72), ((0, 0), (0, 56))),
        ],
        axis=1,
    )
    gathered = lax.all_gather(payload, COL, axis=0, tiled=True)
    pieces = gathered[:, D + 768 : D + 840].reshape(16, 2, 288).astype(F32)
    summed = pieces[:, 0] + pieces[:, 1]
    gain_row = jnp.pad(qk_gain[0].reshape(1, 128), ((0, 0), (0, 160)))
    rows = jnp.concatenate([summed, gain_row], axis=0)[None]
    everyone = ("section",) + ROW
    rows = lax.all_to_all(jnp.broadcast_to(rows, (lax.axis_size(everyone), 17, 288)), everyone, 0, 0)
    modulation = rows[:, :16].reshape(sections, 6, D)
    in_hbm = [pltpu.with_memory_space_constraint(value, pltpu.HBM) for value in (modulation, rows, tables)]
    rec_fresh = call(
        rec_kernel,
        shape_of((1, REC_GROUP, 384), BF),
        [SMEM, VMEM] + [HBM] * 4,
        "rec",
        scratch=[
            pltpu.VMEM((REC_GROUP, D), BF),
            pltpu.VMEM((REC_GROUP, D), BF),
            pltpu.VMEM((576, D), BF),
            pltpu.SemaphoreType.DMA,
        ]
        + small_scratch(REC_GROUP),
    )(scalars, gathered, *in_hbm, weights_qkv)
    targets = pltpu.with_memory_space_constraint(targets, pltpu.HBM)

    half_rows = shape_of((64, 256), BF)
    current, group, outs, first_fresh = tokens, gathered, [], None
    for layer in range(sections):
        packed = pltpu.with_memory_space_constraint(layers[layer], pltpu.HBM)
        if layer > 0:
            group = lax.all_gather(current, COL, axis=0, tiled=True)
        queries, fresh, out_own = call(
            qkv_kernel_of(layer),
            (
                shape_of((GROUP, 384), BF),
                shape_of((copies, GROUP + (REC_GROUP if layer == 0 else 0), 384), BF),
                shape_of((192, D), BF),
            ),
            [VMEM] * 2 + [HBM] * 4,
            "qkv",
            scratch=[pltpu.VMEM((GROUP, D), BF), pltpu.VMEM((576, D), BF), pltpu.SemaphoreType.DMA((32,))]
            + small_scratch(GROUP),
        )(group, rec_fresh, *in_hbm, packed)
        out_other = swapped(out_own, "core")
        fresh = lax.all_to_all(fresh, peers, 0, 0)
        first_fresh = fresh if layer == 0 else first_fresh
        keep, send, weights_out = call(
            attend_kernel_of(layer),
            (half_rows, half_rows, shape_of((2, 192, D), BF)),
            [SMEM] + [VMEM] * 2 + [HBM] * 5,
            "attend",
            scratch=[
                pltpu.VMEM((1024, 384), BF),
                pltpu.VMEM((1024, 384), BF),
                pltpu.VMEM((128, 384), BF),
                pltpu.VMEM((8, 128), jnp.int32),
                pltpu.SemaphoreType.DMA((7,)),
            ],
        )(scalars, queries, fresh, targets, first_fresh, stale_all, out_own, out_other)
        projected = call(project_kernel, shape_of((64, D), BF), [VMEM] * 3, "project")(
            keep, swapped(send, "core"), weights_out
        )
        parts = lax.all_to_all(projected.reshape(8, 8, D), "z", 0, 0)
        current = call(
            residual_kernel_of(layer),
            shape_of((8, D), BF),
            [SMEM, VMEM, VMEM, HBM],
            "residual",
            scratch=[pltpu.VMEM((6, D), F32), pltpu.SemaphoreType.DMA],
        )(scalars, parts, current, in_hbm[0])
        outs.append(current)

    leaving = jnp.stack(outs).reshape(sections * 2, 4, D)
    out = lax.all_to_all(leaving, ("section", "req"), 0, 0).reshape(patches, 2, 4, D)
    return jnp.transpose(out, (0, 2, 1, 3))[None]


def solution(mesh):
    sizes = tuple(mesh.devices.shape)
    fine = Mesh(
        mesh.devices.reshape(sizes[0], 2, sizes[1] // 2, sizes[2] // 2, 2),
        ("section", "req", "half", "z", "core"),
    )
    return jax.shard_map(
        local,
        mesh=fine,
        in_specs=(
            P(None, ROW_AXES, None, None),
            P(),
            P(),
            P(),
            P("section", None, ROW_AXES),
            P("section", None, COL),
            P("section", COL, None),
            P("section", None, None),
            P("section", None, None, COL, None),
            P("section", ROW_AXES, None, None),
            P(),
        ),
        out_specs=P("section", None, ROW_AXES, None, None),
        check_vma=False,
    )
```

```python
import jax
import jax.numpy as jnp
import numpy as np
from jax import lax
from jax.experimental import pallas as pl
from jax.experimental.pallas import tpu as pltpu
from jax.sharding import Mesh
from jax.sharding import PartitionSpec as P

HD = 64
D = 3072
TXT = 226
GH = 30
GW = 45
PLEN = 256
GROUP = 128
REC_GROUP = 32
STALE = 384
BF = jnp.bfloat16
F32 = jnp.float32
COL = ("z", "core")
ROW = ("req", "half")
ROW_AXES = ("req", "half", "z", "core")


SMEM = pl.BlockSpec(memory_space=pltpu.SMEM)
VMEM = pl.BlockSpec(memory_space=pltpu.VMEM)
HBM = pl.BlockSpec(memory_space=pltpu.HBM)


def call(kernel, out_shape, in_specs, name, out_specs=None, scratch=(), aliases=None):
    if out_specs is None:
        out_specs = jax.tree.map(lambda _: VMEM, out_shape)
    return pl.pallas_call(
        kernel,
        out_shape=out_shape,
        in_specs=in_specs,
        out_specs=out_specs,
        scratch_shapes=list(scratch),
        input_output_aliases=aliases or {},
        compiler_params=pltpu.CompilerParams(vmem_limit_bytes=24 * 1024 * 1024),
        name=name,
    )


def iota(shape, dim):
    return lax.broadcasted_iota(jnp.int32, shape, dim)


def shape_of(shape, dtype):
    return jax.ShapeDtypeStruct(shape, dtype)


def frequencies():
    parts = []
    for size in (HD // 4, HD * 3 // 8, HD * 3 // 8):
        rate = 1.0 / np.float32(10000.0) ** (
            np.arange(0, size, 2).astype(np.float32) / np.float32(size)
        )
        parts.append(np.repeat(rate.astype(np.float32), 2))
    rate = np.concatenate(parts)
    return np.concatenate([rate, rate])[None, :].astype(np.float32)


def offset_in_patch(index, half):
    return (2 * ((index >> 2) & 1) + half) * 64 + 4 * (index >> 3) + (index & 3)


def prepare_kernel(scalars, row_ref, ada_ref, rate_ref, rec_ref, mod_out, tables_out):
    half = scalars[0]
    time_row = row_ref[pl.ds(scalars[5], 1), :]
    embedding = (time_row / (1.0 + jnp.exp(-time_row))).astype(BF)
    embedding = jnp.broadcast_to(embedding, (8, embedding.shape[1]))
    part = lax.dot_general(
        embedding, ada_ref[...], (((1,), (1,)), ((), ())), preferred_element_type=F32
    )[0:1]
    high = part.astype(BF)
    mod_out[0:1, :] = high
    mod_out[1:2, :] = (part - high.astype(F32)).astype(BF)

    rate = rate_ref[...]

    def tables(position, rows, at):
        text = position < TXT
        index = jnp.maximum(position - TXT, 0).astype(F32)
        frame = jnp.floor((index + 0.5) * (1.0 / (GH * GW)))
        line = jnp.floor((index + 0.5) * (1.0 / GW))
        width = index - line * GW
        height = line - jnp.floor((line + 0.5) * (1.0 / GH)) * GH
        lane = iota((rows, 128), 1) & (HD - 1)
        coordinate = jnp.where(lane < HD // 4, frame, jnp.where(lane < HD // 4 + HD * 3 // 8, height, width))
        phase = coordinate * rate
        tables_out[0, at : at + rows, :] = jnp.where(text, 1.0, jnp.cos(phase))
        tables_out[1, at : at + rows, :] = jnp.where(text, 0.0, jnp.sin(phase))
        tables_out[2, at : at + rows, :] = jnp.where(text, 1.0, 0.0)

    tables(offset_in_patch(iota((GROUP, 128), 0), half) + scalars[6], GROUP, 0)
    slot = rec_ref[...]
    start = jnp.where(
        slot < PLEN,
        scalars[1],
        jnp.where(slot < 2 * PLEN, scalars[2], jnp.where(slot < 3 * PLEN, scalars[3], scalars[4])),
    )
    tables(start + (slot & (PLEN - 1)), REC_GROUP, GROUP)


def normalize(x_ref, mod_ref, tables_ref, norm_ref, small):
    chunks = D // 128
    rows = x_ref.shape[0]

    def over_chunks(step, start):
        return lax.fori_loop(0, chunks, lambda k, carry: step(pl.ds(pl.multiple_of(k * 128, 128), 128), carry), start, unroll=6)

    def add(lanes, total):
        return total + x_ref[:, lanes].astype(F32)

    mean = jnp.sum(over_chunks(add, jnp.zeros((rows, 128), F32)), axis=1, keepdims=True) * (1.0 / D)

    def add_square(lanes, total):
        centered = x_ref[:, lanes].astype(F32) - mean
        return total + centered * centered

    total = jnp.sum(over_chunks(add_square, jnp.zeros((rows, 128), F32)), axis=1, keepdims=True)
    factor = lax.rsqrt(total * (1.0 / D) + 1e-5)
    for copy in small:
        copy.wait()
    text = tables_ref[2] > 0.5

    def write(lanes, carry):
        shift = jnp.where(text, mod_ref[3:4, lanes], mod_ref[0:1, lanes])
        scale = jnp.where(text, mod_ref[4:5, lanes], mod_ref[1:2, lanes])
        centered = x_ref[:, lanes].astype(F32) - mean
        norm_ref[:, lanes] = (centered * factor * (1.0 + scale) + shift).astype(BF)
        return carry

    over_chunks(write, 0)


def heads_from(mixed, gain_ref, tables_ref, q_out, kv_out):
    rows = mixed.shape[0]
    lane = iota((128, 128), 1)
    block = jnp.where((iota((128, 128), 0) >> 6) == (lane >> 6), 1.0 / HD, 0.0).astype(BF)

    def group_mean(values):
        high = values.astype(BF)
        low = (values - high.astype(F32)).astype(BF)
        return jnp.dot(high, block, preferred_element_type=F32) + jnp.dot(
            low, block, preferred_element_type=F32
        )

    low_half = iota((rows, 128), 1) < HD
    even = (iota((rows, 128), 1) & 1) == 0
    cosine, sine = tables_ref[0], tables_ref[1]
    gain = gain_ref[...]
    other_gain = pltpu.roll(jnp.broadcast_to(gain, (8, 128)), 64, 1)[0:1]
    gains = (gain, other_gain, other_gain, gain)
    plain, turned = [], []
    for k in range(4):
        values = mixed[:, 128 * k : 128 * k + 128]
        plain.append(values)
        centered = values - group_mean(values)
        scaled = centered * lax.rsqrt(group_mean(centered * centered) + 1e-6) * gains[k]
        partner = jnp.where(even, -pltpu.roll(scaled, 127, 1), pltpu.roll(scaled, 1, 1))
        turned.append(scaled * cosine + partner * sine)
    last = jnp.concatenate([mixed[:, 512:576], jnp.zeros((rows, 64), F32)], axis=1)
    keys_values = (
        pltpu.roll(jnp.where(low_half, plain[1], turned[0]), 64, 1).astype(BF),
        jnp.where(low_half, turned[2], plain[2]).astype(BF),
        pltpu.roll(jnp.where(low_half, last, turned[3]), 64, 1).astype(BF),
    )
    for copy in range(kv_out.shape[0]):
        for head in range(3):
            kv_out[copy, 0:rows, 128 * head : 128 * head + 128] = keys_values[head]
    if q_out is None:
        return
    zero = jnp.zeros((rows, 128), F32)
    q_out[:, 0:128] = (jnp.where(low_half, turned[0], zero) * 0.125).astype(BF)
    q_out[:, 128:256] = (jnp.where(low_half, pltpu.roll(turned[1], 64, 1), zero) * 0.125).astype(BF)
    q_out[:, 256:384] = (jnp.where(low_half, turned[3], zero) * 0.125).astype(BF)


def times_weights(norm, weights):
    return lax.dot_general(norm, weights, (((1,), (1,)), ((), ())), preferred_element_type=F32)


def small_copies(mod_hbm, rows_hbm, tables_hbm, layer, rows, mod_ref, gain_ref, tables_ref, sems):
    copies = [
        pltpu.make_async_copy(mod_hbm.at[layer], mod_ref, sems.at[0]),
        pltpu.make_async_copy(rows_hbm.at[4 * layer, pl.ds(16, 1), pl.ds(0, 128)], gain_ref, sems.at[1]),
        pltpu.make_async_copy(tables_hbm.at[:, rows, :], tables_ref, sems.at[2]),
    ]
    for copy in copies:
        copy.start()
    return copies


def small_scratch(rows):
    return [
        pltpu.VMEM((6, D), F32),
        pltpu.VMEM((1, 128), F32),
        pltpu.VMEM((3, rows, 128), F32),
        pltpu.SemaphoreType.DMA((3,)),
    ]


def rec_kernel(
    scalars, gathered_ref, mod_hbm, rows_hbm, tables_hbm, w_ref,
    kv_out, x_ref, norm_ref, w_vmem, sem, mod_ref, gain_ref, tables_ref, sems,
):
    fetch = pltpu.make_async_copy(w_ref, w_vmem, sem)
    fetch.start()
    rows = pl.ds(GROUP, REC_GROUP)
    small = small_copies(mod_hbm, rows_hbm, tables_hbm, scalars[7], rows, mod_ref, gain_ref, tables_ref, sems)
    share = gathered_ref[:, D : D + 768]
    for k in range(4):
        pick = iota((REC_GROUP, GROUP), 1) == 4 * iota((REC_GROUP, GROUP), 0) + k
        pick = jnp.where(pick, 1.0, 0.0).astype(BF)
        x_ref[:, 768 * k : 768 * k + 768] = jnp.dot(pick, share, preferred_element_type=F32).astype(BF)
    normalize(x_ref, mod_ref, tables_ref, norm_ref, small)
    fetch.wait()
    heads_from(times_weights(norm_ref[...], w_vmem[...]), gain_ref, tables_ref, None, kv_out)


def qkv_kernel_of(layer):
    def qkv_kernel(
        x_ref, rec_ref, mod_hbm, rows_hbm, tables_hbm, packed_ref,
        q_out, kv_out, weights_out, gates_out, norm_ref, w_vmem, sems, mod_ref, gain_ref, tables_ref, small_sems,
    ):
        rows = pl.ds(0, GROUP)
        small = small_copies(mod_hbm, rows_hbm, tables_hbm, layer, rows, mod_ref, gain_ref, tables_ref, small_sems)

        def fetch(k):
            to = w_vmem.at[pl.ds(288 * (k % 2), 288), pl.ds(384 * (k // 2), 384)]
            return pltpu.make_async_copy(packed_ref.at[k, pl.ds(0, 288), :], to, sems.at[k])

        def pass_on(k):
            to = weights_out.at[pl.ds(96 * (k % 2), 96), pl.ds(384 * (k // 2), 384)]
            return pltpu.make_async_copy(packed_ref.at[k, pl.ds(288, 96), :], to, sems.at[16 + k])

        for k in range(16):
            fetch(k).start()
        for k in range(16):
            pass_on(k).start()
        normalize(x_ref, mod_ref, tables_ref, norm_ref, small)
        mixed = jnp.zeros((GROUP, 576), F32)
        for piece in range(4):
            for k in range(4 * piece, 4 * piece + 4):
                fetch(k).wait()
            lanes = slice(768 * piece, 768 * piece + 768)
            mixed = mixed + times_weights(norm_ref[:, lanes], w_vmem[:, lanes])
        heads_from(mixed, gain_ref, tables_ref, q_out, kv_out)
        gates_out[0:1, :] = mod_ref[2:3, :]
        gates_out[1:2, :] = mod_ref[5:6, :]
        if layer == 0:
            for copy in range(kv_out.shape[0]):
                kv_out[copy, GROUP:, :] = rec_ref[0]
        for k in range(16):
            pass_on(k).wait()

    return qkv_kernel


def pack_kernel(row_ref, w_ref, out_ref, packed, sems):
    copies = []
    for k in range(4):
        lanes = pl.ds(pl.multiple_of(row_ref[0] * 768 + 384 * (k // 2), 128), 384)
        copies += [
            (w_ref.at[pl.ds(288 * (k % 2), 288), lanes], packed.at[k, pl.ds(0, 288), :]),
            (out_ref.at[pl.ds(96 * (k % 2), 96), lanes], packed.at[k, pl.ds(288, 96), :]),
        ]
    copies = [pltpu.make_async_copy(a, b, sems.at[n]) for n, (a, b) in enumerate(copies)]
    for copy in copies:
        copy.start()
    for copy in copies:
        copy.wait()


def attend(scalars, q_ref, cache_ref, keep_out, send_out):
    patch, core = scalars[7], scalars[9]
    key = iota((8, 1024), 1)
    key_patch = key >> 8
    within = key & (PLEN - 1)
    fresh_offset = (2 * ((within >> 2) & 1) + (within >> 7)) * 64 + 4 * ((within >> 3) & 15) + (within & 3)
    offset = jnp.where(key_patch <= patch, fresh_offset, within)
    count = jnp.where(
        key_patch == 0,
        scalars[11],
        jnp.where(key_patch == 1, scalars[12], jnp.where(key_patch == 2, scalars[13], scalars[14])),
    )
    live = (offset < count)[0:1]
    outs = []
    for head in range(3):
        lanes = slice(128 * head, 128 * head + 128)
        keys_values = cache_ref[:, lanes]
        scores = lax.dot_general(
            q_ref[:, lanes], keys_values, (((1,), (1,)), ((), ())), preferred_element_type=F32
        )
        weights = jnp.where(live, jnp.exp(scores), 0.0)
        total = jnp.sum(weights, axis=1, keepdims=True)
        mixed = jnp.dot(weights.astype(BF), keys_values, preferred_element_type=F32)
        outs.append(mixed / total)
    low = iota((GROUP, 128), 1) < HD
    first = jnp.where(low, pltpu.roll(outs[0], 64, 1), outs[1]).astype(BF)
    second = jnp.where(low, pltpu.roll(outs[2], 64, 1), 0.0).astype(BF)
    for z in range(8):
        to = slice(8 * z, 8 * z + 8)
        even, odd = slice(16 * z, 16 * z + 8), slice(16 * z + 8, 16 * z + 16)
        for value, lanes in ((first, slice(0, 128)), (second, slice(128, 256))):
            keep_out[to, lanes] = jnp.where(core == 0, value[even], value[odd])
            send_out[to, lanes] = jnp.where(core == 0, value[odd], value[even])


def attend_kernel_of(layer):
    def attend_kernel(scalars, q_ref, *refs):
        pieces, refs = refs[: 1 if layer == 0 else 8], refs[1 if layer == 0 else 8 :]
        targets_hbm, rec_ref, stale_ref, own_hbm, other_hbm, keep_out, send_out, weights_out = refs[:8]
        base_ref, cache_ref, rec_vmem, target_ref, sems = refs[8:]
        half = scalars[0]
        section = scalars[7]
        rec_copies = [
            pltpu.make_async_copy(
                rec_ref.at[2 * layer + h, pl.ds(GROUP, REC_GROUP), :],
                rec_vmem.at[pl.ds(REC_GROUP * h, REC_GROUP), :],
                sems.at[4 + h],
            )
            for h in range(2)
        ]
        rec_copies.append(pltpu.make_async_copy(targets_hbm, target_ref, sems.at[6]))
        for copy in rec_copies:
            copy.start()
        from_base = [
            pltpu.make_async_copy(
                stale_ref.at[2 * layer + h], base_ref.at[pl.ds(PLEN + STALE * h, STALE), :], sems.at[h]
            )
            for h in range(2)
        ]
        weights = [
            pltpu.make_async_copy(own_hbm, weights_out.at[0], sems.at[2]),
            pltpu.make_async_copy(other_hbm, weights_out.at[1], sems.at[3]),
        ]
        for copy in from_base + weights:
            copy.start()
        rec_vmem[64:, :] = jnp.zeros((64, 384), BF)
        for copy in rec_copies:
            copy.wait()
        match = iota((1024, 128), 0) == target_ref[0:1, :]
        chosen = jnp.where(match, 1.0, 0.0)
        hit = jnp.sum(chosen, axis=1, keepdims=True) > 0.5
        placed = jnp.dot(chosen.astype(BF), rec_vmem[...], preferred_element_type=F32)
        for copy in from_base:
            copy.wait()
        for patch in range(4):
            rows = slice(PLEN * patch, PLEN * patch + PLEN)
            if layer == 0:

                @pl.when(patch <= section)
                def _(patch=patch, rows=rows):
                    fresh_ref = pieces[0]
                    cache_ref[rows, :] = jnp.concatenate(
                        [fresh_ref[2 * patch, 0:GROUP, :], fresh_ref[2 * patch + 1, 0:GROUP, :]], axis=0
                    )

            if patch == 0:
                continue

            @pl.when(patch > section)
            def _(rows=rows):
                cache_ref[rows, :] = jnp.where(hit[rows], placed[rows], base_ref[rows, :].astype(F32)).astype(BF)

        if layer > 0:
            for back in range(4):

                @pl.when(section >= back)
                def _(back=back):
                    for piece, at in ((pieces[2 * back], half), (pieces[2 * back + 1], 1 - half)):
                        start = pl.multiple_of((section - back) * PLEN + at * GROUP, GROUP)
                        cache_ref[pl.ds(start, GROUP), :] = piece[...]

        attend(scalars, q_ref, cache_ref, keep_out, send_out)
        for copy in weights:
            copy.wait()

    return attend_kernel


def project_kernel(keep_ref, got_ref, weights_ref, out_ref):
    out = jnp.dot(keep_ref[:, 0:192], weights_ref[0], preferred_element_type=F32)
    out = out + jnp.dot(got_ref[:, 0:192], weights_ref[1], preferred_element_type=F32)
    out_ref[...] = out.astype(BF)


def residual_kernel(scalars, parts_ref, x_ref, gates_ref, out_ref):
    row = iota((8, 128), 0)
    offset = (2 * (row >> 2) + scalars[0]) * 64 + 4 * scalars[10] + (row & 3)
    text = (offset + scalars[6]) < TXT
    for k in range(D // 128):
        lanes = slice(128 * k, 128 * k + 128)
        total = parts_ref[0, :, lanes].astype(F32)
        for source in range(1, 8):
            total = total + parts_ref[source, :, lanes].astype(F32)
        gate = jnp.where(text, gates_ref[1:2, lanes], gates_ref[0:1, lanes])
        out_ref[:, lanes] = (x_ref[:, lanes].astype(F32) + gate * total).astype(BF)


def time_block(timestep, time_table):
    return lax.dynamic_slice(time_table, ((timestep[0] // 8) * 8, 0), (8, time_table.shape[1]))


def swapped(value, axis):
    return lax.ppermute(value, axis, [(0, 1), (1, 0)])


def local(
    hidden,
    patch_counts,
    timestep,
    time_table,
    ada_weight,
    qkv_weight,
    out_weight,
    qk_gain,
    stale_kv,
    stale_inputs,
    recompute_slots,
):
    section = lax.axis_index("section")
    req = lax.axis_index("req")
    half = lax.axis_index("half")
    core = lax.axis_index("core")
    col = lax.axis_index("z") * 2 + core
    first_req = req == 0
    sections = lax.axis_size("section")
    patches = hidden.shape[0]

    row_index = req * 2 + half
    weights_qkv = pltpu.with_memory_space_constraint(qkv_weight[0].T, pltpu.HBM)
    packed = call(
        pack_kernel,
        shape_of((4, 384, 384), BF),
        [SMEM, HBM, HBM],
        "pack",
        out_specs=HBM,
        scratch=[pltpu.SemaphoreType.DMA((8,))],
    )(
        row_index[None].astype(jnp.int32),
        weights_qkv,
        pltpu.with_memory_space_constraint(out_weight[0], pltpu.HBM),
    )
    chunks = lax.all_to_all(packed, "section", 0, 0)
    layers = [
        lax.all_gather(chunks[layer], ("req", "half", "section"), axis=0, tiled=False) for layer in range(sections)
    ]
    peers = ("section", "half")
    copies = lax.axis_size(peers)
    stale_share = lax.dynamic_slice(stale_kv, (0, PLEN + STALE * half, req, 0, 0), (1, STALE, 1, 3, 128))
    stale_share = stale_share.reshape(1, STALE, 384)
    stale_all = lax.all_to_all(jnp.broadcast_to(stale_share, (copies, STALE, 384)), peers, 0, 0)

    def of_request(value, axis):
        both = [lax.index_in_dim(value, r, axis, keepdims=False) for r in range(2)]
        return jnp.where(first_req, both[0], both[1]), jnp.where(first_req, both[1], both[0])

    def by_request(value, got):
        own = [lax.index_in_dim(value, r, 1, keepdims=False) for r in range(2)]
        far = [lax.index_in_dim(got, r, 1, keepdims=False) for r in range(2)]
        return jnp.where(
            first_req, jnp.concatenate([own[0], far[0]], axis=0), jnp.concatenate([far[1], own[1]], axis=0)
        )

    patch_rows = lax.dynamic_index_in_dim(hidden, section, 0, keepdims=False)
    tokens = by_request(patch_rows, swapped(patch_rows, "req"))
    rec_tokens = by_request(stale_inputs[0], swapped(stale_inputs[0], "req"))

    counts, _ = of_request(patch_counts, 0)
    starts = jnp.stack([jnp.int32(0), counts[0], counts[0] + counts[1], counts[0] + counts[1] + counts[2]])
    slots, _ = of_request(recompute_slots, 0)
    slots = slots.reshape(2, 2, 16)
    by_half = [slots[:, h].T.reshape(REC_GROUP) for h in range(2)]
    target_own = jnp.where(half == 0, by_half[0], by_half[1])
    targets = jnp.concatenate(by_half + [jnp.full((64,), -1, jnp.int32)])
    targets = jnp.broadcast_to(targets[None, :], (8, 128))

    own_start = lax.dynamic_index_in_dim(starts, section, 0, keepdims=True)
    scalars = jnp.concatenate(
        [half[None], starts, timestep % 8, own_start, jnp.stack([section, row_index, core, col]), counts, req[None]]
    ).astype(jnp.int32)
    mod_part, tables = call(
        prepare_kernel,
        (shape_of((2, 288), BF), shape_of((3, GROUP + REC_GROUP, 128), F32)),
        [SMEM, VMEM, VMEM, VMEM, VMEM],
        "prepare",
    )(
        scalars,
        time_block(timestep, time_table),
        ada_weight[0].T,
        jnp.asarray(frequencies()),
        jnp.broadcast_to(target_own[:, None], (REC_GROUP, 128)),
    )

    payload = jnp.concatenate(
        [
            tokens,
            rec_tokens.reshape(8, 768),
            jnp.pad(mod_part.reshape(8, 72), ((0, 0), (0, 56))),
        ],
        axis=1,
    )
    gathered = lax.all_gather(payload, COL, axis=0, tiled=True)
    pieces = gathered[:, D + 768 : D + 840].reshape(16, 2, 288).astype(F32)
    summed = pieces[:, 0] + pieces[:, 1]
    gain_row = jnp.pad(qk_gain[0].reshape(1, 128), ((0, 0), (0, 160)))
    rows = jnp.concatenate([summed, gain_row], axis=0)[None]
    everyone = ("section",) + ROW
    rows, stale_all = lax.optimization_barrier((rows, stale_all))
    rows = lax.all_to_all(jnp.broadcast_to(rows, (lax.axis_size(everyone), 17, 288)), everyone, 0, 0)
    modulation = rows[:, :16].reshape(sections, 6, D)
    in_hbm = [pltpu.with_memory_space_constraint(value, pltpu.HBM) for value in (modulation, rows, tables)]
    rec_fresh = call(
        rec_kernel,
        shape_of((1, REC_GROUP, 384), BF),
        [SMEM, VMEM] + [HBM] * 4,
        "rec",
        scratch=[
            pltpu.VMEM((REC_GROUP, D), BF),
            pltpu.VMEM((REC_GROUP, D), BF),
            pltpu.VMEM((576, D), BF),
            pltpu.SemaphoreType.DMA,
        ]
        + small_scratch(REC_GROUP),
    )(scalars, gathered, *in_hbm, weights_qkv)
    targets = pltpu.with_memory_space_constraint(targets, pltpu.HBM)

    def upwards(fresh):
        pieces = [fresh, swapped(fresh, "half")]
        for back in range(1, sections):
            pairs = [(i, i + back) for i in range(sections - back)]
            pieces.append(lax.ppermute(fresh, "section", pairs))
            crossed = [(2 * a + h, 2 * b + 1 - h) for a, b in pairs for h in range(2)]
            pieces.append(lax.ppermute(fresh, peers, crossed))
        return pieces

    half_rows = shape_of((64, 256), BF)
    current, group, outs, first_fresh = tokens, gathered, [], None
    for layer in range(sections):
        packed = pltpu.with_memory_space_constraint(layers[layer], pltpu.HBM)
        if layer > 0:
            group = lax.all_gather(current, COL, axis=0, tiled=True)
            group = pltpu.with_memory_space_constraint(group, pltpu.VMEM)
        queries, fresh, out_own, gates = call(
            qkv_kernel_of(layer),
            (
                shape_of((GROUP, 384), BF),
                shape_of((copies, GROUP + REC_GROUP, 384) if layer == 0 else (1, GROUP, 384), BF),
                shape_of((192, D), BF),
                shape_of((2, D), F32),
            ),
            [VMEM] * 2 + [HBM] * 4,
            "qkv",
            scratch=[pltpu.VMEM((GROUP, D), BF), pltpu.VMEM((576, D), BF), pltpu.SemaphoreType.DMA((32,))]
            + small_scratch(GROUP),
        )(group, rec_fresh, *in_hbm, packed)
        out_other = swapped(out_own, "core")
        if layer == 0:
            first_fresh = lax.all_to_all(fresh, peers, 0, 0)
            pieces = [first_fresh]
        else:
            pieces = upwards(fresh[0])
        keep, send, weights_out = call(
            attend_kernel_of(layer),
            (half_rows, half_rows, shape_of((2, 192, D), BF)),
            [SMEM] + [VMEM] * (1 + len(pieces)) + [HBM] * 5,
            "attend",
            scratch=[
                pltpu.VMEM((1024, 384), BF),
                pltpu.VMEM((1024, 384), BF),
                pltpu.VMEM((128, 384), BF),
                pltpu.VMEM((8, 128), jnp.int32),
                pltpu.SemaphoreType.DMA((7,)),
            ],
        )(scalars, queries, *pieces, targets, first_fresh, stale_all, out_own, out_other)
        projected = call(project_kernel, shape_of((64, D), BF), [VMEM] * 3, "project")(
            keep, swapped(send, "core"), weights_out
        )
        parts = lax.all_to_all(projected.reshape(8, 8, D), "z", 0, 0)
        current = call(residual_kernel, shape_of((8, D), BF), [SMEM, VMEM, VMEM, VMEM], "residual")(
            scalars, parts, current, gates
        )
        outs.append(current)

    leaving = jnp.stack(outs).reshape(sections * 2, 4, D)
    out = lax.all_to_all(leaving, ("section", "req"), 0, 0).reshape(patches, 2, 4, D)
    return jnp.transpose(out, (0, 2, 1, 3))[None]


def solution(mesh):
    sizes = tuple(mesh.devices.shape)
    fine = Mesh(
        mesh.devices.reshape(sizes[0], 2, sizes[1] // 2, sizes[2] // 2, 2),
        ("section", "req", "half", "z", "core"),
    )
    return jax.shard_map(
        local,
        mesh=fine,
        in_specs=(
            P(None, ROW_AXES, None, None),
            P(),
            P(),
            P(),
            P("section", None, ROW_AXES),
            P("section", None, COL),
            P("section", COL, None),
            P("section", None, None),
            P("section", None, None, COL, None),
            P("section", ROW_AXES, None, None),
            P(),
        ),
        out_specs=P("section", None, ROW_AXES, None, None),
        check_vma=False,
    )
```

```python
import jax
import jax.numpy as jnp
import numpy as np
from jax import lax
from jax.experimental import pallas as pl
from jax.experimental.pallas import tpu as pltpu
from jax.sharding import Mesh
from jax.sharding import PartitionSpec as P

HD = 64
D = 3072
TXT = 226
GH = 30
GW = 45
PLEN = 256
GROUP = 128
REC_GROUP = 32
STALE = 384
BF = jnp.bfloat16
F32 = jnp.float32
COL = ("z", "core")
ROW = ("req", "half")
ROW_AXES = ("req", "half", "z", "core")


SMEM = pl.BlockSpec(memory_space=pltpu.SMEM)
VMEM = pl.BlockSpec(memory_space=pltpu.VMEM)
HBM = pl.BlockSpec(memory_space=pltpu.HBM)


def call(kernel, out_shape, in_specs, name, out_specs=None, scratch=(), aliases=None):
    if out_specs is None:
        out_specs = jax.tree.map(lambda _: VMEM, out_shape)
    return pl.pallas_call(
        kernel,
        out_shape=out_shape,
        in_specs=in_specs,
        out_specs=out_specs,
        scratch_shapes=list(scratch),
        input_output_aliases=aliases or {},
        compiler_params=pltpu.CompilerParams(vmem_limit_bytes=24 * 1024 * 1024),
        name=name,
    )


def iota(shape, dim):
    return lax.broadcasted_iota(jnp.int32, shape, dim)


def shape_of(shape, dtype):
    return jax.ShapeDtypeStruct(shape, dtype)


def frequencies():
    parts = []
    for size in (HD // 4, HD * 3 // 8, HD * 3 // 8):
        rate = 1.0 / np.float32(10000.0) ** (
            np.arange(0, size, 2).astype(np.float32) / np.float32(size)
        )
        parts.append(np.repeat(rate.astype(np.float32), 2))
    rate = np.concatenate(parts)
    return np.concatenate([rate, rate])[None, :].astype(np.float32)


def offset_in_patch(index, half):
    return (2 * ((index >> 2) & 1) + half) * 64 + 4 * (index >> 3) + (index & 3)


def prepare_kernel(scalars, row_ref, ada_ref, rate_ref, rec_ref, mod_out, tables_out):
    half = scalars[0]
    time_row = row_ref[pl.ds(scalars[5], 1), :]
    embedding = (time_row / (1.0 + jnp.exp(-time_row))).astype(BF)
    embedding = jnp.broadcast_to(embedding, (8, embedding.shape[1]))
    part = lax.dot_general(
        embedding, ada_ref[...], (((1,), (1,)), ((), ())), preferred_element_type=F32
    )[0:1]
    high = part.astype(BF)
    mod_out[0:1, :] = high
    mod_out[1:2, :] = (part - high.astype(F32)).astype(BF)

    rate = rate_ref[...]

    def tables(position, rows, at):
        text = position < TXT
        index = jnp.maximum(position - TXT, 0).astype(F32)
        frame = jnp.floor((index + 0.5) * (1.0 / (GH * GW)))
        line = jnp.floor((index + 0.5) * (1.0 / GW))
        width = index - line * GW
        height = line - jnp.floor((line + 0.5) * (1.0 / GH)) * GH
        lane = iota((rows, 128), 1) & (HD - 1)
        coordinate = jnp.where(lane < HD // 4, frame, jnp.where(lane < HD // 4 + HD * 3 // 8, height, width))
        phase = coordinate * rate
        tables_out[0, at : at + rows, :] = jnp.where(text, 1.0, jnp.cos(phase))
        tables_out[1, at : at + rows, :] = jnp.where(text, 0.0, jnp.sin(phase))
        tables_out[2, at : at + rows, :] = jnp.where(text, 1.0, 0.0)

    tables(offset_in_patch(iota((GROUP, 128), 0), half) + scalars[6], GROUP, 0)
    slot = rec_ref[...]
    start = jnp.where(
        slot < PLEN,
        scalars[1],
        jnp.where(slot < 2 * PLEN, scalars[2], jnp.where(slot < 3 * PLEN, scalars[3], scalars[4])),
    )
    tables(start + (slot & (PLEN - 1)), REC_GROUP, GROUP)


def normalize(x_ref, mod_ref, tables_ref, norm_ref, small):
    chunks = D // 128
    rows = x_ref.shape[0]

    def over_chunks(step, start):
        return lax.fori_loop(0, chunks, lambda k, carry: step(pl.ds(pl.multiple_of(k * 128, 128), 128), carry), start, unroll=6)

    def add(lanes, total):
        return total + x_ref[:, lanes].astype(F32)

    mean = jnp.sum(over_chunks(add, jnp.zeros((rows, 128), F32)), axis=1, keepdims=True) * (1.0 / D)

    def add_square(lanes, total):
        centered = x_ref[:, lanes].astype(F32) - mean
        return total + centered * centered

    total = jnp.sum(over_chunks(add_square, jnp.zeros((rows, 128), F32)), axis=1, keepdims=True)
    factor = lax.rsqrt(total * (1.0 / D) + 1e-5)
    for copy in small:
        copy.wait()
    text = tables_ref[2] > 0.5

    def write(lanes, carry):
        shift = jnp.where(text, mod_ref[3:4, lanes], mod_ref[0:1, lanes])
        scale = jnp.where(text, mod_ref[4:5, lanes], mod_ref[1:2, lanes])
        centered = x_ref[:, lanes].astype(F32) - mean
        norm_ref[:, lanes] = (centered * factor * (1.0 + scale) + shift).astype(BF)
        return carry

    over_chunks(write, 0)


def heads_from(mixed, gain_ref, tables_ref, q_out, kv_out):
    rows = mixed.shape[0]
    lane = iota((128, 128), 1)
    block = jnp.where((iota((128, 128), 0) >> 6) == (lane >> 6), 1.0 / HD, 0.0).astype(BF)

    def group_mean(values):
        high = values.astype(BF)
        low = (values - high.astype(F32)).astype(BF)
        return jnp.dot(high, block, preferred_element_type=F32) + jnp.dot(
            low, block, preferred_element_type=F32
        )

    low_half = iota((rows, 128), 1) < HD
    even = (iota((rows, 128), 1) & 1) == 0
    cosine, sine = tables_ref[0], tables_ref[1]
    gain = gain_ref[...]
    other_gain = pltpu.roll(jnp.broadcast_to(gain, (8, 128)), 64, 1)[0:1]
    gains = (gain, other_gain, other_gain, gain)
    plain, turned = [], []
    for k in range(4):
        values = mixed[:, 128 * k : 128 * k + 128]
        plain.append(values)
        centered = values - group_mean(values)
        scaled = centered * lax.rsqrt(group_mean(centered * centered) + 1e-6) * gains[k]
        partner = jnp.where(even, -pltpu.roll(scaled, 127, 1), pltpu.roll(scaled, 1, 1))
        turned.append(scaled * cosine + partner * sine)
    last = jnp.concatenate([mixed[:, 512:576], jnp.zeros((rows, 64), F32)], axis=1)
    keys_values = (
        pltpu.roll(jnp.where(low_half, plain[1], turned[0]), 64, 1).astype(BF),
        jnp.where(low_half, turned[2], plain[2]).astype(BF),
        pltpu.roll(jnp.where(low_half, last, turned[3]), 64, 1).astype(BF),
    )
    for copy in range(kv_out.shape[0]):
        for head in range(3):
            kv_out[copy, 0:rows, 128 * head : 128 * head + 128] = keys_values[head]
    if q_out is None:
        return
    zero = jnp.zeros((rows, 128), F32)
    q_out[:, 0:128] = (jnp.where(low_half, turned[0], zero) * 0.125).astype(BF)
    q_out[:, 128:256] = (jnp.where(low_half, pltpu.roll(turned[1], 64, 1), zero) * 0.125).astype(BF)
    q_out[:, 256:384] = (jnp.where(low_half, turned[3], zero) * 0.125).astype(BF)


def times_weights(norm, weights):
    return lax.dot_general(norm, weights, (((1,), (1,)), ((), ())), preferred_element_type=F32)


def small_copies(mod_hbm, rows_hbm, tables_hbm, layer, rows, mod_ref, gain_ref, tables_ref, sems):
    copies = [
        pltpu.make_async_copy(mod_hbm.at[layer], mod_ref, sems.at[0]),
        pltpu.make_async_copy(rows_hbm.at[4 * layer, pl.ds(16, 1), pl.ds(0, 128)], gain_ref, sems.at[1]),
        pltpu.make_async_copy(tables_hbm.at[:, rows, :], tables_ref, sems.at[2]),
    ]
    for copy in copies:
        copy.start()
    return copies


def small_scratch(rows):
    return [
        pltpu.VMEM((6, D), F32),
        pltpu.VMEM((1, 128), F32),
        pltpu.VMEM((3, rows, 128), F32),
        pltpu.SemaphoreType.DMA((3,)),
    ]


def rec_kernel(
    scalars, gathered_ref, mod_hbm, rows_hbm, tables_hbm, w_ref,
    kv_out, x_ref, norm_ref, w_vmem, sem, mod_ref, gain_ref, tables_ref, sems,
):
    fetch = pltpu.make_async_copy(w_ref, w_vmem, sem)
    fetch.start()
    rows = pl.ds(GROUP, REC_GROUP)
    small = small_copies(mod_hbm, rows_hbm, tables_hbm, scalars[7], rows, mod_ref, gain_ref, tables_ref, sems)
    share = gathered_ref[:, D : D + 768]
    for k in range(4):
        pick = iota((REC_GROUP, GROUP), 1) == 4 * iota((REC_GROUP, GROUP), 0) + k
        pick = jnp.where(pick, 1.0, 0.0).astype(BF)
        x_ref[:, 768 * k : 768 * k + 768] = jnp.dot(pick, share, preferred_element_type=F32).astype(BF)
    normalize(x_ref, mod_ref, tables_ref, norm_ref, small)
    fetch.wait()
    heads_from(times_weights(norm_ref[...], w_vmem[...]), gain_ref, tables_ref, None, kv_out)


def qkv_kernel_of(layer):
    def qkv_kernel(
        x_ref, rec_ref, mod_hbm, rows_hbm, tables_hbm, packed_ref,
        q_out, kv_out, weights_out, gates_out, norm_ref, w_vmem, sems, mod_ref, gain_ref, tables_ref, small_sems,
    ):
        rows = pl.ds(0, GROUP)
        small = small_copies(mod_hbm, rows_hbm, tables_hbm, layer, rows, mod_ref, gain_ref, tables_ref, small_sems)

        def fetch(k):
            to = w_vmem.at[pl.ds(288 * (k % 2), 288), pl.ds(384 * (k // 2), 384)]
            return pltpu.make_async_copy(packed_ref.at[k, pl.ds(0, 288), :], to, sems.at[k])

        def pass_on(k):
            to = weights_out.at[pl.ds(96 * (k % 2), 96), pl.ds(384 * (k // 2), 384)]
            return pltpu.make_async_copy(packed_ref.at[k, pl.ds(288, 96), :], to, sems.at[16 + k])

        for k in range(16):
            fetch(k).start()
        normalize(x_ref, mod_ref, tables_ref, norm_ref, small)
        for k in range(16):
            pass_on(k).start()
        mixed = jnp.zeros((GROUP, 576), F32)
        for piece in range(4):
            for k in range(4 * piece, 4 * piece + 4):
                fetch(k).wait()
            lanes = slice(768 * piece, 768 * piece + 768)
            mixed = mixed + times_weights(norm_ref[:, lanes], w_vmem[:, lanes])
        heads_from(mixed, gain_ref, tables_ref, q_out, kv_out)
        gates_out[0:1, :] = mod_ref[2:3, :]
        gates_out[1:2, :] = mod_ref[5:6, :]
        if layer == 0:
            for copy in range(kv_out.shape[0]):
                kv_out[copy, GROUP:, :] = rec_ref[0]
        for k in range(16):
            pass_on(k).wait()

    return qkv_kernel


def pack_kernel(row_ref, w_ref, out_ref, packed, sems):
    copies = []
    for k in range(4):
        lanes = pl.ds(pl.multiple_of(row_ref[0] * 768 + 384 * (k // 2), 128), 384)
        copies += [
            (w_ref.at[pl.ds(288 * (k % 2), 288), lanes], packed.at[k, pl.ds(0, 288), :]),
            (out_ref.at[pl.ds(96 * (k % 2), 96), lanes], packed.at[k, pl.ds(288, 96), :]),
        ]
    copies = [pltpu.make_async_copy(a, b, sems.at[n]) for n, (a, b) in enumerate(copies)]
    for copy in copies:
        copy.start()
    for copy in copies:
        copy.wait()


def attend(scalars, q_ref, cache_ref, keep_out, send_out):
    patch, core = scalars[7], scalars[9]
    key = iota((8, 1024), 1)
    key_patch = key >> 8
    within = key & (PLEN - 1)
    fresh_offset = (2 * ((within >> 2) & 1) + (within >> 7)) * 64 + 4 * ((within >> 3) & 15) + (within & 3)
    offset = jnp.where(key_patch <= patch, fresh_offset, within)
    count = jnp.where(
        key_patch == 0,
        scalars[11],
        jnp.where(key_patch == 1, scalars[12], jnp.where(key_patch == 2, scalars[13], scalars[14])),
    )
    live = (offset < count)[0:1]
    outs = []
    for head in range(3):
        lanes = slice(128 * head, 128 * head + 128)
        keys_values = cache_ref[:, lanes]
        scores = lax.dot_general(
            q_ref[:, lanes], keys_values, (((1,), (1,)), ((), ())), preferred_element_type=F32
        )
        weights = jnp.where(live, jnp.exp(scores), 0.0)
        total = jnp.sum(weights, axis=1, keepdims=True)
        mixed = jnp.dot(weights.astype(BF), keys_values, preferred_element_type=F32)
        outs.append(mixed / total)
    low = iota((GROUP, 128), 1) < HD
    first = jnp.where(low, pltpu.roll(outs[0], 64, 1), outs[1]).astype(BF)
    second = jnp.where(low, pltpu.roll(outs[2], 64, 1), 0.0).astype(BF)
    for z in range(8):
        to = slice(8 * z, 8 * z + 8)
        even, odd = slice(16 * z, 16 * z + 8), slice(16 * z + 8, 16 * z + 16)
        for value, lanes in ((first, slice(0, 128)), (second, slice(128, 256))):
            keep_out[to, lanes] = jnp.where(core == 0, value[even], value[odd])
            send_out[to, lanes] = jnp.where(core == 0, value[odd], value[even])


def merge_copies(layer, targets_hbm, rec_ref, stale_ref, base_ref, rec_vmem, target_ref, sems):
    copies = [
        pltpu.make_async_copy(
            rec_ref.at[2 * layer + h, pl.ds(GROUP, REC_GROUP), :],
            rec_vmem.at[pl.ds(REC_GROUP * h, REC_GROUP), :],
            sems.at[h],
        )
        for h in range(2)
    ]
    copies += [
        pltpu.make_async_copy(
            stale_ref.at[2 * layer + h], base_ref.at[pl.ds(PLEN + STALE * h, STALE), :], sems.at[2 + h]
        )
        for h in range(2)
    ]
    copies.append(pltpu.make_async_copy(targets_hbm, target_ref, sems.at[4]))
    for copy in copies:
        copy.start()
    return copies


def merge(copies, base_ref, rec_vmem, target_ref, table_ref):
    rec_vmem[2 * REC_GROUP :, :] = jnp.zeros((128 - 2 * REC_GROUP, 384), BF)
    for copy in copies:
        copy.wait()
    match = iota((3 * PLEN, 128), 0) + PLEN == target_ref[0:1, :]
    chosen = jnp.where(match, 1.0, 0.0)
    hit = jnp.sum(chosen, axis=1, keepdims=True) > 0.5
    placed = jnp.dot(chosen.astype(BF), rec_vmem[...], preferred_element_type=F32)
    table_ref[PLEN:, :] = jnp.where(hit, placed, base_ref[PLEN:, :].astype(F32)).astype(BF)


def merge_scratch():
    return [
        pltpu.VMEM((1024, 384), BF),
        pltpu.VMEM((128, 384), BF),
        pltpu.VMEM((8, 128), jnp.int32),
        pltpu.SemaphoreType.DMA((5,)),
    ]


def table_kernel_of(layer):
    def table_kernel(fresh_ref, targets_hbm, rec_ref, stale_ref, table_out, base_ref, rec_vmem, target_ref, sems):
        del fresh_ref
        copies = merge_copies(layer, targets_hbm, rec_ref, stale_ref, base_ref, rec_vmem, target_ref, sems)
        table_out[0:PLEN, :] = jnp.zeros((PLEN, 384), BF)
        merge(copies, base_ref, rec_vmem, target_ref, table_out)

    return table_kernel


def weight_copies(own_hbm, other_hbm, weights_out, sems):
    copies = [
        pltpu.make_async_copy(own_hbm, weights_out.at[0], sems.at[0]),
        pltpu.make_async_copy(other_hbm, weights_out.at[1], sems.at[1]),
    ]
    for copy in copies:
        copy.start()
    return copies


def attend_first_kernel(
    scalars, q_ref, fresh_ref, targets_hbm, rec_ref, stale_ref, own_hbm, other_hbm,
    keep_out, send_out, weights_out, cache_ref, weight_sems, base_ref, rec_vmem, target_ref, sems,
):
    copies = merge_copies(0, targets_hbm, rec_ref, stale_ref, base_ref, rec_vmem, target_ref, sems)
    weights = weight_copies(own_hbm, other_hbm, weights_out, weight_sems)
    merge(copies, base_ref, rec_vmem, target_ref, cache_ref)
    for patch in range(4):

        @pl.when(patch <= scalars[7])
        def _(patch=patch):
            cache_ref[PLEN * patch : PLEN * patch + PLEN, :] = jnp.concatenate(
                [fresh_ref[2 * patch, 0:GROUP, :], fresh_ref[2 * patch + 1, 0:GROUP, :]], axis=0
            )

    attend(scalars, q_ref, cache_ref, keep_out, send_out)
    for copy in weights:
        copy.wait()


def attend_kernel(
    scalars, q_ref, own_ref, back1_ref, back2_ref, back3_ref, table_ref, own_hbm, other_hbm,
    keep_out, send_out, weights_out, cache_ref, weight_sems,
):
    section, half = scalars[7], scalars[0]
    weights = weight_copies(own_hbm, other_hbm, weights_out, weight_sems)
    for patch in range(1, 4):

        @pl.when(patch > section)
        def _(patch=patch):
            rows = slice(PLEN * patch, PLEN * patch + PLEN)
            cache_ref[rows, :] = table_ref[rows, :]

    for back, piece in enumerate((own_ref, back1_ref, back2_ref, back3_ref)):

        @pl.when(section >= back)
        def _(back=back, piece=piece):
            for at, rows in ((half, slice(0, GROUP)), (1 - half, slice(GROUP, 2 * GROUP))):
                start = pl.multiple_of((section - back) * PLEN + at * GROUP, GROUP)
                cache_ref[pl.ds(start, GROUP), :] = piece[rows, :]

    attend(scalars, q_ref, cache_ref, keep_out, send_out)
    for copy in weights:
        copy.wait()


def project_kernel(keep_ref, got_ref, weights_ref, out_ref):
    out = jnp.dot(keep_ref[:, 0:192], weights_ref[0], preferred_element_type=F32)
    out = out + jnp.dot(got_ref[:, 0:192], weights_ref[1], preferred_element_type=F32)
    out_ref[...] = out.astype(BF)


def residual_kernel(scalars, parts_ref, x_ref, gates_ref, out_ref):
    row = iota((8, 128), 0)
    offset = (2 * (row >> 2) + scalars[0]) * 64 + 4 * scalars[10] + (row & 3)
    text = (offset + scalars[6]) < TXT
    for k in range(D // 128):
        lanes = slice(128 * k, 128 * k + 128)
        total = parts_ref[0, :, lanes].astype(F32)
        for source in range(1, 8):
            total = total + parts_ref[source, :, lanes].astype(F32)
        gate = jnp.where(text, gates_ref[1:2, lanes], gates_ref[0:1, lanes])
        out_ref[:, lanes] = (x_ref[:, lanes].astype(F32) + gate * total).astype(BF)


def time_block(timestep, time_table):
    return lax.dynamic_slice(time_table, ((timestep[0] // 8) * 8, 0), (8, time_table.shape[1]))


def swapped(value, axis):
    return lax.ppermute(value, axis, [(0, 1), (1, 0)])


def local(
    hidden,
    patch_counts,
    timestep,
    time_table,
    ada_weight,
    qkv_weight,
    out_weight,
    qk_gain,
    stale_kv,
    stale_inputs,
    recompute_slots,
):
    section = lax.axis_index("section")
    req = lax.axis_index("req")
    half = lax.axis_index("half")
    core = lax.axis_index("core")
    col = lax.axis_index("z") * 2 + core
    first_req = req == 0
    sections = lax.axis_size("section")
    patches = hidden.shape[0]

    row_index = req * 2 + half
    weights_qkv = pltpu.with_memory_space_constraint(qkv_weight[0].T, pltpu.HBM)
    packed = call(
        pack_kernel,
        shape_of((4, 384, 384), BF),
        [SMEM, HBM, HBM],
        "pack",
        out_specs=HBM,
        scratch=[pltpu.SemaphoreType.DMA((8,))],
    )(
        row_index[None].astype(jnp.int32),
        weights_qkv,
        pltpu.with_memory_space_constraint(out_weight[0], pltpu.HBM),
    )
    chunks = lax.all_to_all(packed, "section", 0, 0)
    layers = [
        lax.all_gather(chunks[layer], ("req", "half", "section"), axis=0, tiled=False) for layer in range(sections)
    ]
    peers = ("section", "half")
    copies = lax.axis_size(peers)
    stale_share = lax.dynamic_slice(stale_kv, (0, PLEN + STALE * half, req, 0, 0), (1, STALE, 1, 3, 128))
    stale_share = stale_share.reshape(1, STALE, 384)
    stale_all = lax.all_to_all(jnp.broadcast_to(stale_share, (copies, STALE, 384)), peers, 0, 0)

    def of_request(value, axis):
        both = [lax.index_in_dim(value, r, axis, keepdims=False) for r in range(2)]
        return jnp.where(first_req, both[0], both[1]), jnp.where(first_req, both[1], both[0])

    def by_request(value, got):
        own = [lax.index_in_dim(value, r, 1, keepdims=False) for r in range(2)]
        far = [lax.index_in_dim(got, r, 1, keepdims=False) for r in range(2)]
        return jnp.where(
            first_req, jnp.concatenate([own[0], far[0]], axis=0), jnp.concatenate([far[1], own[1]], axis=0)
        )

    patch_rows = lax.dynamic_index_in_dim(hidden, section, 0, keepdims=False)
    tokens = by_request(patch_rows, swapped(patch_rows, "req"))
    rec_tokens = by_request(stale_inputs[0], swapped(stale_inputs[0], "req"))

    counts, _ = of_request(patch_counts, 0)
    starts = jnp.stack([jnp.int32(0), counts[0], counts[0] + counts[1], counts[0] + counts[1] + counts[2]])
    slots, _ = of_request(recompute_slots, 0)
    slots = slots.reshape(2, 2, 16)
    by_half = [slots[:, h].T.reshape(REC_GROUP) for h in range(2)]
    target_own = jnp.where(half == 0, by_half[0], by_half[1])
    targets = jnp.concatenate(by_half + [jnp.full((64,), -1, jnp.int32)])
    targets = jnp.broadcast_to(targets[None, :], (8, 128))

    own_start = lax.dynamic_index_in_dim(starts, section, 0, keepdims=True)
    scalars = jnp.concatenate(
        [half[None], starts, timestep % 8, own_start, jnp.stack([section, row_index, core, col]), counts, req[None]]
    ).astype(jnp.int32)
    mod_part, tables = call(
        prepare_kernel,
        (shape_of((2, 288), BF), shape_of((3, GROUP + REC_GROUP, 128), F32)),
        [SMEM, VMEM, VMEM, VMEM, VMEM],
        "prepare",
    )(
        scalars,
        time_block(timestep, time_table),
        ada_weight[0].T,
        jnp.asarray(frequencies()),
        jnp.broadcast_to(target_own[:, None], (REC_GROUP, 128)),
    )

    payload = jnp.concatenate(
        [
            tokens,
            rec_tokens.reshape(8, 768),
            jnp.pad(mod_part.reshape(8, 72), ((0, 0), (0, 56))),
        ],
        axis=1,
    )
    gathered = lax.all_gather(payload, COL, axis=0, tiled=True)
    pieces = gathered[:, D + 768 : D + 840].reshape(16, 2, 288).astype(F32)
    summed = pieces[:, 0] + pieces[:, 1]
    gain_row = jnp.pad(qk_gain[0].reshape(1, 128), ((0, 0), (0, 160)))
    rows = jnp.concatenate([summed, gain_row], axis=0)[None]
    everyone = ("section",) + ROW
    rows, stale_all = lax.optimization_barrier((rows, stale_all))
    rows = lax.all_to_all(jnp.broadcast_to(rows, (lax.axis_size(everyone), 17, 288)), everyone, 0, 0)
    modulation = rows[:, :16].reshape(sections, 6, D)
    in_hbm = [pltpu.with_memory_space_constraint(value, pltpu.HBM) for value in (modulation, rows, tables)]
    rec_fresh = call(
        rec_kernel,
        shape_of((1, REC_GROUP, 384), BF),
        [SMEM, VMEM] + [HBM] * 4,
        "rec",
        scratch=[
            pltpu.VMEM((REC_GROUP, D), BF),
            pltpu.VMEM((REC_GROUP, D), BF),
            pltpu.VMEM((576, D), BF),
            pltpu.SemaphoreType.DMA,
        ]
        + small_scratch(REC_GROUP),
    )(scalars, gathered, *in_hbm, weights_qkv)
    targets = pltpu.with_memory_space_constraint(targets, pltpu.HBM)

    def upwards(fresh):
        both = jnp.concatenate([fresh, swapped(fresh, "half")], axis=0)
        pairs = [[(i, i + back) for i in range(sections - back)] for back in range(1, sections)]
        return [both] + [lax.ppermute(both, "section", steps) for steps in pairs]

    half_rows = shape_of((64, 256), BF)
    current, group, outs, first_fresh = tokens, gathered, [], None
    for layer in range(sections):
        packed = pltpu.with_memory_space_constraint(layers[layer], pltpu.HBM)
        if layer > 0:
            group = lax.all_gather(current, COL, axis=0, tiled=True)
            group = pltpu.with_memory_space_constraint(group, pltpu.VMEM)
        queries, fresh, out_own, gates = call(
            qkv_kernel_of(layer),
            (
                shape_of((GROUP, 384), BF),
                shape_of((copies, GROUP + REC_GROUP, 384) if layer == 0 else (1, GROUP, 384), BF),
                shape_of((192, D), BF),
                shape_of((2, D), F32),
            ),
            [VMEM] * 2 + [HBM] * 4,
            "qkv",
            scratch=[pltpu.VMEM((GROUP, D), BF), pltpu.VMEM((576, D), BF), pltpu.SemaphoreType.DMA((32,))]
            + small_scratch(GROUP),
        )(group, rec_fresh, *in_hbm, packed)
        out_other = swapped(out_own, "core")
        attend_out = (half_rows, half_rows, shape_of((2, 192, D), BF))
        attend_scratch = [pltpu.VMEM((1024, 384), BF), pltpu.SemaphoreType.DMA((2,))]
        if layer == 0:
            first_fresh = lax.all_to_all(fresh, peers, 0, 0)
            keep, send, weights_out = call(
                attend_first_kernel,
                attend_out,
                [SMEM, VMEM, VMEM] + [HBM] * 5,
                "attend_first",
                scratch=attend_scratch + merge_scratch(),
            )(scalars, queries, first_fresh, targets, first_fresh, stale_all, out_own, out_other)
        else:
            pieces = upwards(fresh[0])
            merged = call(
                table_kernel_of(layer),
                shape_of((1024, 384), BF),
                [HBM] * 4,
                "table",
                scratch=merge_scratch(),
            )(fresh, targets, first_fresh, stale_all)
            keep, send, weights_out = call(
                attend_kernel,
                attend_out,
                [SMEM] + [VMEM] * 6 + [HBM] * 2,
                "attend",
                scratch=attend_scratch,
            )(scalars, queries, *pieces, merged, out_own, out_other)
        projected = call(project_kernel, shape_of((64, D), BF), [VMEM] * 3, "project")(
            keep, swapped(send, "core"), weights_out
        )
        parts = lax.all_to_all(projected.reshape(8, 8, D), "z", 0, 0)
        current = call(residual_kernel, shape_of((8, D), BF), [SMEM, VMEM, VMEM, VMEM], "residual")(
            scalars, parts, current, gates
        )
        outs.append(current)

    leaving = jnp.stack(outs).reshape(sections * 2, 4, D)
    out = lax.all_to_all(leaving, ("section", "req"), 0, 0).reshape(patches, 2, 4, D)
    return jnp.transpose(out, (0, 2, 1, 3))[None]


def solution(mesh):
    sizes = tuple(mesh.devices.shape)
    fine = Mesh(
        mesh.devices.reshape(sizes[0], 2, sizes[1] // 2, sizes[2] // 2, 2),
        ("section", "req", "half", "z", "core"),
    )
    return jax.shard_map(
        local,
        mesh=fine,
        in_specs=(
            P(None, ROW_AXES, None, None),
            P(),
            P(),
            P(),
            P("section", None, ROW_AXES),
            P("section", None, COL),
            P("section", COL, None),
            P("section", None, None),
            P("section", None, None, COL, None),
            P("section", ROW_AXES, None, None),
            P(),
        ),
        out_specs=P("section", None, ROW_AXES, None, None),
        check_vma=False,
    )
```

```python
import jax
import jax.numpy as jnp
import numpy as np
from jax import lax
from jax.experimental import pallas as pl
from jax.experimental.pallas import tpu as pltpu
from jax.sharding import Mesh
from jax.sharding import PartitionSpec as P

HD = 64
D = 3072
TXT = 226
GH = 30
GW = 45
PLEN = 256
GROUP = 128
REC_GROUP = 32
STALE = 384
BF = jnp.bfloat16
F32 = jnp.float32
COL = ("z", "core")
ROW = ("req", "half")
ROW_AXES = ("req", "half", "z", "core")


SMEM = pl.BlockSpec(memory_space=pltpu.SMEM)
VMEM = pl.BlockSpec(memory_space=pltpu.VMEM)
HBM = pl.BlockSpec(memory_space=pltpu.HBM)


def call(kernel, out_shape, in_specs, name, out_specs=None, scratch=(), aliases=None):
    if out_specs is None:
        out_specs = jax.tree.map(lambda _: VMEM, out_shape)
    return pl.pallas_call(
        kernel,
        out_shape=out_shape,
        in_specs=in_specs,
        out_specs=out_specs,
        scratch_shapes=list(scratch),
        input_output_aliases=aliases or {},
        compiler_params=pltpu.CompilerParams(vmem_limit_bytes=24 * 1024 * 1024),
        name=name,
    )


def iota(shape, dim):
    return lax.broadcasted_iota(jnp.int32, shape, dim)


def shape_of(shape, dtype):
    return jax.ShapeDtypeStruct(shape, dtype)


def frequencies():
    parts = []
    for size in (HD // 4, HD * 3 // 8, HD * 3 // 8):
        rate = 1.0 / np.float32(10000.0) ** (
            np.arange(0, size, 2).astype(np.float32) / np.float32(size)
        )
        parts.append(np.repeat(rate.astype(np.float32), 2))
    rate = np.concatenate(parts)
    return np.concatenate([rate, rate])[None, :].astype(np.float32)


def offset_in_patch(index, half):
    return (2 * ((index >> 2) & 1) + half) * 64 + 4 * (index >> 3) + (index & 3)


def prepare_kernel(scalars, row_ref, ada_ref, rate_ref, rec_ref, mod_out, tables_out):
    half = scalars[0]
    time_row = row_ref[pl.ds(scalars[5], 1), :]
    embedding = (time_row / (1.0 + jnp.exp(-time_row))).astype(BF)
    embedding = jnp.broadcast_to(embedding, (8, embedding.shape[1]))
    part = lax.dot_general(
        embedding, ada_ref[...], (((1,), (1,)), ((), ())), preferred_element_type=F32
    )[0:1]
    high = part.astype(BF)
    mod_out[0:1, :] = high
    mod_out[1:2, :] = (part - high.astype(F32)).astype(BF)

    rate = rate_ref[...]

    def tables(position, rows, at):
        text = position < TXT
        index = jnp.maximum(position - TXT, 0).astype(F32)
        frame = jnp.floor((index + 0.5) * (1.0 / (GH * GW)))
        line = jnp.floor((index + 0.5) * (1.0 / GW))
        width = index - line * GW
        height = line - jnp.floor((line + 0.5) * (1.0 / GH)) * GH
        lane = iota((rows, 128), 1) & (HD - 1)
        coordinate = jnp.where(lane < HD // 4, frame, jnp.where(lane < HD // 4 + HD * 3 // 8, height, width))
        phase = coordinate * rate
        tables_out[0, at : at + rows, :] = jnp.where(text, 1.0, jnp.cos(phase))
        tables_out[1, at : at + rows, :] = jnp.where(text, 0.0, jnp.sin(phase))
        tables_out[2, at : at + rows, :] = jnp.where(text, 1.0, 0.0)

    tables(offset_in_patch(iota((GROUP, 128), 0), half) + scalars[6], GROUP, 0)
    slot = rec_ref[...]
    start = jnp.where(
        slot < PLEN,
        scalars[1],
        jnp.where(slot < 2 * PLEN, scalars[2], jnp.where(slot < 3 * PLEN, scalars[3], scalars[4])),
    )
    tables(start + (slot & (PLEN - 1)), REC_GROUP, GROUP)


def normalize(x_ref, mod_ref, tables_ref, norm_ref, small):
    chunks = D // 128
    rows = x_ref.shape[0]

    def over_chunks(step, start):
        return lax.fori_loop(0, chunks, lambda k, carry: step(pl.ds(pl.multiple_of(k * 128, 128), 128), carry), start, unroll=12)

    def add(lanes, total):
        return total + x_ref[:, lanes].astype(F32)

    mean = jnp.sum(over_chunks(add, jnp.zeros((rows, 128), F32)), axis=1, keepdims=True) * (1.0 / D)

    def add_square(lanes, total):
        centered = x_ref[:, lanes].astype(F32) - mean
        return total + centered * centered

    total = jnp.sum(over_chunks(add_square, jnp.zeros((rows, 128), F32)), axis=1, keepdims=True)
    factor = lax.rsqrt(total * (1.0 / D) + 1e-5)
    for copy in small:
        copy.wait()
    text = tables_ref[2] > 0.5

    def write(lanes, carry):
        shift = jnp.where(text, mod_ref[3:4, lanes], mod_ref[0:1, lanes])
        scale = jnp.where(text, mod_ref[4:5, lanes], mod_ref[1:2, lanes])
        centered = x_ref[:, lanes].astype(F32) - mean
        norm_ref[:, lanes] = (centered * factor * (1.0 + scale) + shift).astype(BF)
        return carry

    over_chunks(write, 0)


def heads_from(mixed, gain_ref, tables_ref, q_out, kv_out):
    rows = mixed.shape[0]
    lane = iota((128, 128), 1)
    block = jnp.where((iota((128, 128), 0) >> 6) == (lane >> 6), 1.0 / HD, 0.0).astype(BF)

    def group_mean(values):
        high = values.astype(BF)
        low = (values - high.astype(F32)).astype(BF)
        return jnp.dot(high, block, preferred_element_type=F32) + jnp.dot(
            low, block, preferred_element_type=F32
        )

    low_half = iota((rows, 128), 1) < HD
    even = (iota((rows, 128), 1) & 1) == 0
    cosine, sine = tables_ref[0], tables_ref[1]
    gain = gain_ref[...]
    other_gain = pltpu.roll(jnp.broadcast_to(gain, (8, 128)), 64, 1)[0:1]
    gains = (gain, other_gain, other_gain, gain)
    plain, turned = [], []
    for k in range(4):
        values = mixed[:, 128 * k : 128 * k + 128]
        plain.append(values)
        centered = values - group_mean(values)
        scaled = centered * lax.rsqrt(group_mean(centered * centered) + 1e-6) * gains[k]
        partner = jnp.where(even, -pltpu.roll(scaled, 127, 1), pltpu.roll(scaled, 1, 1))
        turned.append(scaled * cosine + partner * sine)
    last = jnp.concatenate([mixed[:, 512:576], jnp.zeros((rows, 64), F32)], axis=1)
    keys_values = (
        pltpu.roll(jnp.where(low_half, plain[1], turned[0]), 64, 1).astype(BF),
        jnp.where(low_half, turned[2], plain[2]).astype(BF),
        pltpu.roll(jnp.where(low_half, last, turned[3]), 64, 1).astype(BF),
    )
    for copy in range(kv_out.shape[0]):
        for head in range(3):
            kv_out[copy, 0:rows, 128 * head : 128 * head + 128] = keys_values[head]
    if q_out is None:
        return
    zero = jnp.zeros((rows, 128), F32)
    q_out[:, 0:128] = (jnp.where(low_half, turned[0], zero) * 0.125).astype(BF)
    q_out[:, 128:256] = (jnp.where(low_half, pltpu.roll(turned[1], 64, 1), zero) * 0.125).astype(BF)
    q_out[:, 256:384] = (jnp.where(low_half, turned[3], zero) * 0.125).astype(BF)


def times_weights(norm, weights):
    return lax.dot_general(norm, weights, (((1,), (1,)), ((), ())), preferred_element_type=F32)


def small_copies(mod_hbm, rows_hbm, tables_hbm, layer, rows, mod_ref, gain_ref, tables_ref, sems):
    copies = [
        pltpu.make_async_copy(mod_hbm.at[layer], mod_ref, sems.at[0]),
        pltpu.make_async_copy(rows_hbm.at[4 * layer, pl.ds(16, 1), pl.ds(0, 128)], gain_ref, sems.at[1]),
        pltpu.make_async_copy(tables_hbm.at[:, rows, :], tables_ref, sems.at[2]),
    ]
    for copy in copies:
        copy.start()
    return copies


def small_scratch(rows):
    return [
        pltpu.VMEM((6, D), F32),
        pltpu.VMEM((1, 128), F32),
        pltpu.VMEM((3, rows, 128), F32),
        pltpu.SemaphoreType.DMA((3,)),
    ]


def rec_kernel(
    scalars, gathered_ref, mod_hbm, rows_hbm, tables_hbm, w_ref,
    kv_out, x_ref, norm_ref, w_vmem, sem, mod_ref, gain_ref, tables_ref, sems,
):
    fetch = pltpu.make_async_copy(w_ref, w_vmem, sem)
    fetch.start()
    rows = pl.ds(GROUP, REC_GROUP)
    small = small_copies(mod_hbm, rows_hbm, tables_hbm, scalars[7], rows, mod_ref, gain_ref, tables_ref, sems)
    share = gathered_ref[:, D : D + 768]
    for k in range(4):
        pick = iota((REC_GROUP, GROUP), 1) == 4 * iota((REC_GROUP, GROUP), 0) + k
        pick = jnp.where(pick, 1.0, 0.0).astype(BF)
        x_ref[:, 768 * k : 768 * k + 768] = jnp.dot(pick, share, preferred_element_type=F32).astype(BF)
    normalize(x_ref, mod_ref, tables_ref, norm_ref, small)
    fetch.wait()
    heads_from(times_weights(norm_ref[...], w_vmem[...]), gain_ref, tables_ref, None, kv_out)


def qkv_kernel_of(layer):
    def qkv_kernel(
        x_ref, mod_hbm, rows_hbm, tables_hbm, packed_ref,
        q_out, kv_out, weights_out, gates_out, norm_ref, w_vmem, sems, mod_ref, gain_ref, tables_ref, small_sems,
    ):
        rows = pl.ds(0, GROUP)
        small = small_copies(mod_hbm, rows_hbm, tables_hbm, layer, rows, mod_ref, gain_ref, tables_ref, small_sems)

        def fetch(k):
            to = w_vmem.at[pl.ds(288 * (k % 2), 288), pl.ds(384 * (k // 2), 384)]
            return pltpu.make_async_copy(packed_ref.at[k, pl.ds(0, 288), :], to, sems.at[k])

        def pass_on(k):
            to = weights_out.at[pl.ds(96 * (k % 2), 96), pl.ds(384 * (k // 2), 384)]
            return pltpu.make_async_copy(packed_ref.at[k, pl.ds(288, 96), :], to, sems.at[16 + k])

        for k in range(16):
            fetch(k).start()
        normalize(x_ref, mod_ref, tables_ref, norm_ref, small)
        for k in range(16):
            pass_on(k).start()
        mixed = jnp.zeros((GROUP, 576), F32)
        for piece in range(4):
            for k in range(4 * piece, 4 * piece + 4):
                fetch(k).wait()
            lanes = slice(768 * piece, 768 * piece + 768)
            mixed = mixed + times_weights(norm_ref[:, lanes], w_vmem[:, lanes])
        heads_from(mixed, gain_ref, tables_ref, q_out, kv_out)
        gates_out[0:1, :] = mod_ref[2:3, :]
        gates_out[1:2, :] = mod_ref[5:6, :]
        for k in range(16):
            pass_on(k).wait()

    return qkv_kernel


def pack_kernel(row_ref, w_ref, out_ref, packed, sems):
    copies = []
    for k in range(4):
        lanes = pl.ds(pl.multiple_of(row_ref[0] * 768 + 384 * (k // 2), 128), 384)
        copies += [
            (w_ref.at[pl.ds(288 * (k % 2), 288), lanes], packed.at[k, pl.ds(0, 288), :]),
            (out_ref.at[pl.ds(96 * (k % 2), 96), lanes], packed.at[k, pl.ds(288, 96), :]),
        ]
    copies = [pltpu.make_async_copy(a, b, sems.at[n]) for n, (a, b) in enumerate(copies)]
    for copy in copies:
        copy.start()
    for copy in copies:
        copy.wait()


def attend(scalars, q_ref, cache_ref, keep_out, send_out):
    patch, core = scalars[7], scalars[9]
    key = iota((8, 1024), 1)
    key_patch = key >> 8
    within = key & (PLEN - 1)
    fresh_offset = (2 * ((within >> 2) & 1) + (within >> 7)) * 64 + 4 * ((within >> 3) & 15) + (within & 3)
    offset = jnp.where(key_patch <= patch, fresh_offset, within)
    count = jnp.where(
        key_patch == 0,
        scalars[11],
        jnp.where(key_patch == 1, scalars[12], jnp.where(key_patch == 2, scalars[13], scalars[14])),
    )
    live = (offset < count)[0:1]
    outs = []
    for head in range(3):
        lanes = slice(128 * head, 128 * head + 128)
        keys_values = cache_ref[:, lanes]
        scores = lax.dot_general(
            q_ref[:, lanes], keys_values, (((1,), (1,)), ((), ())), preferred_element_type=F32
        )
        weights = jnp.where(live, jnp.exp(scores), 0.0)
        total = jnp.sum(weights, axis=1, keepdims=True)
        mixed = jnp.dot(weights.astype(BF), keys_values, preferred_element_type=F32)
        outs.append(mixed / total)
    low = iota((GROUP, 128), 1) < HD
    first = jnp.where(low, pltpu.roll(outs[0], 64, 1), outs[1]).astype(BF)
    second = jnp.where(low, pltpu.roll(outs[2], 64, 1), 0.0).astype(BF)
    for z in range(8):
        to = slice(8 * z, 8 * z + 8)
        even, odd = slice(16 * z, 16 * z + 8), slice(16 * z + 8, 16 * z + 16)
        for value, lanes in ((first, slice(0, 128)), (second, slice(128, 256))):
            keep_out[to, lanes] = jnp.where(core == 0, value[even], value[odd])
            send_out[to, lanes] = jnp.where(core == 0, value[odd], value[even])


def merge_copies(layer, targets_hbm, rec_ref, stale_ref, base_ref, rec_vmem, target_ref, sems):
    copies = [
        pltpu.make_async_copy(
            rec_ref.at[2 * layer + h],
            rec_vmem.at[pl.ds(REC_GROUP * h, REC_GROUP), :],
            sems.at[h],
        )
        for h in range(2)
    ]
    copies += [
        pltpu.make_async_copy(
            stale_ref.at[2 * layer + h], base_ref.at[pl.ds(PLEN + STALE * h, STALE), :], sems.at[2 + h]
        )
        for h in range(2)
    ]
    copies.append(pltpu.make_async_copy(targets_hbm, target_ref, sems.at[4]))
    for copy in copies:
        copy.start()
    return copies


def merge(copies, base_ref, rec_vmem, target_ref, table_ref):
    rec_vmem[2 * REC_GROUP :, :] = jnp.zeros((128 - 2 * REC_GROUP, 384), BF)
    for copy in copies:
        copy.wait()
    match = iota((3 * PLEN, 128), 0) + PLEN == target_ref[0:1, :]
    chosen = jnp.where(match, 1.0, 0.0)
    hit = jnp.sum(chosen, axis=1, keepdims=True) > 0.5
    placed = jnp.dot(chosen.astype(BF), rec_vmem[...], preferred_element_type=F32)
    table_ref[PLEN:, :] = jnp.where(hit, placed, base_ref[PLEN:, :].astype(F32)).astype(BF)


def merge_scratch():
    return [
        pltpu.VMEM((1024, 384), BF),
        pltpu.VMEM((128, 384), BF),
        pltpu.VMEM((8, 128), jnp.int32),
        pltpu.SemaphoreType.DMA((5,)),
    ]


def table_kernel_of(layer):
    def table_kernel(fresh_ref, targets_hbm, rec_ref, stale_ref, table_out, base_ref, rec_vmem, target_ref, sems):
        del fresh_ref
        copies = merge_copies(layer, targets_hbm, rec_ref, stale_ref, base_ref, rec_vmem, target_ref, sems)
        table_out[0:PLEN, :] = jnp.zeros((PLEN, 384), BF)
        merge(copies, base_ref, rec_vmem, target_ref, table_out)

    return table_kernel


def weight_copies(own_hbm, other_hbm, weights_out, sems):
    copies = [
        pltpu.make_async_copy(own_hbm, weights_out.at[0], sems.at[0]),
        pltpu.make_async_copy(other_hbm, weights_out.at[1], sems.at[1]),
    ]
    for copy in copies:
        copy.start()
    return copies


def attend_kernel(
    scalars, q_ref, own_ref, back1_ref, back2_ref, back3_ref, table_ref, own_hbm, other_hbm,
    keep_out, send_out, weights_out, cache_ref, weight_sems,
):
    section, half = scalars[7], scalars[0]
    weights = weight_copies(own_hbm, other_hbm, weights_out, weight_sems)
    for patch in range(1, 4):

        @pl.when(patch > section)
        def _(patch=patch):
            rows = slice(PLEN * patch, PLEN * patch + PLEN)
            cache_ref[rows, :] = table_ref[rows, :]

    for back, piece in enumerate((own_ref, back1_ref, back2_ref, back3_ref)):

        @pl.when(section >= back)
        def _(back=back, piece=piece):
            for at, rows in ((half, slice(0, GROUP)), (1 - half, slice(GROUP, 2 * GROUP))):
                start = pl.multiple_of((section - back) * PLEN + at * GROUP, GROUP)
                cache_ref[pl.ds(start, GROUP), :] = piece[rows, :]

    attend(scalars, q_ref, cache_ref, keep_out, send_out)
    for copy in weights:
        copy.wait()


def project_kernel(keep_ref, got_ref, weights_ref, out_ref):
    out = jnp.dot(keep_ref[:, 0:192], weights_ref[0], preferred_element_type=F32)
    out = out + jnp.dot(got_ref[:, 0:192], weights_ref[1], preferred_element_type=F32)
    out_ref[...] = out.astype(BF)


def residual_kernel(scalars, parts_ref, x_ref, gates_ref, out_ref):
    row = iota((8, 128), 0)
    offset = (2 * (row >> 2) + scalars[0]) * 64 + 4 * scalars[10] + (row & 3)
    text = (offset + scalars[6]) < TXT
    for k in range(D // 128):
        lanes = slice(128 * k, 128 * k + 128)
        total = parts_ref[0, :, lanes].astype(F32)
        for source in range(1, 8):
            total = total + parts_ref[source, :, lanes].astype(F32)
        gate = jnp.where(text, gates_ref[1:2, lanes], gates_ref[0:1, lanes])
        out_ref[:, lanes] = (x_ref[:, lanes].astype(F32) + gate * total).astype(BF)


def time_block(timestep, time_table):
    return lax.dynamic_slice(time_table, ((timestep[0] // 8) * 8, 0), (8, time_table.shape[1]))


def swapped(value, axis):
    return lax.ppermute(value, axis, [(0, 1), (1, 0)])


def local(
    hidden,
    patch_counts,
    timestep,
    time_table,
    ada_weight,
    qkv_weight,
    out_weight,
    qk_gain,
    stale_kv,
    stale_inputs,
    recompute_slots,
):
    section = lax.axis_index("section")
    req = lax.axis_index("req")
    half = lax.axis_index("half")
    core = lax.axis_index("core")
    col = lax.axis_index("z") * 2 + core
    first_req = req == 0
    sections = lax.axis_size("section")
    patches = hidden.shape[0]

    row_index = req * 2 + half
    weights_qkv = pltpu.with_memory_space_constraint(qkv_weight[0].T, pltpu.HBM)
    packed = call(
        pack_kernel,
        shape_of((4, 384, 384), BF),
        [SMEM, HBM, HBM],
        "pack",
        out_specs=HBM,
        scratch=[pltpu.SemaphoreType.DMA((8,))],
    )(
        row_index[None].astype(jnp.int32),
        weights_qkv,
        pltpu.with_memory_space_constraint(out_weight[0], pltpu.HBM),
    )
    chunks = lax.all_to_all(packed, "section", 0, 0)
    layers = [
        lax.all_gather(chunks[layer], ("req", "half", "section"), axis=0, tiled=False) for layer in range(sections)
    ]
    peers = ("section", "half")
    copies = lax.axis_size(peers)
    stale_share = lax.dynamic_slice(stale_kv, (0, PLEN + STALE * half, req, 0, 0), (1, STALE, 1, 3, 128))
    stale_share = stale_share.reshape(1, STALE, 384)
    stale_all = lax.all_to_all(jnp.broadcast_to(stale_share, (copies, STALE, 384)), peers, 0, 0)

    def of_request(value, axis):
        both = [lax.index_in_dim(value, r, axis, keepdims=False) for r in range(2)]
        return jnp.where(first_req, both[0], both[1]), jnp.where(first_req, both[1], both[0])

    def by_request(value, got):
        own = [lax.index_in_dim(value, r, 1, keepdims=False) for r in range(2)]
        far = [lax.index_in_dim(got, r, 1, keepdims=False) for r in range(2)]
        return jnp.where(
            first_req, jnp.concatenate([own[0], far[0]], axis=0), jnp.concatenate([far[1], own[1]], axis=0)
        )

    patch_rows = lax.dynamic_index_in_dim(hidden, section, 0, keepdims=False)
    tokens = by_request(patch_rows, swapped(patch_rows, "req"))
    rec_tokens = by_request(stale_inputs[0], swapped(stale_inputs[0], "req"))

    counts, _ = of_request(patch_counts, 0)
    starts = jnp.stack([jnp.int32(0), counts[0], counts[0] + counts[1], counts[0] + counts[1] + counts[2]])
    slots, _ = of_request(recompute_slots, 0)
    slots = slots.reshape(2, 2, 16)
    by_half = [slots[:, h].T.reshape(REC_GROUP) for h in range(2)]
    target_own = jnp.where(half == 0, by_half[0], by_half[1])
    targets = jnp.concatenate(by_half + [jnp.full((64,), -1, jnp.int32)])
    targets = jnp.broadcast_to(targets[None, :], (8, 128))

    own_start = lax.dynamic_index_in_dim(starts, section, 0, keepdims=True)
    scalars = jnp.concatenate(
        [half[None], starts, timestep % 8, own_start, jnp.stack([section, row_index, core, col]), counts, req[None]]
    ).astype(jnp.int32)
    mod_part, tables = call(
        prepare_kernel,
        (shape_of((2, 288), BF), shape_of((3, GROUP + REC_GROUP, 128), F32)),
        [SMEM, VMEM, VMEM, VMEM, VMEM],
        "prepare",
    )(
        scalars,
        time_block(timestep, time_table),
        ada_weight[0].T,
        jnp.asarray(frequencies()),
        jnp.broadcast_to(target_own[:, None], (REC_GROUP, 128)),
    )

    payload = jnp.concatenate(
        [
            tokens,
            rec_tokens.reshape(8, 768),
            jnp.pad(mod_part.reshape(8, 72), ((0, 0), (0, 56))),
        ],
        axis=1,
    )
    gathered = lax.all_gather(payload, COL, axis=0, tiled=True)
    pieces = gathered[:, D + 768 : D + 840].reshape(16, 2, 288).astype(F32)
    summed = pieces[:, 0] + pieces[:, 1]
    gain_row = jnp.pad(qk_gain[0].reshape(1, 128), ((0, 0), (0, 160)))
    rows = jnp.concatenate([summed, gain_row], axis=0)[None]
    everyone = ("section",) + ROW
    rows, stale_all = lax.optimization_barrier((rows, stale_all))
    rows = lax.all_to_all(jnp.broadcast_to(rows, (lax.axis_size(everyone), 17, 288)), everyone, 0, 0)
    modulation = rows[:, :16].reshape(sections, 6, D)
    in_hbm = [pltpu.with_memory_space_constraint(value, pltpu.HBM) for value in (modulation, rows, tables)]
    rec_fresh = call(
        rec_kernel,
        shape_of((copies, REC_GROUP, 384), BF),
        [SMEM, VMEM] + [HBM] * 4,
        "rec",
        scratch=[
            pltpu.VMEM((REC_GROUP, D), BF),
            pltpu.VMEM((REC_GROUP, D), BF),
            pltpu.VMEM((576, D), BF),
            pltpu.SemaphoreType.DMA,
        ]
        + small_scratch(REC_GROUP),
    )(scalars, gathered, *in_hbm, weights_qkv)
    targets = pltpu.with_memory_space_constraint(targets, pltpu.HBM)

    def upwards(fresh):
        both = jnp.concatenate([fresh, swapped(fresh, "half")], axis=0)
        pairs = [[(i, i + back) for i in range(sections - back)] for back in range(1, sections)]
        return [both] + [lax.ppermute(both, "section", steps) for steps in pairs]

    half_rows = shape_of((64, 256), BF)
    group, rec_fresh = lax.optimization_barrier((gathered, rec_fresh))
    rec_all = lax.all_to_all(rec_fresh, peers, 0, 0)
    current, outs = tokens, []
    for layer in range(sections):
        packed = pltpu.with_memory_space_constraint(layers[layer], pltpu.HBM)
        if layer > 0:
            group = lax.all_gather(current, COL, axis=0, tiled=True)
            group = pltpu.with_memory_space_constraint(group, pltpu.VMEM)
        queries, fresh, out_own, gates = call(
            qkv_kernel_of(layer),
            (
                shape_of((GROUP, 384), BF),
                shape_of((1, GROUP, 384), BF),
                shape_of((192, D), BF),
                shape_of((2, D), F32),
            ),
            [VMEM] + [HBM] * 4,
            "qkv",
            scratch=[pltpu.VMEM((GROUP, D), BF), pltpu.VMEM((576, D), BF), pltpu.SemaphoreType.DMA((32,))]
            + small_scratch(GROUP),
        )(group, *in_hbm, packed)
        out_other = swapped(out_own, "core")
        attend_out = (half_rows, half_rows, shape_of((2, 192, D), BF))
        attend_scratch = [pltpu.VMEM((1024, 384), BF), pltpu.SemaphoreType.DMA((2,))]
        pieces = upwards(fresh[0])
        merged = call(
            table_kernel_of(layer),
            shape_of((1024, 384), BF),
            [HBM] * 4,
            "table",
            scratch=merge_scratch(),
        )(fresh, targets, rec_all, stale_all)
        keep, send, weights_out = call(
            attend_kernel,
            attend_out,
            [SMEM] + [VMEM] * 6 + [HBM] * 2,
            "attend",
            scratch=attend_scratch,
        )(scalars, queries, *pieces, merged, out_own, out_other)
        projected = call(project_kernel, shape_of((64, D), BF), [VMEM] * 3, "project")(
            keep, swapped(send, "core"), weights_out
        )
        parts = lax.all_to_all(projected.reshape(8, 8, D), "z", 0, 0)
        current = call(residual_kernel, shape_of((8, D), BF), [SMEM, VMEM, VMEM, VMEM], "residual")(
            scalars, parts, current, gates
        )
        outs.append(current)

    leaving = jnp.stack(outs).reshape(sections * 2, 4, D)
    out = lax.all_to_all(leaving, ("section", "req"), 0, 0).reshape(patches, 2, 4, D)
    return jnp.transpose(out, (0, 2, 1, 3))[None]


def solution(mesh):
    sizes = tuple(mesh.devices.shape)
    fine = Mesh(
        mesh.devices.reshape(sizes[0], 2, sizes[1] // 2, sizes[2] // 2, 2),
        ("section", "req", "half", "z", "core"),
    )
    return jax.shard_map(
        local,
        mesh=fine,
        in_specs=(
            P(None, ROW_AXES, None, None),
            P(),
            P(),
            P(),
            P("section", None, ROW_AXES),
            P("section", None, COL),
            P("section", COL, None),
            P("section", None, None),
            P("section", None, None, COL, None),
            P("section", ROW_AXES, None, None),
            P(),
        ),
        out_specs=P("section", None, ROW_AXES, None, None),
        check_vma=False,
    )
```

```python
import jax
import jax.numpy as jnp
import numpy as np
from jax import lax
from jax.experimental import pallas as pl
from jax.experimental.pallas import tpu as pltpu
from jax.sharding import Mesh
from jax.sharding import PartitionSpec as P

HD = 64
D = 3072
TXT = 226
GH = 30
GW = 45
PLEN = 256
GROUP = 128
REC_GROUP = 32
STALE = 384
BF = jnp.bfloat16
F32 = jnp.float32
COL = ("z", "core")
ROW = ("req", "half")
ROW_AXES = ("req", "half", "z", "core")


SMEM = pl.BlockSpec(memory_space=pltpu.SMEM)
VMEM = pl.BlockSpec(memory_space=pltpu.VMEM)
HBM = pl.BlockSpec(memory_space=pltpu.HBM)


def call(kernel, out_shape, in_specs, name, out_specs=None, scratch=(), aliases=None):
    if out_specs is None:
        out_specs = jax.tree.map(lambda _: VMEM, out_shape)
    return pl.pallas_call(
        kernel,
        out_shape=out_shape,
        in_specs=in_specs,
        out_specs=out_specs,
        scratch_shapes=list(scratch),
        input_output_aliases=aliases or {},
        compiler_params=pltpu.CompilerParams(vmem_limit_bytes=24 * 1024 * 1024),
        name=name,
    )


def iota(shape, dim):
    return lax.broadcasted_iota(jnp.int32, shape, dim)


def shape_of(shape, dtype):
    return jax.ShapeDtypeStruct(shape, dtype)


def frequencies():
    parts = []
    for size in (HD // 4, HD * 3 // 8, HD * 3 // 8):
        rate = 1.0 / np.float32(10000.0) ** (
            np.arange(0, size, 2).astype(np.float32) / np.float32(size)
        )
        parts.append(np.repeat(rate.astype(np.float32), 2))
    rate = np.concatenate(parts)
    return np.concatenate([rate, rate])[None, :].astype(np.float32)


def offset_in_patch(index, half):
    return (2 * ((index >> 2) & 1) + half) * 64 + 4 * (index >> 3) + (index & 3)


def prepare_kernel(scalars, row_ref, ada_ref, rate_ref, rec_ref, mod_out, tables_out):
    half = scalars[0]
    time_row = row_ref[pl.ds(scalars[5], 1), :]
    embedding = (time_row / (1.0 + jnp.exp(-time_row))).astype(BF)
    embedding = jnp.broadcast_to(embedding, (8, embedding.shape[1]))
    part = lax.dot_general(
        embedding, ada_ref[...], (((1,), (1,)), ((), ())), preferred_element_type=F32
    )[0:1]
    high = part.astype(BF)
    mod_out[0:1, :] = high
    mod_out[1:2, :] = (part - high.astype(F32)).astype(BF)

    rate = rate_ref[...]

    def tables(position, rows, at):
        text = position < TXT
        index = jnp.maximum(position - TXT, 0).astype(F32)
        frame = jnp.floor((index + 0.5) * (1.0 / (GH * GW)))
        line = jnp.floor((index + 0.5) * (1.0 / GW))
        width = index - line * GW
        height = line - jnp.floor((line + 0.5) * (1.0 / GH)) * GH
        lane = iota((rows, 128), 1) & (HD - 1)
        coordinate = jnp.where(lane < HD // 4, frame, jnp.where(lane < HD // 4 + HD * 3 // 8, height, width))
        phase = coordinate * rate
        tables_out[0, at : at + rows, :] = jnp.where(text, 1.0, jnp.cos(phase))
        tables_out[1, at : at + rows, :] = jnp.where(text, 0.0, jnp.sin(phase))
        tables_out[2, at : at + rows, :] = jnp.where(text, 1.0, 0.0)

    tables(offset_in_patch(iota((GROUP, 128), 0), half) + scalars[6], GROUP, 0)
    slot = rec_ref[...]
    start = jnp.where(
        slot < PLEN,
        scalars[1],
        jnp.where(slot < 2 * PLEN, scalars[2], jnp.where(slot < 3 * PLEN, scalars[3], scalars[4])),
    )
    tables(start + (slot & (PLEN - 1)), REC_GROUP, GROUP)


def normalize(x_ref, mod_ref, tables_ref, norm_ref, small):
    chunks = D // 128
    rows = x_ref.shape[0]

    def over_chunks(step, start):
        return lax.fori_loop(0, chunks, lambda k, carry: step(pl.ds(pl.multiple_of(k * 128, 128), 128), carry), start, unroll=6)

    def add(lanes, total):
        return total + x_ref[:, lanes].astype(F32)

    mean = jnp.sum(over_chunks(add, jnp.zeros((rows, 128), F32)), axis=1, keepdims=True) * (1.0 / D)

    def add_square(lanes, total):
        centered = x_ref[:, lanes].astype(F32) - mean
        return total + centered * centered

    total = jnp.sum(over_chunks(add_square, jnp.zeros((rows, 128), F32)), axis=1, keepdims=True)
    factor = lax.rsqrt(total * (1.0 / D) + 1e-5)
    for copy in small:
        copy.wait()
    text = tables_ref[2] > 0.5

    def write(lanes, carry):
        shift = jnp.where(text, mod_ref[3:4, lanes], mod_ref[0:1, lanes])
        scale = jnp.where(text, mod_ref[4:5, lanes], mod_ref[1:2, lanes])
        centered = x_ref[:, lanes].astype(F32) - mean
        norm_ref[:, lanes] = (centered * factor * (1.0 + scale) + shift).astype(BF)
        return carry

    over_chunks(write, 0)


def heads_from(mixed, gain_ref, tables_ref, q_out, kv_out):
    rows = mixed.shape[0]
    lane = iota((128, 128), 1)
    block = jnp.where((iota((128, 128), 0) >> 6) == (lane >> 6), 1.0 / HD, 0.0).astype(BF)

    def group_mean(values):
        high = values.astype(BF)
        low = (values - high.astype(F32)).astype(BF)
        return jnp.dot(high, block, preferred_element_type=F32) + jnp.dot(
            low, block, preferred_element_type=F32
        )

    low_half = iota((rows, 128), 1) < HD
    even = (iota((rows, 128), 1) & 1) == 0
    cosine, sine = tables_ref[0], tables_ref[1]
    gain = gain_ref[...]
    other_gain = pltpu.roll(jnp.broadcast_to(gain, (8, 128)), 64, 1)[0:1]
    gains = (gain, other_gain, other_gain, gain)
    plain, turned = [], []
    for k in range(4):
        values = mixed[:, 128 * k : 128 * k + 128]
        plain.append(values)
        centered = values - group_mean(values)
        scaled = centered * lax.rsqrt(group_mean(centered * centered) + 1e-6) * gains[k]
        partner = jnp.where(even, -pltpu.roll(scaled, 127, 1), pltpu.roll(scaled, 1, 1))
        turned.append(scaled * cosine + partner * sine)
    last = jnp.concatenate([mixed[:, 512:576], jnp.zeros((rows, 64), F32)], axis=1)
    keys_values = (
        pltpu.roll(jnp.where(low_half, plain[1], turned[0]), 64, 1).astype(BF),
        jnp.where(low_half, turned[2], plain[2]).astype(BF),
        pltpu.roll(jnp.where(low_half, last, turned[3]), 64, 1).astype(BF),
    )
    for copy in range(kv_out.shape[0]):
        for head in range(3):
            kv_out[copy, 0:rows, 128 * head : 128 * head + 128] = keys_values[head]
    if q_out is None:
        return
    zero = jnp.zeros((rows, 128), F32)
    q_out[:, 0:128] = (jnp.where(low_half, turned[0], zero) * 0.125).astype(BF)
    q_out[:, 128:256] = (jnp.where(low_half, pltpu.roll(turned[1], 64, 1), zero) * 0.125).astype(BF)
    q_out[:, 256:384] = (jnp.where(low_half, turned[3], zero) * 0.125).astype(BF)


def times_weights(norm, weights):
    return lax.dot_general(norm, weights, (((1,), (1,)), ((), ())), preferred_element_type=F32)


def small_copies(mod_hbm, rows_hbm, tables_hbm, layer, rows, mod_ref, gain_ref, tables_ref, sems):
    copies = [
        pltpu.make_async_copy(mod_hbm.at[layer], mod_ref, sems.at[0]),
        pltpu.make_async_copy(rows_hbm.at[4 * layer, pl.ds(16, 1), pl.ds(0, 128)], gain_ref, sems.at[1]),
        pltpu.make_async_copy(tables_hbm.at[:, rows, :], tables_ref, sems.at[2]),
    ]
    for copy in copies:
        copy.start()
    return copies


def small_scratch(rows):
    return [
        pltpu.VMEM((6, D), F32),
        pltpu.VMEM((1, 128), F32),
        pltpu.VMEM((3, rows, 128), F32),
        pltpu.SemaphoreType.DMA((3,)),
    ]


def rec_kernel(
    scalars, gathered_ref, mod_hbm, rows_hbm, tables_hbm, w_ref,
    kv_out, x_ref, norm_ref, w_vmem, sem, mod_ref, gain_ref, tables_ref, sems,
):
    fetch = pltpu.make_async_copy(w_ref, w_vmem, sem)
    fetch.start()
    rows = pl.ds(GROUP, REC_GROUP)
    small = small_copies(mod_hbm, rows_hbm, tables_hbm, scalars[7], rows, mod_ref, gain_ref, tables_ref, sems)
    share = gathered_ref[:, D : D + 768]
    for k in range(4):
        pick = iota((REC_GROUP, GROUP), 1) == 4 * iota((REC_GROUP, GROUP), 0) + k
        pick = jnp.where(pick, 1.0, 0.0).astype(BF)
        x_ref[:, 768 * k : 768 * k + 768] = jnp.dot(pick, share, preferred_element_type=F32).astype(BF)
    normalize(x_ref, mod_ref, tables_ref, norm_ref, small)
    fetch.wait()
    heads_from(times_weights(norm_ref[...], w_vmem[...]), gain_ref, tables_ref, None, kv_out)


def qkv_kernel_of(layer):
    def qkv_kernel(
        x_ref, rec_ref, mod_hbm, rows_hbm, tables_hbm, packed_ref,
        q_out, kv_out, weights_out, gates_out, norm_ref, w_vmem, sems, mod_ref, gain_ref, tables_ref, small_sems,
    ):
        rows = pl.ds(0, GROUP)
        small = small_copies(mod_hbm, rows_hbm, tables_hbm, layer, rows, mod_ref, gain_ref, tables_ref, small_sems)

        def fetch(k):
            to = w_vmem.at[pl.ds(288 * (k % 2), 288), pl.ds(384 * (k // 2), 384)]
            return pltpu.make_async_copy(packed_ref.at[k, pl.ds(0, 288), :], to, sems.at[k])

        def pass_on(k):
            to = weights_out.at[pl.ds(96 * (k % 2), 96), pl.ds(384 * (k // 2), 384)]
            return pltpu.make_async_copy(packed_ref.at[k, pl.ds(288, 96), :], to, sems.at[16 + k])

        for k in range(16):
            fetch(k).start()
        normalize(x_ref, mod_ref, tables_ref, norm_ref, small)
        for k in range(16):
            pass_on(k).start()
        mixed = jnp.zeros((GROUP, 576), F32)
        for piece in range(4):
            for k in range(4 * piece, 4 * piece + 4):
                fetch(k).wait()
            lanes = slice(768 * piece, 768 * piece + 768)
            mixed = mixed + times_weights(norm_ref[:, lanes], w_vmem[:, lanes])
        heads_from(mixed, gain_ref, tables_ref, q_out, kv_out)
        gates_out[0:1, :] = mod_ref[2:3, :]
        gates_out[1:2, :] = mod_ref[5:6, :]
        if layer == 0:
            for copy in range(kv_out.shape[0]):
                kv_out[copy, GROUP:, :] = rec_ref[0]
        for k in range(16):
            pass_on(k).wait()

    return qkv_kernel


def pack_kernel(row_ref, w_ref, out_ref, packed, sems):
    copies = []
    for k in range(4):
        lanes = pl.ds(pl.multiple_of(row_ref[0] * 768 + 384 * (k // 2), 128), 384)
        copies += [
            (w_ref.at[pl.ds(288 * (k % 2), 288), lanes], packed.at[k, pl.ds(0, 288), :]),
            (out_ref.at[pl.ds(96 * (k % 2), 96), lanes], packed.at[k, pl.ds(288, 96), :]),
        ]
    copies = [pltpu.make_async_copy(a, b, sems.at[n]) for n, (a, b) in enumerate(copies)]
    for copy in copies:
        copy.start()
    for copy in copies:
        copy.wait()


def attend(scalars, q_ref, cache_ref, keep_out, send_out):
    patch, core = scalars[7], scalars[9]
    key = iota((8, 1024), 1)
    key_patch = key >> 8
    within = key & (PLEN - 1)
    fresh_offset = (2 * ((within >> 2) & 1) + (within >> 7)) * 64 + 4 * ((within >> 3) & 15) + (within & 3)
    offset = jnp.where(key_patch <= patch, fresh_offset, within)
    count = jnp.where(
        key_patch == 0,
        scalars[11],
        jnp.where(key_patch == 1, scalars[12], jnp.where(key_patch == 2, scalars[13], scalars[14])),
    )
    live = (offset < count)[0:1]
    outs = []
    for head in range(3):
        lanes = slice(128 * head, 128 * head + 128)
        keys_values = cache_ref[:, lanes]
        scores = lax.dot_general(
            q_ref[:, lanes], keys_values, (((1,), (1,)), ((), ())), preferred_element_type=F32
        )
        weights = jnp.where(live, jnp.exp(scores), 0.0)
        total = jnp.sum(weights, axis=1, keepdims=True)
        mixed = jnp.dot(weights.astype(BF), keys_values, preferred_element_type=F32)
        outs.append(mixed / total)
    low = iota((GROUP, 128), 1) < HD
    first = jnp.where(low, pltpu.roll(outs[0], 64, 1), outs[1]).astype(BF)
    second = jnp.where(low, pltpu.roll(outs[2], 64, 1), 0.0).astype(BF)
    for z in range(8):
        to = slice(8 * z, 8 * z + 8)
        even, odd = slice(16 * z, 16 * z + 8), slice(16 * z + 8, 16 * z + 16)
        for value, lanes in ((first, slice(0, 128)), (second, slice(128, 256))):
            keep_out[to, lanes] = jnp.where(core == 0, value[even], value[odd])
            send_out[to, lanes] = jnp.where(core == 0, value[odd], value[even])


def merge_copies(layer, targets_hbm, rec_ref, stale_ref, base_ref, rec_vmem, target_ref, sems):
    copies = [
        pltpu.make_async_copy(
            rec_ref.at[2 * layer + h, pl.ds(GROUP, REC_GROUP), :],
            rec_vmem.at[pl.ds(REC_GROUP * h, REC_GROUP), :],
            sems.at[h],
        )
        for h in range(2)
    ]
    copies += [
        pltpu.make_async_copy(
            stale_ref.at[2 * layer + h], base_ref.at[pl.ds(PLEN + STALE * h, STALE), :], sems.at[2 + h]
        )
        for h in range(2)
    ]
    copies.append(pltpu.make_async_copy(targets_hbm, target_ref, sems.at[4]))
    for copy in copies:
        copy.start()
    return copies


def merge(copies, base_ref, rec_vmem, target_ref, table_ref):
    rec_vmem[2 * REC_GROUP :, :] = jnp.zeros((128 - 2 * REC_GROUP, 384), BF)
    for copy in copies:
        copy.wait()
    match = iota((3 * PLEN, 128), 0) + PLEN == target_ref[0:1, :]
    chosen = jnp.where(match, 1.0, 0.0)
    hit = jnp.sum(chosen, axis=1, keepdims=True) > 0.5
    placed = jnp.dot(chosen.astype(BF), rec_vmem[...], preferred_element_type=F32)
    table_ref[PLEN:, :] = jnp.where(hit, placed, base_ref[PLEN:, :].astype(F32)).astype(BF)


def merge_scratch():
    return [
        pltpu.VMEM((1024, 384), BF),
        pltpu.VMEM((128, 384), BF),
        pltpu.VMEM((8, 128), jnp.int32),
        pltpu.SemaphoreType.DMA((5,)),
    ]


def table_kernel_of(layer):
    def table_kernel(fresh_ref, targets_hbm, rec_ref, stale_ref, table_out, base_ref, rec_vmem, target_ref, sems):
        del fresh_ref
        copies = merge_copies(layer, targets_hbm, rec_ref, stale_ref, base_ref, rec_vmem, target_ref, sems)
        table_out[0:PLEN, :] = jnp.zeros((PLEN, 384), BF)
        merge(copies, base_ref, rec_vmem, target_ref, table_out)

    return table_kernel


def weight_copies(own_hbm, other_hbm, weights_out, sems):
    copies = [
        pltpu.make_async_copy(own_hbm, weights_out.at[0], sems.at[0]),
        pltpu.make_async_copy(other_hbm, weights_out.at[1], sems.at[1]),
    ]
    for copy in copies:
        copy.start()
    return copies


def attend_all_kernel_of(layer):
    def attend_all_kernel(
        scalars, q_ref, fresh_ref, targets_hbm, rec_ref, stale_ref, own_hbm, other_hbm,
        keep_out, send_out, weights_out, cache_ref, weight_sems, base_ref, rec_vmem, target_ref, sems,
    ):
        copies = merge_copies(layer, targets_hbm, rec_ref, stale_ref, base_ref, rec_vmem, target_ref, sems)
        weights = weight_copies(own_hbm, other_hbm, weights_out, weight_sems)
        merge(copies, base_ref, rec_vmem, target_ref, cache_ref)
        for patch in range(4):

            @pl.when(patch <= scalars[7])
            def _(patch=patch):
                cache_ref[PLEN * patch : PLEN * patch + PLEN, :] = jnp.concatenate(
                    [fresh_ref[2 * patch, 0:GROUP, :], fresh_ref[2 * patch + 1, 0:GROUP, :]], axis=0
                )

        attend(scalars, q_ref, cache_ref, keep_out, send_out)
        for copy in weights:
            copy.wait()

    return attend_all_kernel


def attend_kernel(
    scalars, q_ref, own_ref, back1_ref, back2_ref, back3_ref, table_ref, own_hbm, other_hbm,
    keep_out, send_out, weights_out, cache_ref, weight_sems,
):
    section, half = scalars[7], scalars[0]
    weights = weight_copies(own_hbm, other_hbm, weights_out, weight_sems)
    for patch in range(1, 4):

        @pl.when(patch > section)
        def _(patch=patch):
            rows = slice(PLEN * patch, PLEN * patch + PLEN)
            cache_ref[rows, :] = table_ref[rows, :]

    for back, piece in enumerate((own_ref, back1_ref, back2_ref, back3_ref)):

        @pl.when(section >= back)
        def _(back=back, piece=piece):
            for at, rows in ((half, slice(0, GROUP)), (1 - half, slice(GROUP, 2 * GROUP))):
                start = pl.multiple_of((section - back) * PLEN + at * GROUP, GROUP)
                cache_ref[pl.ds(start, GROUP), :] = piece[rows, :]

    attend(scalars, q_ref, cache_ref, keep_out, send_out)
    for copy in weights:
        copy.wait()


def project_kernel(keep_ref, got_ref, weights_ref, out_ref):
    out = jnp.dot(keep_ref[:, 0:192], weights_ref[0], preferred_element_type=F32)
    out = out + jnp.dot(got_ref[:, 0:192], weights_ref[1], preferred_element_type=F32)
    out_ref[...] = out.astype(BF)


def residual_kernel(scalars, parts_ref, x_ref, gates_ref, out_ref):
    row = iota((8, 128), 0)
    offset = (2 * (row >> 2) + scalars[0]) * 64 + 4 * scalars[10] + (row & 3)
    text = (offset + scalars[6]) < TXT
    for k in range(D // 128):
        lanes = slice(128 * k, 128 * k + 128)
        total = parts_ref[0, :, lanes].astype(F32)
        for source in range(1, 8):
            total = total + parts_ref[source, :, lanes].astype(F32)
        gate = jnp.where(text, gates_ref[1:2, lanes], gates_ref[0:1, lanes])
        out_ref[:, lanes] = (x_ref[:, lanes].astype(F32) + gate * total).astype(BF)


def time_block(timestep, time_table):
    return lax.dynamic_slice(time_table, ((timestep[0] // 8) * 8, 0), (8, time_table.shape[1]))


def swapped(value, axis):
    return lax.ppermute(value, axis, [(0, 1), (1, 0)])


def local(
    hidden,
    patch_counts,
    timestep,
    time_table,
    ada_weight,
    qkv_weight,
    out_weight,
    qk_gain,
    stale_kv,
    stale_inputs,
    recompute_slots,
):
    section = lax.axis_index("section")
    req = lax.axis_index("req")
    half = lax.axis_index("half")
    core = lax.axis_index("core")
    col = lax.axis_index("z") * 2 + core
    first_req = req == 0
    sections = lax.axis_size("section")
    patches = hidden.shape[0]

    row_index = req * 2 + half
    weights_qkv = pltpu.with_memory_space_constraint(qkv_weight[0].T, pltpu.HBM)
    packed = call(
        pack_kernel,
        shape_of((4, 384, 384), BF),
        [SMEM, HBM, HBM],
        "pack",
        out_specs=HBM,
        scratch=[pltpu.SemaphoreType.DMA((8,))],
    )(
        row_index[None].astype(jnp.int32),
        weights_qkv,
        pltpu.with_memory_space_constraint(out_weight[0], pltpu.HBM),
    )
    chunks = lax.all_to_all(packed, "section", 0, 0)
    layers = [
        lax.all_gather(chunks[layer], ("req", "half", "section"), axis=0, tiled=False) for layer in range(sections)
    ]
    peers = ("section", "half")
    copies = lax.axis_size(peers)
    stale_share = lax.dynamic_slice(stale_kv, (0, PLEN + STALE * half, req, 0, 0), (1, STALE, 1, 3, 128))
    stale_share = stale_share.reshape(1, STALE, 384)
    stale_all = lax.all_to_all(jnp.broadcast_to(stale_share, (copies, STALE, 384)), peers, 0, 0)

    def of_request(value, axis):
        both = [lax.index_in_dim(value, r, axis, keepdims=False) for r in range(2)]
        return jnp.where(first_req, both[0], both[1]), jnp.where(first_req, both[1], both[0])

    def by_request(value, got):
        own = [lax.index_in_dim(value, r, 1, keepdims=False) for r in range(2)]
        far = [lax.index_in_dim(got, r, 1, keepdims=False) for r in range(2)]
        return jnp.where(
            first_req, jnp.concatenate([own[0], far[0]], axis=0), jnp.concatenate([far[1], own[1]], axis=0)
        )

    patch_rows = lax.dynamic_index_in_dim(hidden, section, 0, keepdims=False)
    tokens = by_request(patch_rows, swapped(patch_rows, "req"))
    rec_tokens = by_request(stale_inputs[0], swapped(stale_inputs[0], "req"))

    counts, _ = of_request(patch_counts, 0)
    starts = jnp.stack([jnp.int32(0), counts[0], counts[0] + counts[1], counts[0] + counts[1] + counts[2]])
    slots, _ = of_request(recompute_slots, 0)
    slots = slots.reshape(2, 2, 16)
    by_half = [slots[:, h].T.reshape(REC_GROUP) for h in range(2)]
    target_own = jnp.where(half == 0, by_half[0], by_half[1])
    targets = jnp.concatenate(by_half + [jnp.full((64,), -1, jnp.int32)])
    targets = jnp.broadcast_to(targets[None, :], (8, 128))

    own_start = lax.dynamic_index_in_dim(starts, section, 0, keepdims=True)
    scalars = jnp.concatenate(
        [half[None], starts, timestep % 8, own_start, jnp.stack([section, row_index, core, col]), counts, req[None]]
    ).astype(jnp.int32)
    mod_part, tables = call(
        prepare_kernel,
        (shape_of((2, 288), BF), shape_of((3, GROUP + REC_GROUP, 128), F32)),
        [SMEM, VMEM, VMEM, VMEM, VMEM],
        "prepare",
    )(
        scalars,
        time_block(timestep, time_table),
        ada_weight[0].T,
        jnp.asarray(frequencies()),
        jnp.broadcast_to(target_own[:, None], (REC_GROUP, 128)),
    )

    payload = jnp.concatenate(
        [
            tokens,
            rec_tokens.reshape(8, 768),
            jnp.pad(mod_part.reshape(8, 72), ((0, 0), (0, 56))),
        ],
        axis=1,
    )
    gathered = lax.all_gather(payload, COL, axis=0, tiled=True)
    pieces = gathered[:, D + 768 : D + 840].reshape(16, 2, 288).astype(F32)
    summed = pieces[:, 0] + pieces[:, 1]
    gain_row = jnp.pad(qk_gain[0].reshape(1, 128), ((0, 0), (0, 160)))
    rows = jnp.concatenate([summed, gain_row], axis=0)[None]
    everyone = ("section",) + ROW
    rows, stale_all = lax.optimization_barrier((rows, stale_all))
    rows = lax.all_to_all(jnp.broadcast_to(rows, (lax.axis_size(everyone), 17, 288)), everyone, 0, 0)
    modulation = rows[:, :16].reshape(sections, 6, D)
    in_hbm = [pltpu.with_memory_space_constraint(value, pltpu.HBM) for value in (modulation, rows, tables)]
    rec_fresh = call(
        rec_kernel,
        shape_of((1, REC_GROUP, 384), BF),
        [SMEM, VMEM] + [HBM] * 4,
        "rec",
        scratch=[
            pltpu.VMEM((REC_GROUP, D), BF),
            pltpu.VMEM((REC_GROUP, D), BF),
            pltpu.VMEM((576, D), BF),
            pltpu.SemaphoreType.DMA,
        ]
        + small_scratch(REC_GROUP),
    )(scalars, gathered, *in_hbm, weights_qkv)
    targets = pltpu.with_memory_space_constraint(targets, pltpu.HBM)

    def upwards(fresh):
        both = jnp.concatenate([fresh, swapped(fresh, "half")], axis=0)
        pairs = [[(i, i + back) for i in range(sections - back)] for back in range(1, sections)]
        return [both] + [lax.ppermute(both, "section", steps) for steps in pairs]

    half_rows = shape_of((64, 256), BF)
    current, group, outs, first_fresh = tokens, gathered, [], None
    for layer in range(sections):
        packed = pltpu.with_memory_space_constraint(layers[layer], pltpu.HBM)
        if layer > 0:
            group = lax.all_gather(current, COL, axis=0, tiled=True)
            group = pltpu.with_memory_space_constraint(group, pltpu.VMEM)
        to_all = layer in (0, sections - 1)
        queries, fresh, out_own, gates = call(
            qkv_kernel_of(layer),
            (
                shape_of((GROUP, 384), BF),
                shape_of((copies if to_all else 1, GROUP + (REC_GROUP if layer == 0 else 0), 384), BF),
                shape_of((192, D), BF),
                shape_of((2, D), F32),
            ),
            [VMEM] * 2 + [HBM] * 4,
            "qkv",
            scratch=[pltpu.VMEM((GROUP, D), BF), pltpu.VMEM((576, D), BF), pltpu.SemaphoreType.DMA((32,))]
            + small_scratch(GROUP),
        )(group, rec_fresh, *in_hbm, packed)
        out_other = swapped(out_own, "core")
        attend_out = (half_rows, half_rows, shape_of((2, 192, D), BF))
        attend_scratch = [pltpu.VMEM((1024, 384), BF), pltpu.SemaphoreType.DMA((2,))]
        if to_all:
            fresh_all = lax.all_to_all(fresh, peers, 0, 0)
            first_fresh = fresh_all if layer == 0 else first_fresh
            keep, send, weights_out = call(
                attend_all_kernel_of(layer),
                attend_out,
                [SMEM, VMEM, VMEM] + [HBM] * 5,
                "attend_all",
                scratch=attend_scratch + merge_scratch(),
            )(scalars, queries, fresh_all, targets, first_fresh, stale_all, out_own, out_other)
        else:
            pieces = upwards(fresh[0])
            merged = call(
                table_kernel_of(layer),
                shape_of((1024, 384), BF),
                [HBM] * 4,
                "table",
                scratch=merge_scratch(),
            )(fresh, targets, first_fresh, stale_all)
            keep, send, weights_out = call(
                attend_kernel,
                attend_out,
                [SMEM] + [VMEM] * 6 + [HBM] * 2,
                "attend",
                scratch=attend_scratch,
            )(scalars, queries, *pieces, merged, out_own, out_other)
        projected = call(project_kernel, shape_of((64, D), BF), [VMEM] * 3, "project")(
            keep, swapped(send, "core"), weights_out
        )
        parts = lax.all_to_all(projected.reshape(8, 8, D), "z", 0, 0)
        current = call(residual_kernel, shape_of((8, D), BF), [SMEM, VMEM, VMEM, VMEM], "residual")(
            scalars, parts, current, gates
        )
        outs.append(current)

    leaving = jnp.stack(outs).reshape(sections * 2, 4, D)
    out = lax.all_to_all(leaving, ("section", "req"), 0, 0).reshape(patches, 2, 4, D)
    return jnp.transpose(out, (0, 2, 1, 3))[None]


def solution(mesh):
    sizes = tuple(mesh.devices.shape)
    fine = Mesh(
        mesh.devices.reshape(sizes[0], 2, sizes[1] // 2, sizes[2] // 2, 2),
        ("section", "req", "half", "z", "core"),
    )
    return jax.shard_map(
        local,
        mesh=fine,
        in_specs=(
            P(None, ROW_AXES, None, None),
            P(),
            P(),
            P(),
            P("section", None, ROW_AXES),
            P("section", None, COL),
            P("section", COL, None),
            P("section", None, None),
            P("section", None, None, COL, None),
            P("section", ROW_AXES, None, None),
            P(),
        ),
        out_specs=P("section", None, ROW_AXES, None, None),
        check_vma=False,
    )
```

```python
import jax
import jax.numpy as jnp
import numpy as np
from jax import lax
from jax.experimental import pallas as pl
from jax.experimental.pallas import tpu as pltpu
from jax.sharding import Mesh
from jax.sharding import PartitionSpec as P

HD = 64
D = 3072
TXT = 226
GH = 30
GW = 45
PLEN = 256
GROUP = 128
REC_GROUP = 32
STALE = 384
BF = jnp.bfloat16
F32 = jnp.float32
COL = ("z", "core")
ROW = ("req", "half")
ROW_AXES = ("req", "half", "z", "core")


SMEM = pl.BlockSpec(memory_space=pltpu.SMEM)
VMEM = pl.BlockSpec(memory_space=pltpu.VMEM)
HBM = pl.BlockSpec(memory_space=pltpu.HBM)


def call(kernel, out_shape, in_specs, name, out_specs=None, scratch=(), aliases=None):
    if out_specs is None:
        out_specs = jax.tree.map(lambda _: VMEM, out_shape)
    return pl.pallas_call(
        kernel,
        out_shape=out_shape,
        in_specs=in_specs,
        out_specs=out_specs,
        scratch_shapes=list(scratch),
        input_output_aliases=aliases or {},
        compiler_params=pltpu.CompilerParams(vmem_limit_bytes=24 * 1024 * 1024),
        name=name,
    )


def iota(shape, dim):
    return lax.broadcasted_iota(jnp.int32, shape, dim)


def shape_of(shape, dtype):
    return jax.ShapeDtypeStruct(shape, dtype)


def frequencies():
    parts = []
    for size in (HD // 4, HD * 3 // 8, HD * 3 // 8):
        rate = 1.0 / np.float32(10000.0) ** (
            np.arange(0, size, 2).astype(np.float32) / np.float32(size)
        )
        parts.append(np.repeat(rate.astype(np.float32), 2))
    rate = np.concatenate(parts)
    return np.concatenate([rate, rate])[None, :].astype(np.float32)


def offset_in_patch(index, half):
    return (2 * ((index >> 2) & 1) + half) * 64 + 4 * (index >> 3) + (index & 3)


def prepare_kernel(scalars, row_ref, ada_ref, rate_ref, rec_ref, mod_out, tables_out):
    half = scalars[0]
    time_row = row_ref[pl.ds(scalars[5], 1), :]
    embedding = (time_row / (1.0 + jnp.exp(-time_row))).astype(BF)
    embedding = jnp.broadcast_to(embedding, (8, embedding.shape[1]))
    part = lax.dot_general(
        embedding, ada_ref[...], (((1,), (1,)), ((), ())), preferred_element_type=F32
    )[0:1]
    high = part.astype(BF)
    mod_out[0:1, :] = high
    mod_out[1:2, :] = (part - high.astype(F32)).astype(BF)

    rate = rate_ref[...]

    def tables(position, rows, at):
        text = position < TXT
        index = jnp.maximum(position - TXT, 0).astype(F32)
        frame = jnp.floor((index + 0.5) * (1.0 / (GH * GW)))
        line = jnp.floor((index + 0.5) * (1.0 / GW))
        width = index - line * GW
        height = line - jnp.floor((line + 0.5) * (1.0 / GH)) * GH
        lane = iota((rows, 128), 1) & (HD - 1)
        coordinate = jnp.where(lane < HD // 4, frame, jnp.where(lane < HD // 4 + HD * 3 // 8, height, width))
        phase = coordinate * rate
        tables_out[0, at : at + rows, :] = jnp.where(text, 1.0, jnp.cos(phase))
        tables_out[1, at : at + rows, :] = jnp.where(text, 0.0, jnp.sin(phase))
        tables_out[2, at : at + rows, :] = jnp.where(text, 1.0, 0.0)

    tables(offset_in_patch(iota((GROUP, 128), 0), half) + scalars[6], GROUP, 0)
    slot = rec_ref[...]
    start = jnp.where(
        slot < PLEN,
        scalars[1],
        jnp.where(slot < 2 * PLEN, scalars[2], jnp.where(slot < 3 * PLEN, scalars[3], scalars[4])),
    )
    tables(start + (slot & (PLEN - 1)), REC_GROUP, GROUP)


def normalize(x_ref, mod_ref, tables_ref, norm_ref, small):
    chunks = D // 128
    rows = x_ref.shape[0]

    def over_chunks(step, start):
        return lax.fori_loop(0, chunks, lambda k, carry: step(pl.ds(pl.multiple_of(k * 128, 128), 128), carry), start, unroll=6)

    def add(lanes, total):
        return total + x_ref[:, lanes].astype(F32)

    mean = jnp.sum(over_chunks(add, jnp.zeros((rows, 128), F32)), axis=1, keepdims=True) * (1.0 / D)

    def add_square(lanes, total):
        centered = x_ref[:, lanes].astype(F32) - mean
        return total + centered * centered

    total = jnp.sum(over_chunks(add_square, jnp.zeros((rows, 128), F32)), axis=1, keepdims=True)
    factor = lax.rsqrt(total * (1.0 / D) + 1e-5)
    for copy in small:
        copy.wait()
    text = tables_ref[2] > 0.5

    def write(lanes, carry):
        shift = jnp.where(text, mod_ref[3:4, lanes], mod_ref[0:1, lanes])
        scale = jnp.where(text, mod_ref[4:5, lanes], mod_ref[1:2, lanes])
        centered = x_ref[:, lanes].astype(F32) - mean
        norm_ref[:, lanes] = (centered * factor * (1.0 + scale) + shift).astype(BF)
        return carry

    over_chunks(write, 0)


def heads_from(mixed, gain_ref, tables_ref, q_out, kv_out):
    rows = mixed.shape[0]
    lane = iota((128, 128), 1)
    block = jnp.where((iota((128, 128), 0) >> 6) == (lane >> 6), 1.0 / HD, 0.0).astype(BF)

    def group_mean(values):
        high = values.astype(BF)
        low = (values - high.astype(F32)).astype(BF)
        return jnp.dot(high, block, preferred_element_type=F32) + jnp.dot(
            low, block, preferred_element_type=F32
        )

    low_half = iota((rows, 128), 1) < HD
    even = (iota((rows, 128), 1) & 1) == 0
    cosine, sine = tables_ref[0], tables_ref[1]
    gain = gain_ref[...]
    other_gain = pltpu.roll(jnp.broadcast_to(gain, (8, 128)), 64, 1)[0:1]
    gains = (gain, other_gain, other_gain, gain)
    plain, turned = [], []
    for k in range(4):
        values = mixed[:, 128 * k : 128 * k + 128]
        plain.append(values)
        centered = values - group_mean(values)
        scaled = centered * lax.rsqrt(group_mean(centered * centered) + 1e-6) * gains[k]
        partner = jnp.where(even, -pltpu.roll(scaled, 127, 1), pltpu.roll(scaled, 1, 1))
        turned.append(scaled * cosine + partner * sine)
    last = jnp.concatenate([mixed[:, 512:576], jnp.zeros((rows, 64), F32)], axis=1)
    keys_values = (
        pltpu.roll(jnp.where(low_half, plain[1], turned[0]), 64, 1).astype(BF),
        jnp.where(low_half, turned[2], plain[2]).astype(BF),
        pltpu.roll(jnp.where(low_half, last, turned[3]), 64, 1).astype(BF),
    )
    for copy in range(kv_out.shape[0]):
        for head in range(3):
            kv_out[copy, 0:rows, 128 * head : 128 * head + 128] = keys_values[head]
    if q_out is None:
        return
    zero = jnp.zeros((rows, 128), F32)
    q_out[:, 0:128] = (jnp.where(low_half, turned[0], zero) * 0.125).astype(BF)
    q_out[:, 128:256] = (jnp.where(low_half, pltpu.roll(turned[1], 64, 1), zero) * 0.125).astype(BF)
    q_out[:, 256:384] = (jnp.where(low_half, turned[3], zero) * 0.125).astype(BF)


def times_weights(norm, weights):
    return lax.dot_general(norm, weights, (((1,), (1,)), ((), ())), preferred_element_type=F32)


def small_copies(mod_hbm, rows_hbm, tables_hbm, layer, rows, mod_ref, gain_ref, tables_ref, sems):
    copies = [
        pltpu.make_async_copy(mod_hbm.at[layer], mod_ref, sems.at[0]),
        pltpu.make_async_copy(rows_hbm.at[4 * layer, pl.ds(16, 1), pl.ds(0, 128)], gain_ref, sems.at[1]),
        pltpu.make_async_copy(tables_hbm.at[:, rows, :], tables_ref, sems.at[2]),
    ]
    for copy in copies:
        copy.start()
    return copies


def small_scratch(rows):
    return [
        pltpu.VMEM((6, D), F32),
        pltpu.VMEM((1, 128), F32),
        pltpu.VMEM((3, rows, 128), F32),
        pltpu.SemaphoreType.DMA((3,)),
    ]


def rec_kernel(
    scalars, gathered_ref, mod_hbm, rows_hbm, tables_hbm, w_ref,
    kv_out, x_ref, norm_ref, w_vmem, sem, mod_ref, gain_ref, tables_ref, sems,
):
    fetch = pltpu.make_async_copy(w_ref, w_vmem, sem)
    fetch.start()
    rows = pl.ds(GROUP, REC_GROUP)
    small = small_copies(mod_hbm, rows_hbm, tables_hbm, scalars[7], rows, mod_ref, gain_ref, tables_ref, sems)
    share = gathered_ref[:, D : D + 768]
    for k in range(4):
        pick = iota((REC_GROUP, GROUP), 1) == 4 * iota((REC_GROUP, GROUP), 0) + k
        pick = jnp.where(pick, 1.0, 0.0).astype(BF)
        x_ref[:, 768 * k : 768 * k + 768] = jnp.dot(pick, share, preferred_element_type=F32).astype(BF)
    normalize(x_ref, mod_ref, tables_ref, norm_ref, small)
    fetch.wait()
    heads_from(times_weights(norm_ref[...], w_vmem[...]), gain_ref, tables_ref, None, kv_out)


def qkv_kernel_of(layer):
    def qkv_kernel(
        x_ref, rec_ref, mod_hbm, rows_hbm, tables_hbm, packed_ref,
        q_out, kv_out, weights_out, gates_out, norm_ref, w_vmem, sems, mod_ref, gain_ref, tables_ref, small_sems,
    ):
        rows = pl.ds(0, GROUP)
        small = small_copies(mod_hbm, rows_hbm, tables_hbm, layer, rows, mod_ref, gain_ref, tables_ref, small_sems)

        def fetch(k):
            to = w_vmem.at[pl.ds(288 * (k % 2), 288), pl.ds(384 * (k // 2), 384)]
            return pltpu.make_async_copy(packed_ref.at[k, pl.ds(0, 288), :], to, sems.at[k])

        def pass_on(k):
            to = weights_out.at[pl.ds(96 * (k % 2), 96), pl.ds(384 * (k // 2), 384)]
            return pltpu.make_async_copy(packed_ref.at[k, pl.ds(288, 96), :], to, sems.at[16 + k])

        for k in range(16):
            fetch(k).start()
        normalize(x_ref, mod_ref, tables_ref, norm_ref, small)
        for k in range(16):
            pass_on(k).start()
        mixed = jnp.zeros((GROUP, 576), F32)
        for piece in range(4):
            for k in range(4 * piece, 4 * piece + 4):
                fetch(k).wait()
            lanes = slice(768 * piece, 768 * piece + 768)
            mixed = mixed + times_weights(norm_ref[:, lanes], w_vmem[:, lanes])
        heads_from(mixed, gain_ref, tables_ref, q_out, kv_out)
        gates_out[0:1, :] = mod_ref[2:3, :]
        gates_out[1:2, :] = mod_ref[5:6, :]
        if layer == 0:
            for copy in range(kv_out.shape[0]):
                kv_out[copy, GROUP:, :] = rec_ref[0]
        for k in range(16):
            pass_on(k).wait()

    return qkv_kernel


def pack_kernel(row_ref, w_ref, out_ref, packed, sems):
    copies = []
    for k in range(4):
        lanes = pl.ds(pl.multiple_of(row_ref[0] * 768 + 384 * (k // 2), 128), 384)
        copies += [
            (w_ref.at[pl.ds(288 * (k % 2), 288), lanes], packed.at[k, pl.ds(0, 288), :]),
            (out_ref.at[pl.ds(96 * (k % 2), 96), lanes], packed.at[k, pl.ds(288, 96), :]),
        ]
    copies = [pltpu.make_async_copy(a, b, sems.at[n]) for n, (a, b) in enumerate(copies)]
    for copy in copies:
        copy.start()
    for copy in copies:
        copy.wait()


def attend(scalars, q_ref, cache_ref, keep_out, send_out):
    patch, core = scalars[7], scalars[9]
    key = iota((8, 1024), 1)
    key_patch = key >> 8
    within = key & (PLEN - 1)
    fresh_offset = (2 * ((within >> 2) & 1) + (within >> 7)) * 64 + 4 * ((within >> 3) & 15) + (within & 3)
    offset = jnp.where(key_patch <= patch, fresh_offset, within)
    count = jnp.where(
        key_patch == 0,
        scalars[11],
        jnp.where(key_patch == 1, scalars[12], jnp.where(key_patch == 2, scalars[13], scalars[14])),
    )
    live = (offset < count)[0:1]
    outs = []
    for head in range(3):
        lanes = slice(128 * head, 128 * head + 128)
        keys_values = cache_ref[:, lanes]
        scores = lax.dot_general(
            q_ref[:, lanes], keys_values, (((1,), (1,)), ((), ())), preferred_element_type=F32
        )
        weights = jnp.where(live, jnp.exp(scores), 0.0)
        total = jnp.sum(weights, axis=1, keepdims=True)
        mixed = jnp.dot(weights.astype(BF), keys_values, preferred_element_type=F32)
        outs.append(mixed / total)
    low = iota((GROUP, 128), 1) < HD
    first = jnp.where(low, pltpu.roll(outs[0], 64, 1), outs[1]).astype(BF)
    second = jnp.where(low, pltpu.roll(outs[2], 64, 1), 0.0).astype(BF)
    for z in range(8):
        to = slice(8 * z, 8 * z + 8)
        even, odd = slice(16 * z, 16 * z + 8), slice(16 * z + 8, 16 * z + 16)
        for value, lanes in ((first, slice(0, 128)), (second, slice(128, 256))):
            keep_out[to, lanes] = jnp.where(core == 0, value[even], value[odd])
            send_out[to, lanes] = jnp.where(core == 0, value[odd], value[even])


def merge_copies(layer, targets_hbm, rec_ref, stale_ref, base_ref, rec_vmem, target_ref, sems):
    copies = [
        pltpu.make_async_copy(
            rec_ref.at[2 * layer + h, pl.ds(GROUP, REC_GROUP), :],
            rec_vmem.at[pl.ds(REC_GROUP * h, REC_GROUP), :],
            sems.at[h],
        )
        for h in range(2)
    ]
    copies += [
        pltpu.make_async_copy(
            stale_ref.at[2 * layer + h], base_ref.at[pl.ds(PLEN + STALE * h, STALE), :], sems.at[2 + h]
        )
        for h in range(2)
    ]
    copies.append(pltpu.make_async_copy(targets_hbm, target_ref, sems.at[4]))
    for copy in copies:
        copy.start()
    return copies


def merge(copies, base_ref, rec_vmem, target_ref, table_ref):
    rec_vmem[2 * REC_GROUP :, :] = jnp.zeros((128 - 2 * REC_GROUP, 384), BF)
    for copy in copies:
        copy.wait()
    match = iota((3 * PLEN, 128), 0) + PLEN == target_ref[0:1, :]
    chosen = jnp.where(match, 1.0, 0.0)
    hit = jnp.sum(chosen, axis=1, keepdims=True) > 0.5
    placed = jnp.dot(chosen.astype(BF), rec_vmem[...], preferred_element_type=F32)
    table_ref[PLEN:, :] = jnp.where(hit, placed, base_ref[PLEN:, :].astype(F32)).astype(BF)


def merge_scratch():
    return [
        pltpu.VMEM((1024, 384), BF),
        pltpu.VMEM((128, 384), BF),
        pltpu.VMEM((8, 128), jnp.int32),
        pltpu.SemaphoreType.DMA((5,)),
    ]


def table_kernel_of(layer):
    def table_kernel(fresh_ref, targets_hbm, rec_ref, stale_ref, table_out, base_ref, rec_vmem, target_ref, sems):
        del fresh_ref
        copies = merge_copies(layer, targets_hbm, rec_ref, stale_ref, base_ref, rec_vmem, target_ref, sems)
        table_out[0:PLEN, :] = jnp.zeros((PLEN, 384), BF)
        merge(copies, base_ref, rec_vmem, target_ref, table_out)

    return table_kernel


def weight_copies(own_hbm, other_hbm, weights_out, sems):
    copies = [
        pltpu.make_async_copy(own_hbm, weights_out.at[0], sems.at[0]),
        pltpu.make_async_copy(other_hbm, weights_out.at[1], sems.at[1]),
    ]
    for copy in copies:
        copy.start()
    return copies


def attend_all_kernel_of(layer):
    def attend_all_kernel(
        scalars, q_ref, fresh_ref, targets_hbm, rec_ref, stale_ref, own_hbm, other_hbm,
        keep_out, send_out, weights_out, cache_ref, weight_sems, base_ref, rec_vmem, target_ref, sems,
    ):
        copies = merge_copies(layer, targets_hbm, rec_ref, stale_ref, base_ref, rec_vmem, target_ref, sems)
        weights = weight_copies(own_hbm, other_hbm, weights_out, weight_sems)
        merge(copies, base_ref, rec_vmem, target_ref, cache_ref)
        for patch in range(4):

            @pl.when(patch <= scalars[7])
            def _(patch=patch):
                cache_ref[PLEN * patch : PLEN * patch + PLEN, :] = jnp.concatenate(
                    [fresh_ref[2 * patch, 0:GROUP, :], fresh_ref[2 * patch + 1, 0:GROUP, :]], axis=0
                )

        attend(scalars, q_ref, cache_ref, keep_out, send_out)
        for copy in weights:
            copy.wait()

    return attend_all_kernel


def attend_kernel(
    scalars, q_ref, own_ref, back1_ref, back2_ref, back3_ref, table_ref, own_hbm, other_hbm,
    keep_out, send_out, weights_out, cache_ref, weight_sems,
):
    section, half = scalars[7], scalars[0]
    weights = weight_copies(own_hbm, other_hbm, weights_out, weight_sems)
    for patch in range(1, 4):

        @pl.when(patch > section)
        def _(patch=patch):
            rows = slice(PLEN * patch, PLEN * patch + PLEN)
            cache_ref[rows, :] = table_ref[rows, :]

    for back, piece in enumerate((own_ref, back1_ref, back2_ref, back3_ref)):

        @pl.when(section >= back)
        def _(back=back, piece=piece):
            for at, rows in ((half, slice(0, GROUP)), (1 - half, slice(GROUP, 2 * GROUP))):
                start = pl.multiple_of((section - back) * PLEN + at * GROUP, GROUP)
                cache_ref[pl.ds(start, GROUP), :] = piece[rows, :]

    attend(scalars, q_ref, cache_ref, keep_out, send_out)
    for copy in weights:
        copy.wait()


def project_kernel(keep_ref, got_ref, weights_ref, out_ref):
    out = jnp.dot(keep_ref[:, 0:192], weights_ref[0], preferred_element_type=F32)
    out = out + jnp.dot(got_ref[:, 0:192], weights_ref[1], preferred_element_type=F32)
    out_ref[...] = out.astype(BF)


def residual_kernel(scalars, parts_ref, x_ref, gates_ref, out_ref):
    row = iota((8, 128), 0)
    offset = (2 * (row >> 2) + scalars[0]) * 64 + 4 * scalars[10] + (row & 3)
    text = (offset + scalars[6]) < TXT
    for k in range(D // 128):
        lanes = slice(128 * k, 128 * k + 128)
        total = parts_ref[0, :, lanes].astype(F32)
        for source in range(1, 8):
            total = total + parts_ref[source, :, lanes].astype(F32)
        gate = jnp.where(text, gates_ref[1:2, lanes], gates_ref[0:1, lanes])
        out_ref[:, lanes] = (x_ref[:, lanes].astype(F32) + gate * total).astype(BF)


def time_block(timestep, time_table):
    return lax.dynamic_slice(time_table, ((timestep[0] // 8) * 8, 0), (8, time_table.shape[1]))


def swapped(value, axis):
    return lax.ppermute(value, axis, [(0, 1), (1, 0)])


def local(
    hidden,
    patch_counts,
    timestep,
    time_table,
    ada_weight,
    qkv_weight,
    out_weight,
    qk_gain,
    stale_kv,
    stale_inputs,
    recompute_slots,
):
    section = lax.axis_index("section")
    req = lax.axis_index("req")
    half = lax.axis_index("half")
    core = lax.axis_index("core")
    col = lax.axis_index("z") * 2 + core
    first_req = req == 0
    sections = lax.axis_size("section")
    patches = hidden.shape[0]

    row_index = req * 2 + half
    weights_qkv = pltpu.with_memory_space_constraint(qkv_weight[0].T, pltpu.HBM)
    packed = call(
        pack_kernel,
        shape_of((4, 384, 384), BF),
        [SMEM, HBM, HBM],
        "pack",
        out_specs=HBM,
        scratch=[pltpu.SemaphoreType.DMA((8,))],
    )(
        row_index[None].astype(jnp.int32),
        weights_qkv,
        pltpu.with_memory_space_constraint(out_weight[0], pltpu.HBM),
    )
    chunks = lax.all_to_all(packed, "section", 0, 0)
    layers = [
        lax.all_gather(chunks[layer], ("req", "half", "section"), axis=0, tiled=False) for layer in range(sections)
    ]
    peers = ("section", "half")
    copies = lax.axis_size(peers)
    stale_share = lax.dynamic_slice(stale_kv, (0, PLEN + STALE * half, req, 0, 0), (1, STALE, 1, 3, 128))
    stale_share = stale_share.reshape(1, STALE, 384)
    stale_all = lax.all_to_all(jnp.broadcast_to(stale_share, (copies, STALE, 384)), peers, 0, 0)

    def of_request(value, axis):
        both = [lax.index_in_dim(value, r, axis, keepdims=False) for r in range(2)]
        return jnp.where(first_req, both[0], both[1]), jnp.where(first_req, both[1], both[0])

    def by_request(value, got):
        own = [lax.index_in_dim(value, r, 1, keepdims=False) for r in range(2)]
        far = [lax.index_in_dim(got, r, 1, keepdims=False) for r in range(2)]
        return jnp.where(
            first_req, jnp.concatenate([own[0], far[0]], axis=0), jnp.concatenate([far[1], own[1]], axis=0)
        )

    patch_rows = lax.dynamic_index_in_dim(hidden, section, 0, keepdims=False)
    tokens = by_request(patch_rows, swapped(patch_rows, "req"))
    rec_tokens = by_request(stale_inputs[0], swapped(stale_inputs[0], "req"))

    counts, _ = of_request(patch_counts, 0)
    starts = jnp.stack([jnp.int32(0), counts[0], counts[0] + counts[1], counts[0] + counts[1] + counts[2]])
    slots, _ = of_request(recompute_slots, 0)
    slots = slots.reshape(2, 2, 16)
    by_half = [slots[:, h].T.reshape(REC_GROUP) for h in range(2)]
    target_own = jnp.where(half == 0, by_half[0], by_half[1])
    targets = jnp.concatenate(by_half + [jnp.full((64,), -1, jnp.int32)])
    targets = jnp.broadcast_to(targets[None, :], (8, 128))

    own_start = lax.dynamic_index_in_dim(starts, section, 0, keepdims=True)
    scalars = jnp.concatenate(
        [half[None], starts, timestep % 8, own_start, jnp.stack([section, row_index, core, col]), counts, req[None]]
    ).astype(jnp.int32)
    mod_part, tables = call(
        prepare_kernel,
        (shape_of((2, 288), BF), shape_of((3, GROUP + REC_GROUP, 128), F32)),
        [SMEM, VMEM, VMEM, VMEM, VMEM],
        "prepare",
    )(
        scalars,
        time_block(timestep, time_table),
        ada_weight[0].T,
        jnp.asarray(frequencies()),
        jnp.broadcast_to(target_own[:, None], (REC_GROUP, 128)),
    )

    payload = jnp.concatenate(
        [
            tokens,
            rec_tokens.reshape(8, 768),
            jnp.pad(mod_part.reshape(8, 72), ((0, 0), (0, 56))),
        ],
        axis=1,
    )
    gathered = lax.all_gather(payload, COL, axis=0, tiled=True)
    pieces = gathered[:, D + 768 : D + 840].reshape(16, 2, 288).astype(F32)
    summed = pieces[:, 0] + pieces[:, 1]
    gain_row = jnp.pad(qk_gain[0].reshape(1, 128), ((0, 0), (0, 160)))
    rows = jnp.concatenate([summed, gain_row], axis=0)[None]
    everyone = ("section",) + ROW
    rows, stale_all = lax.optimization_barrier((rows, stale_all))
    rows = lax.all_to_all(jnp.broadcast_to(rows, (lax.axis_size(everyone), 17, 288)), everyone, 0, 0)
    modulation = rows[:, :16].reshape(sections, 6, D)
    in_hbm = [pltpu.with_memory_space_constraint(value, pltpu.HBM) for value in (modulation, rows, tables)]
    rec_fresh = call(
        rec_kernel,
        shape_of((1, REC_GROUP, 384), BF),
        [SMEM, VMEM] + [HBM] * 4,
        "rec",
        scratch=[
            pltpu.VMEM((REC_GROUP, D), BF),
            pltpu.VMEM((REC_GROUP, D), BF),
            pltpu.VMEM((576, D), BF),
            pltpu.SemaphoreType.DMA,
        ]
        + small_scratch(REC_GROUP),
    )(scalars, gathered, *in_hbm, weights_qkv)
    targets = pltpu.with_memory_space_constraint(targets, pltpu.HBM)

    def upwards(fresh, out_own):
        both = jnp.concatenate([fresh, swapped(fresh, "half")], axis=0)
        pairs = [[(i, i + back) for i in range(sections - back)] for back in range(1, sections)]
        both, out_own = lax.optimization_barrier((both, out_own))
        return out_own, [both] + [lax.ppermute(both, "section", steps) for steps in pairs]

    half_rows = shape_of((64, 256), BF)
    current, group, outs, first_fresh = tokens, gathered, [], None
    for layer in range(sections):
        packed = pltpu.with_memory_space_constraint(layers[layer], pltpu.HBM)
        if layer > 0:
            group = lax.all_gather(current, COL, axis=0, tiled=True)
            group = pltpu.with_memory_space_constraint(group, pltpu.VMEM)
        to_all = layer in (0, sections - 1)
        queries, fresh, out_own, gates = call(
            qkv_kernel_of(layer),
            (
                shape_of((GROUP, 384), BF),
                shape_of((copies if to_all else 1, GROUP + (REC_GROUP if layer == 0 else 0), 384), BF),
                shape_of((192, D), BF),
                shape_of((2, D), F32),
            ),
            [VMEM] * 2 + [HBM] * 4,
            "qkv",
            scratch=[pltpu.VMEM((GROUP, D), BF), pltpu.VMEM((576, D), BF), pltpu.SemaphoreType.DMA((32,))]
            + small_scratch(GROUP),
        )(group, rec_fresh, *in_hbm, packed)
        attend_out = (half_rows, half_rows, shape_of((2, 192, D), BF))
        attend_scratch = [pltpu.VMEM((1024, 384), BF), pltpu.SemaphoreType.DMA((2,))]
        if to_all:
            out_other = swapped(out_own, "core")
            fresh_all = lax.all_to_all(fresh, peers, 0, 0)
            first_fresh = fresh_all if layer == 0 else first_fresh
            keep, send, weights_out = call(
                attend_all_kernel_of(layer),
                attend_out,
                [SMEM, VMEM, VMEM] + [HBM] * 5,
                "attend_all",
                scratch=attend_scratch + merge_scratch(),
            )(scalars, queries, fresh_all, targets, first_fresh, stale_all, out_own, out_other)
        else:
            out_own, pieces = upwards(fresh[0], out_own)
            out_other = swapped(out_own, "core")
            merged = call(
                table_kernel_of(layer),
                shape_of((1024, 384), BF),
                [HBM] * 4,
                "table",
                scratch=merge_scratch(),
            )(fresh, targets, first_fresh, stale_all)
            keep, send, weights_out = call(
                attend_kernel,
                attend_out,
                [SMEM] + [VMEM] * 6 + [HBM] * 2,
                "attend",
                scratch=attend_scratch,
            )(scalars, queries, *pieces, merged, out_own, out_other)
        projected = call(project_kernel, shape_of((64, D), BF), [VMEM] * 3, "project")(
            keep, swapped(send, "core"), weights_out
        )
        parts = lax.all_to_all(projected.reshape(8, 8, D), "z", 0, 0)
        current = call(residual_kernel, shape_of((8, D), BF), [SMEM, VMEM, VMEM, VMEM], "residual")(
            scalars, parts, current, gates
        )
        outs.append(current)

    leaving = jnp.stack(outs).reshape(sections * 2, 4, D)
    out = lax.all_to_all(leaving, ("section", "req"), 0, 0).reshape(patches, 2, 4, D)
    return jnp.transpose(out, (0, 2, 1, 3))[None]


def solution(mesh):
    sizes = tuple(mesh.devices.shape)
    fine = Mesh(
        mesh.devices.reshape(sizes[0], 2, sizes[1] // 2, sizes[2] // 2, 2),
        ("section", "req", "half", "z", "core"),
    )
    return jax.shard_map(
        local,
        mesh=fine,
        in_specs=(
            P(None, ROW_AXES, None, None),
            P(),
            P(),
            P(),
            P("section", None, ROW_AXES),
            P("section", None, COL),
            P("section", COL, None),
            P("section", None, None),
            P("section", None, None, COL, None),
            P("section", ROW_AXES, None, None),
            P(),
        ),
        out_specs=P("section", None, ROW_AXES, None, None),
        check_vma=False,
    )
```
